32 devices in a mesh: seq: 8 (over y, x, core), tp: 4 (over z).
Axes of the slice: x: 2, y: 2, z: 4, core: 2. Of those that a mesh axis runs over, the one named last changes fastest.
Arguments:
- layer_in: bfloat16 [2, 2048, 2048], P(None, 'seq'), may hold values from -6 to 6
- attn_gain: float32 [2048], replicated, may hold values from 0.1 to 1.9
- query_down: bfloat16 [2048, 1024], replicated, may hold values from -0.125 to 0.125
- latent_gain: float32 [1024], replicated, may hold values from 0.1 to 1.9
- query_up: bfloat16 [1024, 4096], P(None, 'tp'), may hold values from -0.1875 to 0.1875
- key_value: bfloat16 [2048, 512], replicated, may hold values from -0.125 to 0.125
- attn_out: bfloat16 [4096, 2048], P('tp'), may hold values from -1.5 to 1.5
- ffn_gain: float32 [2048], replicated, may hold values from 0.1 to 1.9
- gate_proj: bfloat16 [2048, 5632], P(None, 'tp'), may hold values from -0.125 to 0.125
- up_proj: bfloat16 [2048, 5632], P(None, 'tp'), may hold values from -0.125 to 0.125
- down_proj: bfloat16 [5632, 2048], P('tp'), may hold values from -0.078125 to 0.078125
- out_grad: bfloat16 [2, 2048, 2048], P(None, 'seq'), may hold values from -6 to 6
- doc_lengths: int32 [2, 8], replicated, may hold values from 1 to 1536, 2048 in all within a row
Outputs:
- layer_out: bfloat16 [2, 2048, 2048], P(None, 'seq')
- input_grad: bfloat16 [2, 2048, 2048], P(None, 'seq')
- attn_gain_grad: float32 [2048], P('seq')
- query_down_grad: float32 [2048, 1024], P('seq')
- latent_gain_grad: float32 [1024], P('seq')
- query_up_grad: float32 [1024, 4096], P('seq', 'tp')
- key_value_grad: float32 [2048, 512], P('seq')
- attn_out_grad: float32 [4096, 2048], P('tp', 'seq')
- ffn_gain_grad: float32 [2048], P('seq')
- gate_proj_grad: float32 [2048, 5632], P('seq', 'tp')
- up_proj_grad: float32 [2048, 5632], P('seq', 'tp')
- down_proj_grad: float32 [5632, 2048], P('tp', 'seq')
The draws below stay inside these ranges and needn't reach their ends.
Inputs may be any that keep to these rules, and one draw needn't show every extreme that they name: `doc_lengths`: in each row the 8 lengths add up to 2048, and the longest is exactly 1536.
All inputs are finite; a program needn't handle non-finite values.
Results may differ from the reference program's by a relative error of at most 0.019.
Values may be sent and summed in bfloat16 or wider, within the bound.
No kernel may reach another device: no remote copies, remote signals or barrier semaphores. Data moves between devices by JAX's collectives and lax.ppermute only.
A program may use at most 256 MiB of HBM per device.

```python
import math
import jax
import jax.numpy as jnp
import numpy as np
from jax import lax

D = 2048
QL = 1024
HEADS = 16
HD = 256
FF = 5632
ROWS = 2
DOCS = 8
ROW_LEN = 2048


def spiked(array, stream_key, source, target, parts, factor):
    def block_of(position):
        return (jnp.arange(array.shape[position]) // (array.shape[position] // parts)).reshape((-1,) + (1,) * (array.ndim - 1 - position))

    one_side = jax.random.permutation(stream_key, parts)[block_of(target)]
    second = (block_of(target) + parts // 2) % parts
    return jnp.where((block_of(source) == one_side) | (block_of(source) == second), factor * array, array)


def level_of(own_key, dims, shards, low, largest):
    def one(dim, parts):
        heights = jax.random.uniform(jax.random.fold_in(jax.random.fold_in(own_key, 6), dim), (parts,), jnp.float32, low / len(shards), largest / len(shards))
        return jnp.repeat(jnp.exp(heights), dims[dim] // parts).reshape((-1,) + (1,) * (len(dims) - dim - 1))

    loudness = one(*shards[0])
    for cut in shards[1:]:
        loudness = loudness * one(*cut)
    return loudness


def split_up(amount, total, reach, slope):
    weights = [(1 << 20) // math.isqrt(grade ** slope) + 1 for grade in range(2, amount + 1)]
    spare, counts = total - reach - (amount - 1), [1] * (amount - 1)
    while spare > 0:
        movable = [i for i in range(amount - 1) if counts[i] < reach]
        mass, remaining = sum([weights[i] for i in movable]), spare
        for i in movable:
            more = min(reach - counts[i], max(1, remaining * weights[i] // mass), spare)
            counts[i] = counts[i] + more
            spare = spare - more
    return np.array([reach] + counts)


def uneven(key, count, total, bound, lean):
    if count == 2:
        one = jax.random.randint(key, (), max(1, total - bound), min(bound, total - 1) + 1)
        return jnp.stack([one, total - one])
    sizes = jnp.asarray(split_up(count, total, bound, lean), jnp.int32)
    twos = (count - 1) // 2
    giver, taker = sizes[1:1 + 2 * twos:2], sizes[2:2 + 2 * twos:2]
    margin = jnp.minimum(giver - 1, bound - taker)
    moved = jax.random.randint(jax.random.fold_in(key, 1), (twos,), 0, 1 << 20) % (margin + 1)
    sizes = sizes.at[1:1 + 2 * twos:2].set(giver - moved).at[2:2 + 2 * twos:2].set(taker + moved)
    return sizes[jax.random.permutation(jax.random.fold_in(key, 2), count)]


def noise(own_key, shape, deviation, bound, shards=(), kind=jnp.bfloat16):
    values = jax.random.normal(own_key, shape, jnp.float32) * deviation
    if len(shards) > 0:
        values = level_of(own_key, shape, shards, -0.22, 0.18) * values
    return jnp.clip(values, min=-bound, max=bound).astype(kind)


def heavy_noise(rng, extent, width, most, pieces, heavy, held_as=jnp.bfloat16):
    drawn = width * jax.random.normal(rng, extent, jnp.float32)
    if pieces:
        drawn = drawn * level_of(rng, extent, pieces, -0.22, 0.18)
    return jnp.clip(spiked(drawn, jax.random.fold_in(rng, 3), *heavy), -most, most).astype(held_as)


def setup_inputs(seed: int = 0) -> dict:
    splits = jax.random.split(jax.random.key(seed), 14)
    layer_in = noise(splits[0], (ROWS, ROW_LEN, D), 1.0, 6.0, ((1, 8),))
    attn_gain = jnp.clip(1.0 + 0.18 * jax.random.normal(splits[1], (D,), jnp.float32), 0.1, 1.9)
    query_down = noise(splits[2], (D, QL), D ** -0.5, 0.125)
    latent_gain = jnp.clip(1.0 + 0.18 * jax.random.normal(splits[3], (QL,), jnp.float32), 0.1, 1.9)
    query_up = noise(splits[4], (QL, HEADS * HD), QL ** -0.5, 0.1875, ((1, 4),))
    key_value = noise(splits[5], (D, 2 * HD), D ** -0.5, 0.125)
    attn_out = noise(splits[6], (HEADS * HD, D), (max(HEADS * HD // 256, 4)) ** -0.5, 1.5, ((0, 4),))
    ffn_gain = jnp.clip(1.0 + 0.18 * jax.random.normal(splits[7], (D,), jnp.float32), 0.1, 1.9)
    gate_proj = noise(splits[8], (D, FF), D ** -0.5, 0.125, ((1, 4),))
    up_proj = noise(splits[9], (D, FF), D ** -0.5, 0.125, ((1, 4),))
    down_proj = noise(splits[10], (FF, D), FF ** -0.5, 0.078125, ((0, 4),))
    out_grad = heavy_noise(splits[11], (ROWS, ROW_LEN, D), 1.0, 6.0, ((1, 8),), (1, 2, 8, 2.0))
    doc_lengths = jax.vmap(lambda own: uneven(own, DOCS, ROW_LEN, 3 * ROW_LEN // 4, 2))(jax.random.split(splits[12], ROWS)).reshape((ROWS, DOCS)).astype(jnp.int32)
    return {"layer_in": layer_in, "attn_gain": attn_gain, "query_down": query_down, "latent_gain": latent_gain, "query_up": query_up, "key_value": key_value, "attn_out": attn_out, "ffn_gain": ffn_gain, "gate_proj": gate_proj, "up_proj": up_proj, "down_proj": down_proj, "out_grad": out_grad, "doc_lengths": doc_lengths}


EPS = 1e-05
ROPE_BASE = 10000.0
NEG_FILL = -1e+30
HIGH = lax.Precision.HIGHEST

@jax.custom_vjp
def low(v):
    return lax.optimization_barrier(v.astype(jnp.bfloat16)).astype(jnp.float32)

@jax.custom_vjp
def low_back(v):
    return v

def low_keep(v):
    return (low(v), None)

def low_pass(kept, grad):
    return (grad,)

def back_keep(v):
    return (v, None)

def back_low(kept, grad):
    return (low(grad),)
low.defvjp(low_keep, low_pass)
low_back.defvjp(back_keep, back_low)

def product(left, right):
    return jnp.dot(left, right, precision=HIGH, preferred_element_type=jnp.float32)

def rms_norm(values, gain_vec):
    inv_rms = lax.rsqrt(lax.optimization_barrier(jnp.mean(values * values, axis=-1, keepdims=True)) + EPS)
    return values * inv_rms * gain_vec

def doc_layout(lengths, places):
    doc_ends = jnp.cumsum(lengths).astype(jnp.int32)
    starts = doc_ends - lengths
    owners = lax.optimization_barrier(jnp.sum((places[:, None] >= doc_ends[None, :]).astype(jnp.int32), axis=1))
    member = owners[:, None] == jnp.arange(lengths.shape[0], dtype=jnp.int32)[None, :]
    inner_pos = places - lax.optimization_barrier(jnp.sum(jnp.where(member, starts[None, :], 0), axis=1))
    return (owners, inner_pos)

def rotate(values, inner_pos, direction):
    half_dim = values.shape[-1] // 2
    frequency = ROPE_BASE ** (-jnp.arange(half_dim, dtype=jnp.float32) / half_dim)
    angles = inner_pos.astype(jnp.float32)[..., None] * frequency
    for padding_axis in range(values.ndim - 1 - angles.ndim + 1):
        angles = angles[..., None, :]
    cosine = jnp.cos(angles)
    sine_part = jnp.sin(angles) * direction
    front_half = values[..., :half_dim]
    back_half = values[..., half_dim:]
    return jnp.concatenate([front_half * cosine - back_half * sine_part, back_half * cosine + front_half * sine_part], axis=-1)

def attend(queries, key_rows, value_rows, owners):
    length = queries.shape[0]
    block_rows = math.gcd(512, length)
    places = jnp.arange(length, dtype=jnp.int32)

    def one_block(block_id):
        offset = block_id * block_rows
        q_block = lax.dynamic_slice_in_dim(queries, offset, block_rows, 0)
        q_owner = lax.dynamic_slice_in_dim(owners, offset, block_rows, 0)
        q_place = offset + jnp.arange(block_rows, dtype=jnp.int32)
        scores = jnp.einsum('qhd,kd->hqk', q_block, key_rows, precision=HIGH) * HD ** (-0.5)
        scores = low_back(scores)
        allowed = (q_owner[:, None] == owners[None, :]) & (places[None, :] <= q_place[:, None])
        scores = jnp.where(allowed[None], scores, NEG_FILL)
        row_peak = lax.optimization_barrier(jnp.max(scores, axis=-1, keepdims=True))
        expo_vals = jnp.exp(scores - row_peak)
        weights = low(expo_vals / lax.optimization_barrier(jnp.sum(expo_vals, axis=-1, keepdims=True)))
        return jnp.einsum('hqk,kd->qhd', weights, value_rows, precision=HIGH)
    blocks = lax.map(jax.checkpoint(one_block), jnp.arange(length // block_rows, dtype=jnp.int32))
    return blocks.reshape(length, -1)

def row_forward(params, row_in, owners, inner_pos):
    attn_gain, query_down, latent_gain, query_up, key_value, attn_out, ffn_gain, gate_proj, up_proj, down_proj = params
    length = row_in.shape[0]
    normed = low(rms_norm(row_in, attn_gain))
    latent = low_back(product(normed, query_down))
    latent_norm = low(rms_norm(latent, latent_gain))
    raw_query = low_back(product(latent_norm, query_up)).reshape(length, HEADS, HD)
    queries = low(rotate(raw_query, inner_pos, 1.0))
    kv_proj = low_back(product(normed, key_value))
    key_rows = low(rotate(kv_proj[:, :HD], inner_pos, 1.0))
    value_rows = low(kv_proj[:, HD:])
    context = low(low_back(attend(queries, key_rows, value_rows, owners)))
    middle = row_in + low_back(product(context, attn_out))
    second_norm = low(rms_norm(middle, ffn_gain))
    gate_act = low_back(product(second_norm, gate_proj))
    up_act = low_back(product(second_norm, up_proj))
    hidden = low(jax.nn.silu(gate_act) * up_act)
    return middle + low_back(product(hidden, down_proj))

def reference(layer_in, attn_gain, query_down, latent_gain, query_up, key_value, attn_out, ffn_gain, gate_proj, up_proj, down_proj, out_grad, doc_lengths):
    params = tuple((weight.astype(jnp.float32) for weight in (attn_gain, query_down, latent_gain, query_up, key_value, attn_out, ffn_gain, gate_proj, up_proj, down_proj)))
    places = jnp.arange(ROW_LEN, dtype=jnp.int32)

    def one_row(totals, row_data):
        row_in, row_grad, lengths = row_data
        owners, inner_pos = doc_layout(lengths, places)

        def forward_only(weights_in, acts_in):
            return row_forward(weights_in, acts_in, owners, inner_pos)
        output, pullback = jax.vjp(forward_only, params, row_in.astype(jnp.float32))
        grads, row_input_grad = pullback(row_grad.astype(jnp.float32))
        totals = jax.tree.map(jnp.add, totals, grads)
        return (totals, (output.astype(jnp.bfloat16), row_input_grad.astype(jnp.bfloat16)))
    zeros_start = tuple((jnp.zeros_like(weight) for weight in params))
    totals, outputs = lax.scan(one_row, zeros_start, (layer_in, out_grad, doc_lengths))
    return (outputs[0], outputs[1], totals[0], totals[1], totals[2], totals[3], totals[4], totals[5], totals[6], totals[7], totals[8], totals[9])
```

```python
import jax
import jax.numpy as jnp
from jax import lax
from jax.sharding import PartitionSpec as P

HD = 256
EPS = 1e-05
ROPE_BASE = 10000.0
NEG_FILL = -1e30
BF = jnp.bfloat16
F32 = jnp.float32


def matmul(left, right):
    return jnp.dot(left, right, preferred_element_type=F32)


def dot_rows(left, right):
    return lax.dot_general(left, right, (((0,), (0,)), ((), ())), preferred_element_type=F32)


def dot_cols(left, right):
    return lax.dot_general(left, right, (((1,), (1,)), ((), ())), preferred_element_type=F32)


def unit_norm(values):
    inv_rms = lax.rsqrt(jnp.mean(values * values, axis=-1, keepdims=True) + EPS)
    return values * inv_rms, inv_rms


def rms_backward(grad_out, unit_rows, inv_rms, gain_vec):
    scaled = grad_out * gain_vec
    return inv_rms * (scaled - unit_rows * jnp.mean(scaled * unit_rows, axis=-1, keepdims=True))


def doc_layout(lengths, places):
    doc_ends = jnp.cumsum(lengths)
    starts = doc_ends - lengths
    owners = jnp.sum((places[:, None] >= doc_ends[None, :]).astype(jnp.int32), axis=1)
    member = owners[:, None] == jnp.arange(lengths.shape[0], dtype=jnp.int32)[None, :]
    inner_pos = places - jnp.sum(jnp.where(member, starts[None, :], 0), axis=1)
    return owners, inner_pos


def turn(values, cosine, sine):
    half = values.shape[-1] // 2
    front, back = values[..., :half], values[..., half:]
    return jnp.concatenate([front * cosine - back * sine, back * cosine + front * sine], axis=-1)


def build(n_seq, n_tp):
    seq_bits = n_seq.bit_length() - 1
    tp_bits = n_tp.bit_length() - 1

    def swap(value, axis, bit):
        count = n_seq if axis == "seq" else n_tp
        return lax.ppermute(value, axis, [(i, i ^ (1 << bit)) for i in range(count)])

    def pick(blocks, where, axis):
        return lax.dynamic_index_in_dim(blocks, where, axis, keepdims=False)

    def tp_scatter(part, me):
        tokens, width = part.shape
        held = part.astype(BF).reshape(n_tp, tokens // n_tp, width)
        for bit in range(tp_bits):
            mine = (me >> bit) & 1
            pairs = held.reshape(held.shape[0] // 2, 2, *held.shape[1:])
            got = swap(pick(pairs, 1 - mine, 1), "tp", bit)
            total = pick(pairs, mine, 1).astype(F32) + got.astype(F32)
            held = total if bit == tp_bits - 1 else total.astype(BF)
        return held[0]

    def tp_gather(block, me):
        held = block[None]
        for bit in reversed(range(tp_bits)):
            mine = (me >> bit) & 1
            got = swap(held, "tp", bit)
            low = jnp.where(mine == 0, held, got)
            high = jnp.where(mine == 0, got, held)
            held = jnp.stack([low, high], axis=1).reshape(-1, *block.shape)
        return held.reshape(-1, block.shape[-1])

    def seq_gather(block, order):
        have = {0: block}
        for bit in order:
            keys = sorted(have)
            got = swap(jnp.stack([have[k] for k in keys]), "seq", bit)
            for i, k in enumerate(keys):
                have[k | (1 << bit)] = got[i]
        return [have[r] for r in range(n_seq)]

    def halve(blocks, me_bits, bit, bits_left, last):
        axis = bits_left.index(bit)
        mine = me_bits[bit]
        got = swap(pick(blocks, 1 - mine, axis), "seq", bit)
        total = pick(blocks, mine, axis).astype(F32) + got.astype(F32)
        return total if last else total.astype(BF)

    def seq_finish(blocks, me_bits, left):
        rows = blocks.shape[len(left)]
        front = lax.slice_in_dim(blocks, 0, rows // 2, axis=len(left))
        back = lax.slice_in_dim(blocks, rows // 2, rows, axis=len(left))
        done = []
        for piece, order in ((front, sorted(left)), (back, sorted(left, reverse=True))):
            rest = list(left)
            for i, bit in enumerate(order):
                piece = halve(piece, me_bits, bit, rest, i == len(order) - 1)
                rest.remove(bit)
            done.append(piece)
        return jnp.concatenate(done, axis=0)

    def split_cols(acts, me_bits):
        tokens, width = acts.shape
        blocks = acts.reshape(tokens, n_seq // 2, 2, width // n_seq)
        return (
            pick(blocks, 1 - me_bits[0], 2).reshape(tokens, width // 2),
            pick(blocks, me_bits[0], 2).reshape(tokens, width // 2),
        )

    upper = list(reversed(range(1, seq_bits)))

    def grad_rows(acts_pair, deltas, me_bits):
        away, home = acts_pair
        got = swap(dot_rows(away, deltas).astype(BF), "seq", 0)
        kept = (dot_rows(home, deltas) + got.astype(F32)).astype(BF)
        rows = kept.shape[0] // (n_seq // 2)
        return seq_finish(kept.reshape([2] * len(upper) + [rows, kept.shape[1]]), me_bits, upper)

    def grad_cols(acts, deltas_pair, me_bits):
        away, home = deltas_pair
        got = swap(dot_rows(acts, away).astype(BF), "seq", 0)
        kept = (dot_rows(acts, home) + got.astype(F32)).astype(BF)
        cols = kept.shape[1] // (n_seq // 2)
        blocks = kept.reshape(kept.shape[0], n_seq // 2, cols).transpose(1, 0, 2)
        return seq_finish(blocks.reshape([2] * len(upper) + [kept.shape[0], cols]), me_bits, upper)

    def shards(
        layer_in, attn_gain, query_down, latent_gain, query_up, key_value, attn_out,
        ffn_gain, gate_proj, up_proj, down_proj, out_grad, doc_lengths,
    ):
        n_rows, length, model_dim = layer_in.shape
        seq_me = lax.axis_index("seq")
        tp_me = lax.axis_index("tp")
        me_bits = [(seq_me >> b) & 1 for b in range(seq_bits)]
        heads = query_up.shape[1] // HD
        block = length // n_tp
        scale = HD ** (-0.5)
        places = seq_me * length + jnp.arange(length, dtype=jnp.int32)
        key_places = jnp.concatenate(
            [(seq_me ^ r) * length + jnp.arange(length, dtype=jnp.int32) for r in range(n_seq)]
        )
        frequency = ROPE_BASE ** (-jnp.arange(HD // 2, dtype=F32) / (HD // 2))
        rows = range(n_rows)

        def own(full):
            return lax.dynamic_slice_in_dim(full, tp_me * block, block, 0)

        normed, unit_in, inv_in, latent_norm, unit_lat, inv_lat = [], [], [], [], [], []
        queries, keys, values, masks, cosines, sines = [], [], [], [], [], []
        for r in rows:
            x = layer_in[r].astype(F32)
            unit, inv = unit_norm(x)
            n1 = (unit * attn_gain).astype(BF)
            owners, inner = doc_layout(doc_lengths[r], places)
            key_owner, _ = doc_layout(doc_lengths[r], key_places)
            masks.append(
                (owners[:, None] == key_owner[None, :]) & (key_places[None, :] <= places[:, None])
            )
            angles = inner.astype(F32)[:, None] * frequency
            cosine, sine = jnp.cos(angles), jnp.sin(angles)
            kv = matmul(n1, key_value)
            k_own = turn(kv[:, :HD], cosine, sine).astype(BF)
            v_own = kv[:, HD:].astype(BF)
            order = list(range(1, seq_bits))
            keys.append(jnp.concatenate(seq_gather(k_own, order + [0]), axis=0))
            values.append(jnp.concatenate(seq_gather(v_own, order[::-1] + [0]), axis=0))
            lat = matmul(n1, query_down)
            ul, il = unit_norm(lat)
            ln = (ul * latent_gain).astype(BF)
            raw = matmul(ln, query_up).reshape(length, heads, HD)
            q = turn(raw, cosine[:, None, :], sine[:, None, :]).astype(BF)
            queries.append(q.transpose(1, 0, 2).reshape(heads * length, HD))
            normed.append(n1), unit_in.append(unit), inv_in.append(inv)
            latent_norm.append(ln), unit_lat.append(own(ul)), inv_lat.append(own(il))
            cosines.append(cosine), sines.append(sine)

        def masked(r, scores):
            shaped = scores.reshape(heads, length, -1)
            return shaped, masks[r][None]

        context, log_total, context_low = [], [], []
        middle, normed2, unit_mid, inv_mid = [], [], [], []
        for r in rows:
            scores, allowed = masked(r, dot_cols(queries[r], keys[r]) * scale)
            scores = jnp.where(allowed, scores, NEG_FILL)
            peak = jnp.max(scores, axis=-1, keepdims=True)
            expo = jnp.where(allowed, jnp.exp(scores - peak), 0.0)
            total = jnp.sum(expo, axis=-1, keepdims=True)
            ctx = matmul(expo.astype(BF).reshape(heads * length, -1), values[r])
            ctx = ctx.reshape(heads, length, HD) / total
            log_total.append(peak + jnp.log(total))
            context.append(ctx)
            flat = ctx.astype(BF).transpose(1, 0, 2).reshape(length, heads * HD)
            context_low.append(flat)
            attn = tp_scatter(matmul(flat, attn_out), tp_me)
            mid = own(layer_in[r]).astype(F32) + attn
            unit, inv = unit_norm(mid)
            middle.append(mid), unit_mid.append(unit), inv_mid.append(inv)
            normed2.append(tp_gather((unit * ffn_gain).astype(BF), tp_me))

        hidden, gate_delta, up_delta, layer_out = [], [], [], []
        mid_low, mid_delta, gain_mid = [], [], 0.0
        for r in rows:
            dhidden = dot_cols(out_grad[r], down_proj)
            gate = matmul(normed2[r], gate_proj)
            up = matmul(normed2[r], up_proj)
            sig = jax.nn.sigmoid(gate)
            swish = gate * sig
            hid = (swish * up).astype(BF)
            dgate = (dhidden * up * sig * (1.0 + gate * (1.0 - sig))).astype(BF)
            dup = (dhidden * swish).astype(BF)
            hidden.append(hid), gate_delta.append(dgate), up_delta.append(dup)
            d2 = tp_scatter(dot_cols(dgate, gate_proj) + dot_cols(dup, up_proj), tp_me)
            gain_mid = gain_mid + jnp.sum(d2 * unit_mid[r], axis=0)
            delta = own(out_grad[r]).astype(F32) + rms_backward(d2, unit_mid[r], inv_mid[r], ffn_gain)
            mid_low.append(tp_gather(delta.astype(BF), tp_me))
        for r in rows:
            ffn = tp_scatter(matmul(hidden[r], down_proj), tp_me)
            layer_out.append(tp_gather((middle[r] + ffn).astype(BF), tp_me))

        def joined(parts):
            return jnp.concatenate(parts, axis=0)

        dy_pair = split_cols(joined([out_grad[r] for r in rows]), me_bits)
        down_grad = grad_cols(joined(hidden), dy_pair, me_bits)
        n2_pair = split_cols(joined(normed2), me_bits)
        gate_grad = grad_rows(n2_pair, joined(gate_delta), me_bits)
        up_grad = grad_rows(n2_pair, joined(up_delta), me_bits)

        latent_delta, kv_delta, query_delta, gain_lat = [], [], [], 0.0
        for r in rows:
            dctx = dot_cols(mid_low[r], attn_out).astype(BF)
            dctx = dctx.reshape(length, heads, HD).transpose(1, 0, 2)
            row_delta = jnp.sum(dctx.astype(F32) * context[r], axis=-1, keepdims=True)
            dctx = dctx.reshape(heads * length, HD)
            scores, allowed = masked(r, dot_cols(queries[r], keys[r]) * scale)
            probs = jnp.where(allowed, jnp.exp(scores - log_total[r]), 0.0)
            dprobs = dot_cols(dctx, values[r]).reshape(probs.shape)
            dscores = (probs * (dprobs - row_delta)).astype(BF).reshape(heads * length, -1)
            dq = matmul(dscores, keys[r]) * scale
            dk = dot_rows(dscores, queries[r]) * scale
            dv = dot_rows(probs.astype(BF).reshape(heads * length, -1), dctx)
            dkv = jnp.concatenate([dk, dv], axis=-1).astype(BF).reshape(n_seq, length, 2 * HD)
            got = swap(dkv.reshape(n_seq // 2, 2, length, 2 * HD)[:, 1], "seq", 0)
            kept = dkv.reshape(n_seq // 2, 2, length, 2 * HD)[:, 0].astype(F32) + got.astype(F32)
            kept = kept.astype(BF).reshape([2] * len(upper) + [length, 2 * HD])
            zero_bits = [0] * seq_bits
            kv_sum = seq_finish(kept, zero_bits, upper)
            dq = dq.reshape(heads, length, HD).transpose(1, 0, 2)
            q_low = turn(dq, cosines[r][:, None, :], -sines[r][:, None, :]).astype(BF)
            q_low = q_low.reshape(length, heads * HD)
            query_delta.append(q_low)
            lat = tp_scatter(dot_cols(q_low, query_up), tp_me)
            gain_lat = gain_lat + jnp.sum(lat * unit_lat[r], axis=0)
            lat_low = rms_backward(lat, unit_lat[r], inv_lat[r], latent_gain).astype(BF)
            latent_delta.append(tp_gather(lat_low, tp_me))
            kv_own = tp_scatter(kv_sum, tp_me)
            dk_own = turn(kv_own[:, :HD], own(cosines[r]), -own(sines[r]))
            kv_low = jnp.concatenate([dk_own, kv_own[:, HD:]], axis=-1).astype(BF)
            kv_delta.append(tp_gather(kv_low, tp_me))

        low_pair = split_cols(joined(mid_low), me_bits)
        out_weight_grad = grad_cols(joined(context_low), low_pair, me_bits)
        lat_pair = split_cols(joined(latent_norm), me_bits)
        query_up_grad = grad_rows(lat_pair, joined(query_delta), me_bits)

        input_grad, gain_in = [], 0.0
        for r in rows:
            dn = dot_cols(latent_delta[r], query_down) + dot_cols(kv_delta[r], key_value)
            gain_in = gain_in + jnp.sum(dn * unit_in[r], axis=0)
            delta = mid_low[r].astype(F32) + rms_backward(dn, unit_in[r], inv_in[r], attn_gain)
            input_grad.append(delta.astype(BF))

        lat_cols = query_down.shape[1] // n_tp
        kv_cols = key_value.shape[1] // n_tp
        lat_all, kv_all = joined(latent_delta), joined(kv_delta)
        part = jnp.concatenate(
            [
                lax.dynamic_slice_in_dim(lat_all, tp_me * lat_cols, lat_cols, 1),
                lax.dynamic_slice_in_dim(kv_all, tp_me * kv_cols, kv_cols, 1),
            ],
            axis=1,
        )
        shared = grad_rows(split_cols(joined(normed), me_bits), part, me_bits)
        shared = tp_gather(shared.astype(BF), tp_me).reshape(n_tp, -1, lat_cols + kv_cols)
        shared = shared.astype(F32)
        down_q = shared[:, :, :lat_cols].transpose(1, 0, 2).reshape(-1, n_tp * lat_cols)
        kv_grad = shared[:, :, lat_cols:].transpose(1, 0, 2).reshape(-1, n_tp * kv_cols)

        gains = jnp.concatenate(
            [
                jnp.where(tp_me == 0, gain_in, 0.0).reshape(n_seq, -1),
                gain_mid.reshape(n_seq, -1),
                gain_lat.reshape(n_seq, -1),
            ],
            axis=1,
        )
        gains = gains.reshape([2] * seq_bits + [-1])
        left = list(reversed(range(seq_bits)))
        for bit in range(seq_bits):
            gains = halve(gains, me_bits, bit, left, True)
            left.remove(bit)
        for bit in range(tp_bits):
            gains = gains + swap(gains, "tp", bit)
        d_part = model_dim // n_seq
        return (
            jnp.stack(layer_out),
            jnp.stack(input_grad),
            gains[:d_part],
            down_q,
            gains[2 * d_part :],
            query_up_grad,
            kv_grad,
            out_weight_grad,
            gains[d_part : 2 * d_part],
            gate_grad,
            up_grad,
            down_grad,
        )

    return shards


def solution(mesh):
    return jax.shard_map(
        build(mesh.shape["seq"], mesh.shape["tp"]),
        mesh=mesh,
        in_specs=(
            P(None, "seq", None), P(), P(), P(), P(None, "tp"), P(), P("tp", None), P(),
            P(None, "tp"), P(None, "tp"), P("tp", None), P(None, "seq", None), P(),
        ),
        out_specs=(
            P(None, "seq", None), P(None, "seq", None), P("seq"), P("seq", None), P("seq"),
            P("seq", "tp"), P("seq", None), P("tp", "seq"), P("seq"), P("seq", "tp"),
            P("seq", "tp"), P("tp", "seq"),
        ),
        check_vma=False,
    )
```

```python
import functools

import jax
import jax.numpy as jnp
from jax import lax
from jax.experimental import pallas as pl
from jax.experimental.pallas import tpu as pltpu
from jax.sharding import PartitionSpec as P

HD = 256
EPS = 1e-05
ROPE_BASE = 10000.0
NEG_FILL = -1e30
BF = jnp.bfloat16
F32 = jnp.float32
VMEM_BYTES = 58 * 1024 * 1024
COST = 1e12


def dot(left, right):
    return jnp.dot(left, right, preferred_element_type=F32)


def dot_rows(left, right):
    return lax.dot_general(left, right, (((0,), (0,)), ((), ())), preferred_element_type=F32)


def dot_cols(left, right):
    return lax.dot_general(left, right, (((1,), (1,)), ((), ())), preferred_element_type=F32)


def inverse_rms(values):
    return lax.rsqrt(jnp.mean(values * values, axis=-1, keepdims=True) + EPS)


def back_norm(grad_out, unit_rows, inv_rms, gain):
    scaled = grad_out * gain
    return inv_rms * (scaled - unit_rows * jnp.mean(scaled * unit_rows, axis=-1, keepdims=True))


def turn(values, cosine, sine):
    half = HD // 2
    front, back = values[:, :half], values[:, half:]
    return front * cosine - back * sine, back * cosine + front * sine


def full_spec(shape):
    return pl.BlockSpec(tuple(shape), lambda *_: (0,) * len(shape))


def shape_of(shape, kind=BF):
    return jax.ShapeDtypeStruct(tuple(shape), kind)


def write_pieces(me, source, outs, layout):
    block = outs[0].shape[0] // len(layout[0])
    for out, rels in zip(outs, layout):
        for j, rel in enumerate(rels):
            out[j * block : (j + 1) * block, :] = source[block_rows(me ^ rel, block), :].astype(BF)


MICROS = {
    "front": 4, "query": 7, "attend": 13, "middle": 3, "ffn": 19, "mid_back": 3, "grad": 9, "attend_back": 20,
    "latent_back": 3, "ffn_sum": 3, "spread": 3, "kv_split": 3, "key_back": 3, "join": 3, "input": 8, "shared": 3,
}


def run(kernel, scalars, inputs, outputs, grid=(1,), scratch=(), name=None, carried=()):
    n_in, n_scalars = len(inputs), len(scalars)
    moved = sum(a.size * a.dtype.itemsize for a, _ in inputs)

    def body(*refs):
        kernel(*refs[: n_scalars + n_in], *refs[n_scalars + n_in + len(carried) :])

    return pl.pallas_call(
        body,
        out_shape=[s for s, _ in outputs],
        grid_spec=pltpu.PrefetchScalarGridSpec(
            num_scalar_prefetch=n_scalars,
            grid=grid,
            in_specs=[s for _, s in inputs] + [pl.BlockSpec(memory_space=pl.ANY)] * len(carried),
            out_specs=[s for _, s in outputs],
            scratch_shapes=list(scratch),
        ),
        input_output_aliases={n_scalars + n_in + k: index for k, (index, _) in enumerate(carried)},
        compiler_params=pltpu.CompilerParams(
            dimension_semantics=("arbitrary",) * len(grid), vmem_limit_bytes=VMEM_BYTES
        ),
        cost_estimate=pl.CostEstimate(flops=int(MICROS[name] * COST), bytes_accessed=moved, transcendentals=0),
        name=name,
    )(*scalars, *[a for a, _ in inputs], *[a for _, a in carried])


def total_of(refs):
    total = refs[0][...].astype(F32)
    for ref in refs[1:]:
        total = total + ref[...].astype(F32)
    return total


def row_total(refs, r, n_rows, block):
    total = 0.0
    for ref in refs:
        at = r * (ref.shape[0] // n_rows)
        total = total + ref[at : at + block, :].astype(F32)
    return total


def block_rows(index, size):
    return pl.ds(pl.multiple_of(index * size, size), size)


def front_kernel(info, x_ref, gain_ref, w_ref, cos_ref, sin_ref, n_ref, kv_ref):
    x = x_ref[0].astype(F32)
    normed = (x * inverse_rms(x) * gain_ref[...]).astype(BF)
    n_ref[...] = normed
    kv = dot(normed, w_ref[...])
    front, back = turn(kv[:, :HD], cos_ref[0], sin_ref[0])
    kv_ref[:, : HD // 2] = front.astype(BF)
    kv_ref[:, HD // 2 : HD] = back.astype(BF)
    kv_ref[:, HD:] = kv[:, HD:].astype(BF)


def query_kernel(info, n_ref, wd_ref, gain_ref, wu_ref, cos_ref, sin_ref, ln_ref, ul_ref, il_ref, q_ref, held):
    latent = dot(n_ref[...], wd_ref[...])
    inv = inverse_rms(latent)
    unit = latent * inv
    normed = (unit * gain_ref[...]).astype(BF)
    ln_ref[...] = normed
    block = ul_ref.shape[0]
    held[...] = latent
    mine = held[block_rows(info[0], block), :]
    inv_mine = inverse_rms(mine)
    ul_ref[...] = mine * inv_mine
    il_ref[...] = jnp.broadcast_to(inv_mine, il_ref.shape)
    raw = dot(normed, wu_ref[...])
    cosine, sine = cos_ref[0], sin_ref[0]
    for h in range(raw.shape[1] // HD):
        front, back = turn(raw[:, h * HD : (h + 1) * HD], cosine, sine)
        q_ref[:, h * HD : h * HD + HD // 2] = front.astype(BF)
        q_ref[:, h * HD + HD // 2 : (h + 1) * HD] = back.astype(BF)


def starts_of(docs, row, places):
    end, start = 0, jnp.zeros_like(places)
    for d in range(docs.shape[1]):
        size = docs[row, d]
        end = end + size
        start = start + jnp.where(places >= end, size, 0)
    return start


def attend_kernel(row, order, layout, info, docs, q_ref, ka_ref, kb_ref, w_ref, ctx_ref, lse_ref, *rest):
    pieces, (acc, bias) = rest[: len(layout)], rest[len(layout) :]
    h = pl.program_id(0)
    length = q_ref.shape[0]
    half = len(order) // 2 * length
    me_tp, me_seq = info[0], info[1]

    @pl.when(h == 0)
    def _():
        places = me_seq * length + lax.broadcasted_iota(jnp.int32, (length, 1), 0)
        start = starts_of(docs, row, places)
        column = lax.broadcasted_iota(jnp.int32, (1, length), 1)
        for b, rel in enumerate(order):
            key = (me_seq ^ rel) * length + column
            allowed = (key >= start) & (key <= places)
            bias[:, b * length : (b + 1) * length] = jnp.where(allowed, 0.0, NEG_FILL)

    q = q_ref[...]
    scale = HD ** (-0.5)
    sa = dot_cols(q, ka_ref[:, :HD]) * scale + bias[:, :half]
    sb = dot_cols(q, kb_ref[:, :HD]) * scale + bias[:, half:]
    peak = jnp.maximum(jnp.max(sa, axis=-1, keepdims=True), jnp.max(sb, axis=-1, keepdims=True))
    pa = jnp.exp(sa - peak)
    pb = jnp.exp(sb - peak)
    total = jnp.sum(pa, axis=-1, keepdims=True) + jnp.sum(pb, axis=-1, keepdims=True)
    out = dot(pa.astype(BF), ka_ref[:, HD:]) + dot(pb.astype(BF), kb_ref[:, HD:])
    out = (out / total).astype(BF)
    ctx_ref[...] = out
    lse = jnp.broadcast_to(peak + jnp.log(total), (length, 128))
    lse_ref[0] = jnp.transpose(lse)[:1, :]
    part = dot(out, w_ref[...])

    @pl.when(h == 0)
    def _():
        acc[...] = part

    @pl.when(h > 0)
    def _():
        acc[...] += part

    @pl.when(h == pl.num_programs(0) - 1)
    def _():
        write_pieces(me_tp, acc, pieces, layout)


def middle_kernel(info, *refs):
    parts, (x_ref, gain_ref, mid_ref, n2_ref) = refs[:-4], refs[-4:]
    mid = x_ref[0].astype(F32) + total_of(parts)
    mid_ref[...] = mid
    n2_ref[...] = (mid * inverse_rms(mid) * gain_ref[...]).astype(BF)


def place_pieces(me, pieces, out_ref, rels):
    per = len(rels) // len(pieces)
    block = pieces[0].shape[0] // per
    for i, rel in enumerate(rels):
        at = i % per * block
        out_ref[block_rows(me ^ rel, block), :] = pieces[i // per][at : at + block, :]


def ffn_kernel(n_parts, rels, layout, ff_layout, info, *refs):
    parts = refs[:n_parts]
    dy_ref, wg_hbm, wu_hbm, wd_hbm = refs[n_parts : n_parts + 4]
    outs = refs[n_parts + 4 :]
    n2_ref, hidden_ref = outs[:2]
    ff_refs, pieces = outs[2:4], outs[4 : 4 + len(layout)]
    wg, wu, wd, acc, sems = outs[4 + len(layout) :]
    me = info[0]
    width = hidden_ref.shape[2]
    step = 256
    chunks = [(i, min(step, width - i)) for i in range(0, width, step)]

    def copies(c):
        at, size = chunks[c]
        return (
            pltpu.make_async_copy(wg_hbm.at[:, pl.ds(at, size)], wg.at[:, pl.ds(at, size)], sems.at[0, c]),
            pltpu.make_async_copy(wu_hbm.at[:, pl.ds(at, size)], wu.at[:, pl.ds(at, size)], sems.at[1, c]),
            pltpu.make_async_copy(wd_hbm.at[pl.ds(at, size), :], wd.at[pl.ds(at, size), :], sems.at[2, c]),
        )

    for c in range(len(chunks)):
        for copy in copies(c):
            copy.start()
    place_pieces(me, parts, n2_ref, rels)
    n2 = n2_ref[...]
    dy = dy_ref[0]
    for c, (at, size) in enumerate(chunks):
        here = slice(at, at + size)
        for copy in copies(c):
            copy.wait()
        gate = dot(n2, wg[:, here])
        up = dot(n2, wu[:, here])
        dhid = dot_cols(dy, wd[here, :])
        sig = 1.0 / (1.0 + jnp.exp(-gate))
        swish = gate * sig
        hidden_ref[0, :, here] = (swish * up).astype(BF)
        hidden_ref[1, :, here] = (dhid * up * sig * (1.0 + gate * (1.0 - sig))).astype(BF)
        hidden_ref[2, :, here] = (dhid * swish).astype(BF)
    hid, dgate, dup = hidden_ref[0], hidden_ref[1], hidden_ref[2]
    cut = min(512, acc.shape[1])
    for at in range(0, acc.shape[1], cut):
        here = slice(at, at + cut)
        acc[:, here] = dot_cols(dgate, wg[here, :]) + dot_cols(dup, wu[here, :])
    write_pieces(me, acc, pieces, layout)
    for at in range(0, acc.shape[1], cut):
        here = slice(at, at + cut)
        acc[:, here] = dot(hid, wd[:, here])
    write_pieces(me, acc, ff_refs, ff_layout)


def mid_back_kernel(info, *refs):
    parts, (mid_ref, dy_ref, gain_ref, low_ref, dgain_ref) = refs[:-5], refs[-5:]
    d2 = total_of(parts)
    mid = mid_ref[...]
    inv = inverse_rms(mid)
    unit = mid * inv
    dgain_ref[...] = jnp.sum(d2 * unit, axis=0, keepdims=True)
    low_ref[...] = (dy_ref[0].astype(F32) + back_norm(d2, unit, inv, gain_ref[...])).astype(BF)


def attend_back_kernel(row, order, n_parts, rels, layout, info, docs, *refs):
    lows, refs = refs[:n_parts], refs[n_parts:]
    q_ref, ka_ref, kb_ref, lse_ref, wo_ref, wq_ref, cos_ref, sin_ref = refs[:8]
    low_ref, qlow_ref, keep_ref, send_ref = refs[8:12]
    pieces = refs[12:14]
    bias, dkv, lat = refs[14:]
    h = pl.program_id(0)
    length = q_ref.shape[0]
    half = len(order) // 2 * length
    me_tp, me_seq = info[0], info[1]
    scale = HD ** (-0.5)

    @pl.when(h == 0)
    def _():
        place_pieces(me_tp, lows, low_ref, rels)
        places = me_seq * length + lax.broadcasted_iota(jnp.int32, (1, length), 1)
        start = starts_of(docs, row, places)
        column = lax.broadcasted_iota(jnp.int32, (length, 1), 0)
        for b, rel in enumerate(order):
            key = (me_seq ^ rel) * length + column
            allowed = (key >= start) & (key <= places)
            bias[b * length : (b + 1) * length, :] = jnp.where(allowed, 0.0, NEG_FILL)

    q = q_ref[...]
    dctx = dot_cols(low_ref[...], wo_ref[...]).astype(BF)
    lse = lse_ref[0]
    probs, dprobs = [], []
    delta = 0.0
    for i, kv_ref in enumerate((ka_ref, kb_ref)):
        scores = dot_cols(kv_ref[:, :HD], q) * scale + bias[i * half : (i + 1) * half, :]
        prob = jnp.exp(scores - lse)
        dprob = dot_cols(kv_ref[:, HD:], dctx)
        delta = delta + jnp.sum(prob * dprob, axis=0, keepdims=True)
        probs.append(prob), dprobs.append(dprob)
    dq = 0.0
    for i, kv_ref in enumerate((ka_ref, kb_ref)):
        rows = slice(i * half, (i + 1) * half)
        dscore = (probs[i] * (dprobs[i] - delta)).astype(BF)
        dq = dq + dot_rows(dscore, kv_ref[:, :HD])
        dk = dot(dscore, q) * scale
        dv = dot(probs[i].astype(BF), dctx)

        @pl.when(h == 0)
        def _():
            dkv[rows, :HD] = dk
            dkv[rows, HD:] = dv

        @pl.when(h > 0)
        def _():
            dkv[rows, :HD] += dk
            dkv[rows, HD:] += dv

    front, back = turn(dq * scale, cos_ref[0], -sin_ref[0])
    qlow_ref[:, : HD // 2] = front.astype(BF)
    qlow_ref[:, HD // 2 :] = back.astype(BF)
    part = dot_cols(qlow_ref[...], wq_ref[...])

    @pl.when(h == 0)
    def _():
        lat[...] = part

    @pl.when(h > 0)
    def _():
        lat[...] += part

    @pl.when(h == pl.num_programs(0) - 1)
    def _():
        keep_ref[...] = dkv[:half, :].astype(BF)
        send_ref[...] = dkv[half:, :].astype(BF)
        write_pieces(me_tp, lat, pieces, layout)


def kv_split_kernel(n_rows, layout, info, *refs):
    pieces, held = refs[-3:-1], refs[-1]
    count = (len(refs) - 3) // n_rows
    rows = pieces[0].shape[0] // n_rows
    for r in range(n_rows):
        held[...] = total_of(refs[r * count : (r + 1) * count])
        outs = [piece.at[r * rows : (r + 1) * rows, :] for piece in pieces]
        write_pieces(info[0], held, outs, layout)


def latent_back_kernel(n_rows, info, *refs):
    units, invs = refs[-3 - 2 * n_rows : -3 - n_rows], refs[-3 - n_rows : -3]
    parts, (gain_ref, low_ref, dgain_ref) = refs[: -3 - 2 * n_rows], refs[-3:]
    block = low_ref.shape[0] // n_rows
    dgain = 0.0
    for r in range(n_rows):
        rows = slice(r * block, (r + 1) * block)
        unit, grad = units[r][...], row_total(parts, r, n_rows, block)
        dgain = dgain + jnp.sum(grad * unit, axis=0, keepdims=True)
        low_ref[rows, :] = back_norm(grad, unit, invs[r][:, :1], gain_ref[...]).astype(BF)
    dgain_ref[...] = dgain


def key_back_kernel(n_rows, info, *refs):
    parts, (cos_ref, sin_ref, out_ref) = refs[:-3], refs[-3:]
    block = out_ref.shape[0] // n_rows
    for r in range(n_rows):
        rows = slice(r * block, (r + 1) * block)
        total = row_total(parts, r, n_rows, block)
        front, back = turn(total[:, :HD], cos_ref[r], -sin_ref[r])
        out_ref[rows, : HD // 2] = front.astype(BF)
        out_ref[rows, HD // 2 : HD] = back.astype(BF)
        out_ref[rows, HD:] = total[:, HD:].astype(BF)


def ffn_sum_kernel(n_rows, info, *refs):
    parts, mids, out_ref = refs[: -1 - n_rows], refs[-1 - n_rows : -1], refs[-1]
    block = out_ref.shape[0] // n_rows
    for r in range(n_rows):
        out_ref[r * block : (r + 1) * block, :] = (row_total(parts, r, n_rows, block) + mids[r][...]).astype(BF)


def spread_kernel(rels, info, *refs):
    pieces, out_ref = refs[:-1], refs[-1]
    n_rows, per = out_ref.shape[0], len(rels) // len(pieces)
    block = out_ref.shape[1] // len(rels)
    for i, rel in enumerate(rels):
        for row in range(n_rows):
            at = (i % per * n_rows + row) * block
            out_ref[row, block_rows(info[0] ^ rel, block), :] = pieces[i // per][at : at + block, :]


def join_kernel(n_rows, rels, with_part, info, *refs):
    lats, kvs, outs = refs[:2], refs[2:4], refs[4:]
    me, n_tp = info[0], len(rels)
    per = n_tp // 2
    block = lats[0].shape[0] // (n_rows * per)
    lat_ref, kv_ref = outs[:2]
    for i, rel in enumerate(rels):
        for r in range(n_rows):
            rows = block_rows(r * n_tp + (me ^ rel), block)
            at = (i % per * n_rows + r) * block
            lat_ref[rows, :] = lats[i // per][at : at + block, :]
            kv_ref[rows, :] = kvs[i // per][at : at + block, :]
    if with_part:
        lat_cols, kv_cols = lat_ref.shape[1] // n_tp, kv_ref.shape[1] // n_tp
        outs[2][:, :lat_cols] = lat_ref[:, block_rows(me, lat_cols)]
        outs[2][:, lat_cols:] = kv_ref[:, block_rows(me, kv_cols)]


def input_kernel(info, lat_ref, kv_ref, x_ref, wd_ref, wkv_ref, low_ref, gain_ref, out_ref, dgain_ref):
    dn = dot_cols(lat_ref[...], wd_ref[...]) + dot_cols(kv_ref[...], wkv_ref[...])
    x = x_ref[0].astype(F32)
    inv = inverse_rms(x)
    unit = x * inv
    dgain_ref[...] = jnp.sum(dn * unit, axis=0, keepdims=True)
    out_ref[0] = (low_ref[...].astype(F32) + back_norm(dn, unit, inv, gain_ref[...])).astype(BF)


def grad_kernel(table, *refs):
    count = (len(refs) - 2) // 2
    keep_ref, send_ref = refs[2 * count :]

    def load(ref):
        value = ref[...]
        return value.reshape(-1, value.shape[-1])

    total = dot_rows(load(refs[0]), load(refs[count]))
    for i in range(1, count):
        total = total + dot_rows(load(refs[i]), load(refs[count + i]))
    total = total.astype(BF)
    i, half = pl.program_id(0), pl.num_programs(0) // 2

    @pl.when(i < half)
    def _():
        keep_ref[...] = total

    @pl.when(i >= half)
    def _():
        send_ref[...] = total


def shared_kernel(n_tp, lat_cols, kv_cols, info, *refs):
    parts, (lat_ref, kv_ref) = refs[:n_tp], refs[n_tp:]
    for r in range(n_tp):
        value = parts[r][...].astype(F32)
        lat_ref[:, block_rows(info[0] ^ r, lat_cols)] = value[:, :lat_cols]
        kv_ref[:, block_rows(info[0] ^ r, kv_cols)] = value[:, lat_cols:]


def build(n_seq, n_tp):
    seq_bits = n_seq.bit_length() - 1
    tp_bits = n_tp.bit_length() - 1

    def swap(value, axis, mask):
        count = n_seq if axis == "seq" else n_tp
        return lax.ppermute(value, axis, [(i, i ^ mask) for i in range(count)])

    def spread(bits):
        order = [0]
        for bit in bits:
            order = order + [o | (1 << bit) for o in order]
        return order

    upward = list(range(1, seq_bits))
    routes = (upward + [0], upward[::-1] + [0])
    tp_route = list(reversed(range(tp_bits)))
    tp_rels = spread(tp_route)
    halves = [tp_rels[: n_tp // 2], tp_rels[n_tp // 2 :]]
    singles = [[r] for r in range(n_tp)]
    layouts = [singles, halves]
    rels_back = [list(range(n_tp)), tp_rels]

    def gather(block):
        return [block] + [swap(block, "tp", r) for r in range(1, n_tp)]

    def shards(
        layer_in, attn_gain, query_down, latent_gain, query_up, key_value, attn_out,
        ffn_gain, gate_proj, up_proj, down_proj, out_grad, doc_lengths,
    ):
        n_rows, length, model_dim = layer_in.shape
        lat_dim, q_width = query_up.shape
        ff_dim = gate_proj.shape[1]
        heads = q_width // HD
        block = length // n_tp
        half_keys = n_seq // 2 * length
        rows = range(n_rows)
        seq_me, tp_me = lax.axis_index("seq"), lax.axis_index("tp")
        state = [jnp.stack([tp_me, seq_me, jnp.zeros_like(tp_me)]).astype(jnp.int32)]
        me_bits = [(seq_me >> b) & 1 for b in range(seq_bits)]
        last, due = [], []

        def wait(*arrays):
            due.extend(arrays)

        def after(value):
            ready = last[-1:] + due
            due.clear()
            return lax.optimization_barrier((value, *ready))[0] if ready else value

        def step(kernel, inputs, outputs, table=None, docs=False, **kw):
            scalars = (after(state[0] if table is None else table),) + ((doc_lengths,) if docs else ())
            out = run(kernel, scalars, inputs, outputs, **kw)
            last.append(min(out, key=lambda o: o.size))
            return out

        def total(values, kind):
            out = after(values[-1][0])[values[-1][1]].astype(F32)
            for array, index in values[:-1]:
                out = out + array[index].astype(F32)
            out = out.astype(kind)
            last.append(out)
            return out

        def add(parts, rows, at, kind):
            return total([(p, slice(at * rows, (at + 1) * rows)) for p in parts], kind)

        def halve(parts, rows, axis, bit):
            half = rows // 2
            return parts + [swap(add(parts, half, 1, BF), axis, 1 << bit)], half

        def halve_all(parts, rows, axis, bits):
            for bit in reversed(bits):
                parts, rows = halve(parts, rows, axis, bit)
            return parts, rows

        places = seq_me * length + jnp.arange(length, dtype=jnp.int32)
        ends = jnp.cumsum(doc_lengths, axis=1)
        passed = places[None, :, None] >= ends[:, None, :]
        inner = places[None, :] - jnp.sum(jnp.where(passed, doc_lengths[:, None, :], 0), axis=-1)
        frequency = ROPE_BASE ** (-jnp.arange(HD // 2, dtype=F32) / (HD // 2))
        angles = inner.astype(F32)[:, :, None] * frequency
        cosine, sine = jnp.cos(angles), jnp.sin(angles)
        gain_row = lambda gain: (gain.reshape(1, -1), full_spec((1, gain.shape[0])))

        def whole(array):
            return array, full_spec(array.shape)

        def first(array, count):
            return array, full_spec((count, array.shape[1]))

        def row_of(array, r):
            return array, pl.BlockSpec((1,) + array.shape[1:], lambda *_: (r, 0, 0))

        def own_of(array, r):
            shape = (1, block, array.shape[2])
            return array, pl.BlockSpec(shape, lambda i, info, *_: (r, info[0], 0))

        def new(shape, kind=BF):
            return shape_of(shape, kind), full_spec(shape)

        def head_cols(array):
            return array, pl.BlockSpec((array.shape[0], HD), lambda h, *_: (0, h))

        def head_rows(array):
            return array, pl.BlockSpec((HD, array.shape[1]), lambda h, *_: (h, 0))

        def row_pieces(r, width):
            rows_out = n_tp // 2 * block
            spec = pl.BlockSpec((rows_out, width), lambda *_: (r, 0))
            return [(shape_of((n_rows * rows_out, width)), spec)] * 2

        def pieces_of(layout, width):
            return [new((len(rels) * block, width)) for rels in layout]

        hbm = pl.BlockSpec(memory_space=pl.ANY)
        chunks = -(-ff_dim // 256)

        def rows_of(width, r, spec=None):
            return shape_of((n_rows * length, width)), spec or pl.BlockSpec((length, width), lambda *_: (r, 0))

        def row_block(array, r):
            return array, pl.BlockSpec((length, array.shape[1]), lambda *_: (r, 0))

        def going(held, *pairs):
            return [(index, held[key]) for index, key in pairs] if held else []

        def front(r, held):
            return step(
                front_kernel,
                [row_of(layer_in, r), gain_row(attn_gain), whole(key_value), row_of(cosine, r), row_of(sine, r)],
                [rows_of(model_dim, r), new((length, 2 * HD))], name="front", carried=going(held, (0, 0)),
            )

        def query(r, held):
            return step(
                query_kernel,
                [row_block(normed, r), whole(query_down), gain_row(latent_gain), whole(query_up),
                 row_of(cosine, r), row_of(sine, r)],
                [rows_of(lat_dim, r), new((block, lat_dim), F32), new((block, 128), F32), new((length, q_width))],
                scratch=[pltpu.VMEM((length, lat_dim), F32)], name="query", carried=going(held, (0, 0)),
            )

        def attend(r, held):
            return step(
                functools.partial(attend_kernel, r, spread(routes[r % 2]), layouts[r]),
                [head_cols(queries[r]), whole(near[r]), whole(far[r]), head_rows(attn_out)],
                [
                    rows_of(q_width, r, pl.BlockSpec((length, HD), lambda h, *_: (r, h))),
                    (shape_of((heads, 1, length), F32), pl.BlockSpec((1, 1, length), lambda h, *_: (h, 0, 0))),
                ] + pieces_of(layouts[r], model_dim),
                docs=True, grid=(heads,),
                scratch=[pltpu.VMEM((length, model_dim), F32), pltpu.VMEM((length, 2 * half_keys), F32)],
                name="attend", carried=going(held, (0, 0)),
            )

        def mid_step(r, parts):
            return step(
                middle_kernel, [first(p, block) for p in parts] + [own_of(layer_in, r), gain_row(ffn_gain)],
                [new((block, model_dim), F32), new((block, model_dim))], name="middle",
            )

        def ffn(r, held):
            return step(
                functools.partial(ffn_kernel, len(normed2[r]), range(n_tp), layouts[r], halves),
                [whole(p) for p in normed2[r]] + [row_of(out_grad, r),
                 (gate_proj, hbm), (up_proj, hbm), (down_proj, hbm)],
                [rows_of(model_dim, r),
                 (shape_of((3, n_rows * length, ff_dim)), pl.BlockSpec((3, length, ff_dim), lambda *_: (0, r, 0)))]
                + row_pieces(r, model_dim) + pieces_of(layouts[r], model_dim),
                scratch=[
                    pltpu.VMEM((model_dim, ff_dim), BF), pltpu.VMEM((model_dim, ff_dim), BF),
                    pltpu.VMEM((ff_dim, model_dim), BF), pltpu.VMEM((length, model_dim), F32),
                    pltpu.SemaphoreType.DMA((3, chunks)),
                ],
                name="ffn", carried=going(held, *[(i, i) for i in range(4)]),
            )

        def mid_back(r, parts):
            return step(
                mid_back_kernel,
                [first(p, block) for p in parts] + [whole(middle[r]), own_of(out_grad, r), gain_row(ffn_gain)],
                [new((block, model_dim)), new((1, model_dim), F32)], name="mid_back",
            )

        def attend_back(r, held):
            return step(
                functools.partial(attend_back_kernel, r, spread(routes[r % 2]), len(mid_low[r]), rels_back[r], halves),
                [whole(p) for p in mid_low[r]]
                + [head_cols(queries[r]), whole(near[r]), whole(far[r]),
                   (lse[r], pl.BlockSpec((1, 1, length), lambda h, *_: (h, 0, 0))),
                   head_rows(attn_out), head_cols(query_up), row_of(cosine, r), row_of(sine, r)],
                [rows_of(model_dim, r), rows_of(q_width, r, pl.BlockSpec((length, HD), lambda h, *_: (r, h))),
                 new((half_keys, 2 * HD)), new((half_keys, 2 * HD))] + row_pieces(r, lat_dim),
                docs=True, grid=(heads,),
                scratch=[pltpu.VMEM((2 * half_keys, length), F32), pltpu.VMEM((2 * half_keys, 2 * HD), F32),
                         pltpu.VMEM((length, lat_dim), F32)],
                name="attend_back", carried=going(held, (0, 0), (1, 1), (4, 4), (5, 5)),
            )

        def halve_rows(parts, count):
            half = count // 2 * block
            width = parts[0].shape[1]
            values = [(p.reshape(n_rows, -1, width), (slice(None), slice(half, 2 * half))) for p in parts]
            away = total(values, BF).reshape(n_rows * half, width)
            return parts + [swap(away, "tp", 1 << tp_route[count.bit_length() - 2])]

        def joined_pair(held):
            pair = jnp.concatenate([after(held[0]), held[1]], axis=0)
            last.append(pair)
            return pair

        def gather_start(piece):
            return piece, swap(piece, "tp", 1 << tp_route[0])

        def gather_end(held):
            for bit in tp_route[1:]:
                held = joined_pair(held)
                held = held, swap(held, "tp", 1 << bit)
            return list(held)

        def both(array):
            return [array, swap(array, "seq", 1)]

        def weight_grad(acts, deltas, by_cols, route):
            acts, deltas = [[a if isinstance(a, tuple) else (a, None) for a in pair] for pair in (acts, deltas)]
            bits = routes[route][:-1]
            order = [o for o in spread(bits)]
            count = n_seq // 2
            size = (deltas if by_cols else acts)[0][0].shape[-1] // n_seq
            if size % 128:
                flat = [jnp.concatenate([a for a, _ in pair], axis=0) for pair in (acts, deltas)]
                full = dot_rows(*flat).astype(BF)
                blocks = jnp.take(full.reshape(n_seq, -1, full.shape[1]), jnp.stack([seq_me ^ o for o in order]), axis=0)
                parts, left = halve([blocks.reshape(-1, full.shape[1])], count * size, "seq", bits[-1])
            else:

                def operands(arrays, cut):
                    out = []
                    for array, which in arrays:
                        lead = array.shape[:-1]
                        if which is not None:
                            out.append((array, pl.BlockSpec((1,) + array.shape[1:], lambda i, t: (which, 0, 0))))
                        elif cut:
                            zeros = (0,) * len(lead)
                            out.append((array, pl.BlockSpec(lead + (size,), lambda i, t, z=zeros: z + (t[i],))))
                        else:
                            out.append(whole(array))
                    return out

                shape = (acts[0][0].shape[-1], size) if by_cols else (size, deltas[0][0].shape[-1])
                half = count // 2
                part = shape_of((half * shape[0], shape[1]))
                keep, away = step(
                    grad_kernel, operands(acts, not by_cols) + operands(deltas, by_cols),
                    [(part, pl.BlockSpec(shape, lambda i, t: (jnp.minimum(i, half - 1), 0))),
                     (part, pl.BlockSpec(shape, lambda i, t: (jnp.maximum(i - half, 0), 0)))],
                    table=jnp.stack([seq_me ^ o for o in order]).astype(jnp.int32), grid=(count,), name="grad",
                )
                parts, left = [keep, swap(away, "seq", 1 << bits[-1])], keep.shape[0]
            yield parts[-1]
            parts, left = halve_all(parts, left, "seq", bits[:-1])
            yield parts[-1]
            yield add(parts, left, 0, F32)

        dy_both = both(out_grad)
        held, out = [], None
        for r in rows:
            out = front(r, out)
            held.append([out[1], swap(out[1], "seq", 1 << routes[r % 2][0])])
        normed = out[0]
        normed_both = both(normed)
        unit_lat, inv_lat, queries = [], [], []

        def widen(r, bit):
            pair = joined_pair(held[r])
            held[r] = [pair, swap(pair, "seq", 1 << bit)]

        out = None
        for r in rows:
            out = query(r, out)
            unit_lat.append(out[1]), inv_lat.append(out[2]), queries.append(out[3])
            if r == 0:
                wait(dy_both[1], normed_both[1])
                for bit in range(1, seq_bits - 1):
                    for k in rows:
                        widen(k, routes[k % 2][bit])
        latent_norm = out[0]
        latent_both = both(latent_norm)
        near, far = [None] * n_rows, [None] * n_rows
        for r in rows:
            widen(r, 0)
            near[r], far[r] = held[r]
        wait(latent_both[1])
        lse, part1, out = [], [], None

        def sent_over(pieces):
            if len(pieces) == 2:
                return [pieces[0], swap(pieces[1], "tp", 1)]
            return [pieces[0]] + [swap(pieces[r], "tp", r) for r in range(1, n_tp)]

        for r in rows:
            out = attend(r, out)
            lse.append(out[1])
            part1.append(sent_over(out[2:]))
        context = out[0]
        context_both = both(context)
        sent = n_tp // 2 * block
        middle, normed2 = [], []
        mid, n2 = mid_step(0, part1[0])
        middle.append(mid)
        normed2.append(gather(n2))
        wait(context_both[1])
        part1[1], _ = halve_all(part1[1], sent, "tp", tp_route[:-1])
        wait(*normed2[0])
        mid, n2 = mid_step(1, part1[1])
        middle.append(mid)
        normed2.append(gather(n2))

        part2, out = [], None
        for r in rows:
            out = ffn(r, out)
            part2.append(sent_over(out[4:]))
        n2_all, hidden, ffn_keep, ffn_send = out[:4]
        hidden_both = both(hidden)
        pick = lambda k: [(h, k) for h in hidden_both]
        mid_low, dgain_mid = [], []
        low, dg = mid_back(0, part2[0])
        mid_low.append(gather(low)), dgain_mid.append(dg)
        wait(hidden_both[1])
        part2[1], _ = halve_all(part2[1], sent, "tp", tp_route[:-1])
        n2_both = both(after(n2_all))
        grad_down = weight_grad(pick(0), dy_both, True, 0)
        grad_gate = weight_grad(n2_both, pick(1), False, 1)
        grad_up = weight_grad(n2_both, pick(2), False, 0)
        down_2 = next(grad_down)
        gate_2 = next(grad_gate)
        low, dg = mid_back(1, part2[1])
        wait(*mid_low[0])
        mid_low.append(gather_start(after(low))), dgain_mid.append(dg)

        kv_parts = []
        out = attend_back(0, None)
        kv_parts.append(([out[2], swap(out[3], "seq", 1 << routes[0][-1])], half_keys))
        wait(down_2)
        mid_low[1] = gather_end(mid_low[1])
        up_2 = next(grad_up)
        kv_parts[0] = halve(*kv_parts[0], "seq", routes[0][-2])
        ffn_parts = [ffn_keep, swap(after(ffn_send), "tp", 1)]
        wait(gate_2)
        out = attend_back(1, out)
        low_all, query_low = out[:2]
        kv_parts.append(([out[2], swap(out[3], "seq", 1 << routes[1][-1])], half_keys))
        lat_parts = [out[4], swap(out[5], "tp", 1)]
        kv_parts[0] = halve_all(*kv_parts[0], "seq", routes[0][:-2])
        wait(ffn_parts[1])
        kv_parts[1] = halve(*kv_parts[1], "seq", routes[1][-2])
        for count in [n_tp >> i for i in range(1, tp_bits)]:
            ffn_parts = halve_rows(ffn_parts, count)
        wait(up_2)
        for count in [n_tp >> i for i in range(1, tp_bits)]:
            lat_parts = halve_rows(lat_parts, count)
        low_both = both(after(low_all))
        wait(kv_parts[0][0][-1])
        grad_out = weight_grad(context_both, low_both, True, 1)
        out_2 = next(grad_out)
        kv_parts[1] = halve_all(*kv_parts[1], "seq", routes[1][:-2])
        query_low_both = both(after(query_low))
        lat_low, dgain_lat = step(
            functools.partial(latent_back_kernel, n_rows),
            [whole(p) for p in lat_parts] + [whole(u) for u in unit_lat] + [whole(i) for i in inv_lat]
            + [gain_row(latent_gain)],
            [new((n_rows * block, lat_dim)), new((1, lat_dim), F32)], name="latent_back",
        )
        lat_blocks = gather_start(lat_low)
        grad_query = weight_grad(latent_both, query_low_both, False, 0)
        query_2 = next(grad_query)
        wait(ffn_parts[-1])
        kv_parts = step(
            functools.partial(kv_split_kernel, n_rows, halves),
            [first(p, length) for parts, _ in kv_parts for p in parts],
            [new((n_rows * sent, 2 * HD))] * 2,
            scratch=[pltpu.VMEM((length, 2 * HD), F32)], name="kv_split",
        )
        kv_parts = [kv_parts[0], swap(kv_parts[1], "tp", 1)]
        ffn_own = step(
            functools.partial(ffn_sum_kernel, n_rows), [whole(p) for p in ffn_parts] + [whole(m) for m in middle],
            [new((n_rows * block, model_dim))], name="ffn_sum",
        )[0]
        lat_blocks = gather_end(lat_blocks)
        ffn_blocks = gather_start(after(ffn_own))
        wait(out_2)
        for count in [n_tp >> i for i in range(1, tp_bits)]:
            kv_parts = halve_rows(kv_parts, count)
        down_3 = next(grad_down)
        wait(query_2)
        gate_3 = next(grad_gate)
        own_rows = pl.BlockSpec((n_rows, block, HD // 2), lambda i, info, *_: (0, info[0], 0))
        kv_low = step(
            functools.partial(key_back_kernel, n_rows),
            [whole(p) for p in kv_parts] + [(cosine, own_rows), (sine, own_rows)],
            [new((n_rows * block, 2 * HD))], name="key_back",
        )[0]
        kv_blocks = gather_start(kv_low)
        wait(down_3)
        up_3 = next(grad_up)
        wait(ffn_blocks[1])
        down_grad = next(grad_down)
        kv_blocks = gather_end(kv_blocks)
        wait(gate_3)
        ffn_blocks = gather_end(ffn_blocks)
        out_3 = next(grad_out)
        wait(up_3)
        query_3 = next(grad_query)

        lat_cols, kv_cols = lat_dim // n_tp, 2 * HD // n_tp
        with_part = kv_cols % 128 == 0
        joined = step(
            functools.partial(join_kernel, n_rows, tp_rels, with_part),
            [whole(p) for p in lat_blocks] + [whole(p) for p in kv_blocks],
            [new((n_rows * length, lat_dim)), new((n_rows * length, 2 * HD))]
            + ([new((n_rows * length, lat_cols + kv_cols))] if with_part else []),
            name="join",
        )
        lat_all, kv_all = joined[:2]
        if with_part:
            delta = joined[2]
        else:
            delta = jnp.concatenate(
                [lax.dynamic_slice_in_dim(lat_all, tp_me * lat_cols, lat_cols, 1),
                 lax.dynamic_slice_in_dim(kv_all, tp_me * kv_cols, kv_cols, 1)], axis=1)
        delta_both = both(delta)
        dgain_in = []

        def input_step(r, held):
            out = step(
                input_kernel,
                [row_block(lat_all, r), row_block(kv_all, r), row_of(layer_in, r), whole(query_down), whole(key_value),
                 row_block(low_all, r), gain_row(attn_gain)],
                [(shape_of(layer_in.shape), pl.BlockSpec((1, length, model_dim), lambda *_: (r, 0, 0))),
                 new((1, model_dim), F32)],
                name="input", carried=going(held, (0, 0)),
            )
            dgain_in.append(out[1])
            return out

        wait(out_3, query_3)
        gate_grad = next(grad_gate)
        grad_shared = weight_grad(normed_both, delta_both, False, 0)
        shared_2 = next(grad_shared)
        out = input_step(0, None)
        wait(shared_2)
        shared_3 = next(grad_shared)
        input_grad = input_step(1, out)[0]
        wait(shared_3)

        own_dim = model_dim // n_seq
        shared = gather(next(grad_shared).astype(BF))

        gains = jnp.concatenate(
            [
                jnp.where(tp_me == 0, sum(dgain_in), 0.0).reshape(n_seq, -1),
                sum(dgain_mid).reshape(n_seq, -1),
                dgain_lat.reshape(n_seq, -1),
            ],
            axis=1,
        )
        for bit in range(seq_bits):
            pairs = gains.reshape(-1, 2, gains.shape[-1])
            flip = lax.dynamic_index_in_dim(pairs, 1 - me_bits[bit], 1, keepdims=False)
            mine = lax.dynamic_index_in_dim(pairs, me_bits[bit], 1, keepdims=False)
            gains = mine + swap(flip, "seq", 1 << bit)
        for bit in range(tp_bits):
            gains = gains + swap(gains, "tp", 1 << bit)
        gains = gains[0]
        up_grad, out_weight_grad, query_up_grad = next(grad_up), next(grad_out), next(grad_query)
        layer_out = step(
            functools.partial(spread_kernel, tp_rels), [whole(p) for p in ffn_blocks], [new(layer_in.shape)],
            name="spread",
        )[0]
        if not with_part:
            blocks = jnp.take(jnp.stack(shared), jnp.stack([tp_me ^ r for r in range(n_tp)]), axis=0).astype(F32)
            down_q = blocks[:, :, :lat_cols].transpose(1, 0, 2).reshape(own_dim, lat_dim)
            kv_grad = blocks[:, :, lat_cols:].transpose(1, 0, 2).reshape(own_dim, 2 * HD)
        else:
            down_q, kv_grad = step(
                functools.partial(shared_kernel, n_tp, lat_cols, kv_cols), [whole(p) for p in shared],
                [new((own_dim, lat_dim), F32), new((own_dim, 2 * HD), F32)], name="shared",
            )
        return (
            layer_out, input_grad, gains[:own_dim], down_q, gains[2 * own_dim :], query_up_grad,
            kv_grad, out_weight_grad.reshape(q_width, own_dim), gains[own_dim : 2 * own_dim], gate_grad, up_grad,
            down_grad.reshape(ff_dim, own_dim),
        )

    return shards


def solution(mesh):
    return jax.shard_map(
        build(mesh.shape["seq"], mesh.shape["tp"]),
        mesh=mesh,
        in_specs=(
            P(None, "seq", None), P(), P(), P(), P(None, "tp"), P(), P("tp", None), P(),
            P(None, "tp"), P(None, "tp"), P("tp", None), P(None, "seq", None), P(),
        ),
        out_specs=(
            P(None, "seq", None), P(None, "seq", None), P("seq"), P("seq", None), P("seq"),
            P("seq", "tp"), P("seq", None), P("tp", "seq"), P("seq"), P("seq", "tp"),
            P("seq", "tp"), P("tp", "seq"),
        ),
        check_vma=False,
    )
```

```python
import functools

import jax
import jax.numpy as jnp
from jax import lax
from jax.experimental import pallas as pl
from jax.experimental.pallas import tpu as pltpu
from jax.sharding import PartitionSpec as P

HD = 256
EPS = 1e-05
ROPE_BASE = 10000.0
NEG_FILL = -1e30
BF = jnp.bfloat16
F32 = jnp.float32
VMEM_BYTES = 58 * 1024 * 1024
COST = 1e12


def dot(left, right):
    return jnp.dot(left, right, preferred_element_type=F32)


def dot_rows(left, right):
    return lax.dot_general(left, right, (((0,), (0,)), ((), ())), preferred_element_type=F32)


def dot_cols(left, right):
    return lax.dot_general(left, right, (((1,), (1,)), ((), ())), preferred_element_type=F32)


def inverse_rms(values):
    return lax.rsqrt(jnp.mean(values * values, axis=-1, keepdims=True) + EPS)


def back_norm(grad_out, unit_rows, inv_rms, gain):
    scaled = grad_out * gain
    return inv_rms * (scaled - unit_rows * jnp.mean(scaled * unit_rows, axis=-1, keepdims=True))


def turn(values, cosine, sine):
    half = HD // 2
    front, back = values[:, :half], values[:, half:]
    return front * cosine - back * sine, back * cosine + front * sine


def full_spec(shape):
    return pl.BlockSpec(tuple(shape), lambda *_: (0,) * len(shape))


def shape_of(shape, kind=BF):
    return jax.ShapeDtypeStruct(tuple(shape), kind)


def write_pieces(me, source, outs, layout):
    block = outs[0].shape[0] // len(layout[0])
    for out, rels in zip(outs, layout):
        for j, rel in enumerate(rels):
            out[j * block : (j + 1) * block, :] = source[block_rows(me ^ rel, block), :].astype(BF)


MICROS = {
    "front": 4, "query": 7, "attend": 13, "middle": 3, "ffn": 19, "mid_back": 3, "grad": 9, "own_grad": 12, "pause": 3, "attend_back": 20,
    "latent_back": 3, "ffn_sum": 3, "spread": 3, "kv_split": 3, "key_back": 3, "join": 3, "input": 8, "shared": 3,
}


def run(kernel, scalars, inputs, outputs, grid=(1,), scratch=(), name=None, carried=()):
    n_in, n_scalars = len(inputs), len(scalars)
    moved = sum(a.size * a.dtype.itemsize for a, _ in inputs)

    def body(*refs):
        kernel(*refs[: n_scalars + n_in], *refs[n_scalars + n_in + len(carried) :])

    return pl.pallas_call(
        body,
        out_shape=[s for s, _ in outputs],
        grid_spec=pltpu.PrefetchScalarGridSpec(
            num_scalar_prefetch=n_scalars,
            grid=grid,
            in_specs=[s for _, s in inputs] + [pl.BlockSpec(memory_space=pl.ANY)] * len(carried),
            out_specs=[s for _, s in outputs],
            scratch_shapes=list(scratch),
        ),
        input_output_aliases={n_scalars + n_in + k: index for k, (index, _) in enumerate(carried)},
        compiler_params=pltpu.CompilerParams(
            dimension_semantics=("arbitrary",) * len(grid), vmem_limit_bytes=VMEM_BYTES
        ),
        cost_estimate=pl.CostEstimate(flops=int(MICROS[name] * COST), bytes_accessed=moved, transcendentals=0),
        name=name,
    )(*scalars, *[a for a, _ in inputs], *[a for _, a in carried])


def total_of(refs):
    total = refs[0][...].astype(F32)
    for ref in refs[1:]:
        total = total + ref[...].astype(F32)
    return total


def row_total(refs, r, n_rows, block):
    total = 0.0
    for ref in refs:
        at = r * (ref.shape[0] // n_rows)
        total = total + ref[at : at + block, :].astype(F32)
    return total


def block_rows(index, size):
    return pl.ds(pl.multiple_of(index * size, size), size)


def front_kernel(info, x_ref, gain_ref, w_ref, cos_ref, sin_ref, n_ref, kv_ref):
    x = x_ref[0].astype(F32)
    normed = (x * inverse_rms(x) * gain_ref[...]).astype(BF)
    n_ref[...] = normed
    kv = dot(normed, w_ref[...])
    front, back = turn(kv[:, :HD], cos_ref[0], sin_ref[0])
    kv_ref[:, : HD // 2] = front.astype(BF)
    kv_ref[:, HD // 2 : HD] = back.astype(BF)
    kv_ref[:, HD:] = kv[:, HD:].astype(BF)


def query_kernel(info, n_ref, wd_ref, gain_ref, wu_ref, cos_ref, sin_ref, ln_ref, ul_ref, il_ref, q_ref, held):
    latent = dot(n_ref[...], wd_ref[...])
    inv = inverse_rms(latent)
    unit = latent * inv
    normed = (unit * gain_ref[...]).astype(BF)
    ln_ref[...] = normed
    block = ul_ref.shape[0]
    held[...] = latent
    mine = held[block_rows(info[0], block), :]
    inv_mine = inverse_rms(mine)
    ul_ref[...] = mine * inv_mine
    il_ref[...] = jnp.broadcast_to(inv_mine, il_ref.shape)
    raw = dot(normed, wu_ref[...])
    cosine, sine = cos_ref[0], sin_ref[0]
    for h in range(raw.shape[1] // HD):
        front, back = turn(raw[:, h * HD : (h + 1) * HD], cosine, sine)
        q_ref[:, h * HD : h * HD + HD // 2] = front.astype(BF)
        q_ref[:, h * HD + HD // 2 : (h + 1) * HD] = back.astype(BF)


def starts_of(docs, row, places):
    end, start = 0, jnp.zeros_like(places)
    for d in range(docs.shape[1]):
        size = docs[row, d]
        end = end + size
        start = start + jnp.where(places >= end, size, 0)
    return start


def attend_kernel(row, order, layout, info, docs, q_ref, ka_ref, kb_ref, w_ref, ctx_ref, lse_ref, *rest):
    pieces, (acc, bias) = rest[: len(layout)], rest[len(layout) :]
    h = pl.program_id(0)
    length = q_ref.shape[0]
    half = len(order) // 2 * length
    me_tp, me_seq = info[0], info[1]

    @pl.when(h == 0)
    def _():
        places = me_seq * length + lax.broadcasted_iota(jnp.int32, (length, 1), 0)
        start = starts_of(docs, row, places)
        column = lax.broadcasted_iota(jnp.int32, (1, length), 1)
        for b, rel in enumerate(order):
            key = (me_seq ^ rel) * length + column
            allowed = (key >= start) & (key <= places)
            bias[:, b * length : (b + 1) * length] = jnp.where(allowed, 0.0, NEG_FILL)

    q = q_ref[...]
    scale = HD ** (-0.5)
    sa = dot_cols(q, ka_ref[:, :HD]) * scale + bias[:, :half]
    sb = dot_cols(q, kb_ref[:, :HD]) * scale + bias[:, half:]
    peak = jnp.maximum(jnp.max(sa, axis=-1, keepdims=True), jnp.max(sb, axis=-1, keepdims=True))
    pa = jnp.exp(sa - peak)
    pb = jnp.exp(sb - peak)
    total = jnp.sum(pa, axis=-1, keepdims=True) + jnp.sum(pb, axis=-1, keepdims=True)
    out = dot(pa.astype(BF), ka_ref[:, HD:]) + dot(pb.astype(BF), kb_ref[:, HD:])
    out = (out / total).astype(BF)
    ctx_ref[...] = out
    lse = jnp.broadcast_to(peak + jnp.log(total), (length, 128))
    lse_ref[0] = jnp.transpose(lse)[:1, :]
    part = dot(out, w_ref[...])

    @pl.when(h == 0)
    def _():
        acc[...] = part

    @pl.when(h > 0)
    def _():
        acc[...] += part

    @pl.when(h == pl.num_programs(0) - 1)
    def _():
        write_pieces(me_tp, acc, pieces, layout)


def middle_kernel(info, *refs):
    parts, (x_ref, gain_ref, mid_ref, n2_ref) = refs[:-4], refs[-4:]
    mid = x_ref[0].astype(F32) + total_of(parts)
    mid_ref[...] = mid
    n2_ref[...] = (mid * inverse_rms(mid) * gain_ref[...]).astype(BF)


def place_pieces(me, pieces, out_ref, rels):
    per = len(rels) // len(pieces)
    block = pieces[0].shape[0] // per
    for i, rel in enumerate(rels):
        at = i % per * block
        out_ref[block_rows(me ^ rel, block), :] = pieces[i // per][at : at + block, :]


def ffn_kernel(n_parts, rels, layout, ff_layout, info, *refs):
    parts = refs[:n_parts]
    dy_ref, wg_hbm, wu_hbm, wd_hbm = refs[n_parts : n_parts + 4]
    outs = refs[n_parts + 4 :]
    n2_ref, hidden_ref = outs[:2]
    ff_refs, pieces = outs[2:4], outs[4 : 4 + len(layout)]
    wg, wu, wd, acc, sems = outs[4 + len(layout) :]
    me = info[0]
    width = hidden_ref.shape[2]
    step = 256
    chunks = [(i, min(step, width - i)) for i in range(0, width, step)]

    def copies(c):
        at, size = chunks[c]
        return (
            pltpu.make_async_copy(wg_hbm.at[:, pl.ds(at, size)], wg.at[:, pl.ds(at, size)], sems.at[0, c]),
            pltpu.make_async_copy(wu_hbm.at[:, pl.ds(at, size)], wu.at[:, pl.ds(at, size)], sems.at[1, c]),
            pltpu.make_async_copy(wd_hbm.at[pl.ds(at, size), :], wd.at[pl.ds(at, size), :], sems.at[2, c]),
        )

    for c in range(len(chunks)):
        for copy in copies(c):
            copy.start()
    place_pieces(me, parts, n2_ref, rels)
    n2 = n2_ref[...]
    dy = dy_ref[0]
    for c, (at, size) in enumerate(chunks):
        here = slice(at, at + size)
        for copy in copies(c):
            copy.wait()
        gate = dot(n2, wg[:, here])
        up = dot(n2, wu[:, here])
        dhid = dot_cols(dy, wd[here, :])
        sig = 1.0 / (1.0 + jnp.exp(-gate))
        swish = gate * sig
        hidden_ref[0, :, here] = (swish * up).astype(BF)
        hidden_ref[1, :, here] = (dhid * up * sig * (1.0 + gate * (1.0 - sig))).astype(BF)
        hidden_ref[2, :, here] = (dhid * swish).astype(BF)
    hid, dgate, dup = hidden_ref[0], hidden_ref[1], hidden_ref[2]
    cut = min(512, acc.shape[1])
    for at in range(0, acc.shape[1], cut):
        here = slice(at, at + cut)
        acc[:, here] = dot_cols(dgate, wg[here, :]) + dot_cols(dup, wu[here, :])
    write_pieces(me, acc, pieces, layout)
    for at in range(0, acc.shape[1], cut):
        here = slice(at, at + cut)
        acc[:, here] = dot(hid, wd[:, here])
    write_pieces(me, acc, ff_refs, ff_layout)


def mid_back_kernel(info, *refs):
    parts, (mid_ref, dy_ref, gain_ref, low_ref) = refs[:-4], refs[-4:]
    d2 = total_of(parts)
    mid = mid_ref[...]
    inv = inverse_rms(mid)
    unit = mid * inv
    low_ref[...] = (dy_ref[0].astype(F32) + back_norm(d2, unit, inv, gain_ref[...])).astype(BF)


def attend_back_kernel(row, order, n_parts, rels, layout, info, docs, *refs):
    lows, refs = refs[:n_parts], refs[n_parts:]
    q_ref, ka_ref, kb_ref, lse_ref, wo_ref, wq_ref, cos_ref, sin_ref = refs[:8]
    low_ref, qlow_ref, keep_ref, send_ref = refs[8:12]
    pieces = refs[12:14]
    bias, dkv, lat = refs[14:]
    h = pl.program_id(0)
    length = q_ref.shape[0]
    half = len(order) // 2 * length
    me_tp, me_seq = info[0], info[1]
    scale = HD ** (-0.5)

    @pl.when(h == 0)
    def _():
        place_pieces(me_tp, lows, low_ref, rels)
        places = me_seq * length + lax.broadcasted_iota(jnp.int32, (1, length), 1)
        start = starts_of(docs, row, places)
        column = lax.broadcasted_iota(jnp.int32, (length, 1), 0)
        for b, rel in enumerate(order):
            key = (me_seq ^ rel) * length + column
            allowed = (key >= start) & (key <= places)
            bias[b * length : (b + 1) * length, :] = jnp.where(allowed, 0.0, NEG_FILL)

    q = q_ref[...]
    dctx = dot_cols(low_ref[...], wo_ref[...]).astype(BF)
    lse = lse_ref[0]
    probs, dprobs = [], []
    delta = 0.0
    for i, kv_ref in enumerate((ka_ref, kb_ref)):
        scores = dot_cols(kv_ref[:, :HD], q) * scale + bias[i * half : (i + 1) * half, :]
        prob = jnp.exp(scores - lse)
        dprob = dot_cols(kv_ref[:, HD:], dctx)
        delta = delta + jnp.sum(prob * dprob, axis=0, keepdims=True)
        probs.append(prob), dprobs.append(dprob)
    dq = 0.0
    for i, kv_ref in enumerate((ka_ref, kb_ref)):
        rows = slice(i * half, (i + 1) * half)
        dscore = (probs[i] * (dprobs[i] - delta)).astype(BF)
        dq = dq + dot_rows(dscore, kv_ref[:, :HD])
        dk = dot(dscore, q) * scale
        dv = dot(probs[i].astype(BF), dctx)

        @pl.when(h == 0)
        def _():
            dkv[rows, :HD] = dk
            dkv[rows, HD:] = dv

        @pl.when(h > 0)
        def _():
            dkv[rows, :HD] += dk
            dkv[rows, HD:] += dv

    front, back = turn(dq * scale, cos_ref[0], -sin_ref[0])
    qlow_ref[:, : HD // 2] = front.astype(BF)
    qlow_ref[:, HD // 2 :] = back.astype(BF)
    part = dot_cols(qlow_ref[...], wq_ref[...])

    @pl.when(h == 0)
    def _():
        lat[...] = part

    @pl.when(h > 0)
    def _():
        lat[...] += part

    @pl.when(h == pl.num_programs(0) - 1)
    def _():
        keep_ref[...] = dkv[:half, :].astype(BF)
        send_ref[...] = dkv[half:, :].astype(BF)
        write_pieces(me_tp, lat, pieces, layout)


def kv_split_kernel(n_rows, layout, info, *refs):
    pieces, held = refs[-1 - len(layout) : -1], refs[-1]
    count = (len(refs) - 1 - len(layout)) // n_rows
    rows = pieces[0].shape[0] // n_rows
    for r in range(n_rows):
        held[...] = total_of(refs[r * count : (r + 1) * count])
        outs = [piece.at[r * rows : (r + 1) * rows, :] for piece in pieces]
        write_pieces(info[0], held, outs, layout)


def latent_back_kernel(n_rows, info, *refs):
    units, invs = refs[-2 - 2 * n_rows : -2 - n_rows], refs[-2 - n_rows : -2]
    parts, (gain_ref, low_ref) = refs[: -2 - 2 * n_rows], refs[-2:]
    block = low_ref.shape[0] // n_rows
    for r in range(n_rows):
        rows = slice(r * block, (r + 1) * block)
        unit, grad = units[r][...], row_total(parts, r, n_rows, block)
        low_ref[rows, :] = back_norm(grad, unit, invs[r][:, :1], gain_ref[...]).astype(BF)


def key_back_kernel(n_rows, info, *refs):
    parts, (cos_ref, sin_ref, out_ref) = refs[:-3], refs[-3:]
    block = out_ref.shape[0] // n_rows
    for r in range(n_rows):
        rows = slice(r * block, (r + 1) * block)
        total = row_total(parts, r, n_rows, block)
        front, back = turn(total[:, :HD], cos_ref[r], -sin_ref[r])
        out_ref[rows, : HD // 2] = front.astype(BF)
        out_ref[rows, HD // 2 : HD] = back.astype(BF)
        out_ref[rows, HD:] = total[:, HD:].astype(BF)


def ffn_sum_kernel(n_rows, info, *refs):
    parts, mids, out_ref = refs[: -1 - n_rows], refs[-1 - n_rows : -1], refs[-1]
    block = out_ref.shape[0] // n_rows
    for r in range(n_rows):
        out_ref[r * block : (r + 1) * block, :] = (row_total(parts, r, n_rows, block) + mids[r][...]).astype(BF)


def spread_kernel(rels, info, *refs):
    pieces, out_ref = refs[:-1], refs[-1]
    n_rows, per = out_ref.shape[0], len(rels) // len(pieces)
    block = out_ref.shape[1] // len(rels)
    for i, rel in enumerate(rels):
        for row in range(n_rows):
            at = (i % per * n_rows + row) * block
            out_ref[row, block_rows(info[0] ^ rel, block), :] = pieces[i // per][at : at + block, :]


def join_kernel(n_rows, rels, count, info, *refs):
    pieces, all_ref = refs[:count], refs[count]
    me, n_tp = info[0], len(rels)
    per = n_tp // count
    block = pieces[0].shape[0] // (n_rows * per)
    for i, rel in enumerate(rels):
        for r in range(n_rows):
            at = (i % per * n_rows + r) * block
            all_ref[block_rows(r * n_tp + (me ^ rel), block), :] = pieces[i // per][at : at + block, :]
    if len(refs) > count + 1:
        part_ref = refs[count + 1]
        part_ref[...] = all_ref[:, block_rows(me, part_ref.shape[1])]


def input_kernel(info, lat_ref, kv_ref, x_ref, wd_ref, wkv_ref, low_ref, gain_ref, out_ref):
    dn = dot_cols(lat_ref[...], wd_ref[...]) + dot_cols(kv_ref[...], wkv_ref[...])
    x = x_ref[0].astype(F32)
    inv = inverse_rms(x)
    unit = x * inv
    out_ref[0] = (low_ref[...].astype(F32) + back_norm(dn, unit, inv, gain_ref[...])).astype(BF)


def grad_kernel(table, *refs):
    count = (len(refs) - 2) // 2
    keep_ref, send_ref = refs[2 * count :]

    def load(ref):
        value = ref[...]
        return value.reshape(-1, value.shape[-1])

    total = dot_rows(load(refs[0]), load(refs[count]))
    for i in range(1, count):
        total = total + dot_rows(load(refs[i]), load(refs[count + i]))
    total = total.astype(BF)
    i, half = pl.program_id(0), pl.num_programs(0) // 2

    @pl.when(i < half)
    def _():
        keep_ref[...] = total

    @pl.when(i >= half)
    def _():
        send_ref[...] = total


def own_grad_kernel(info, acts_ref, *refs):
    deltas, out_ref = refs[:-1], refs[-1]
    acts = acts_ref[...]
    acts = acts.reshape(-1, acts.shape[-1])
    at = 0
    for delta_ref in deltas:
        delta = delta_ref[...]
        delta = delta.reshape(-1, delta.shape[-1])
        out_ref[:, at : at + delta.shape[1]] = dot_rows(acts, delta).astype(BF)
        at += delta.shape[1]


def pause_kernel(info, out_ref):
    for i in range(out_ref.shape[0]):
        out_ref[i] = info[i]


def shared_kernel(n_tp, info, *refs):
    parts, out_ref = refs[:n_tp], refs[n_tp]
    for r in range(n_tp):
        out_ref[:, block_rows(info[0] ^ r, parts[r].shape[1])] = parts[r][...].astype(F32)


def build(n_seq, n_tp):
    seq_bits = n_seq.bit_length() - 1
    tp_bits = n_tp.bit_length() - 1

    def swap(value, axis, mask):
        count = n_seq if axis == "seq" else n_tp
        return lax.ppermute(value, axis, [(i, i ^ mask) for i in range(count)])

    def spread(bits):
        order = [0]
        for bit in bits:
            order = order + [o | (1 << bit) for o in order]
        return order

    upward = list(range(1, seq_bits))
    routes = (upward + [0], upward[::-1] + [0])
    tp_route = list(reversed(range(tp_bits)))
    tp_rels = spread(tp_route)
    halves = [tp_rels[: n_tp // 2], tp_rels[n_tp // 2 :]]
    singles = [[r] for r in range(n_tp)]
    layouts = [singles, halves]

    def gather(block):
        return [block] + [swap(block, "tp", r) for r in range(1, n_tp)]

    def shards(
        layer_in, attn_gain, query_down, latent_gain, query_up, key_value, attn_out,
        ffn_gain, gate_proj, up_proj, down_proj, out_grad, doc_lengths,
    ):
        n_rows, length, model_dim = layer_in.shape
        lat_dim, q_width = query_up.shape
        ff_dim = gate_proj.shape[1]
        heads = q_width // HD
        block = length // n_tp
        half_keys = n_seq // 2 * length
        rows = range(n_rows)
        seq_me, tp_me = lax.axis_index("seq"), lax.axis_index("tp")
        state = [jnp.stack([tp_me, seq_me, jnp.zeros_like(tp_me)]).astype(jnp.int32)]
        last, due = [], []

        def wait(*arrays):
            due.extend(arrays)

        def pause():
            state[0] = step(
                pause_kernel, [], [(shape_of((3,), jnp.int32), pl.BlockSpec(memory_space=pltpu.SMEM))], name="pause",
            )[0]

        def after(value):
            ready = last[-1:] + due
            due.clear()
            return lax.optimization_barrier((value, *ready))[0] if ready else value

        def step(kernel, inputs, outputs, table=None, docs=False, **kw):
            scalars = (after(state[0] if table is None else table),) + ((doc_lengths,) if docs else ())
            out = run(kernel, scalars, inputs, outputs, **kw)
            last.append(min(out, key=lambda o: o.size))
            return out

        def total(values, kind):
            out = after(values[-1][0])[values[-1][1]].astype(F32)
            for array, index in values[:-1]:
                out = out + array[index].astype(F32)
            out = out.astype(kind)
            last.append(out)
            return out

        def add(parts, rows, at, kind):
            return total([(p, slice(at * rows, (at + 1) * rows)) for p in parts], kind)

        def halve(parts, rows, axis, bit):
            half = rows // 2
            return parts + [swap(add(parts, half, 1, BF), axis, 1 << bit)], half

        def halve_all(parts, rows, axis, bits):
            for bit in reversed(bits):
                parts, rows = halve(parts, rows, axis, bit)
            return parts, rows

        places = seq_me * length + jnp.arange(length, dtype=jnp.int32)
        ends = jnp.cumsum(doc_lengths, axis=1)
        passed = places[None, :, None] >= ends[:, None, :]
        inner = places[None, :] - jnp.sum(jnp.where(passed, doc_lengths[:, None, :], 0), axis=-1)
        frequency = ROPE_BASE ** (-jnp.arange(HD // 2, dtype=F32) / (HD // 2))
        angles = inner.astype(F32)[:, :, None] * frequency
        cosine, sine = jnp.cos(angles), jnp.sin(angles)
        gain_row = lambda gain: (gain.reshape(1, -1), full_spec((1, gain.shape[0])))

        def whole(array):
            return array, full_spec(array.shape)

        def first(array, count):
            return array, full_spec((count, array.shape[1]))

        def row_of(array, r):
            return array, pl.BlockSpec((1,) + array.shape[1:], lambda *_: (r, 0, 0))

        def own_of(array, r):
            shape = (1, block, array.shape[2])
            return array, pl.BlockSpec(shape, lambda i, info, *_: (r, info[0], 0))

        def new(shape, kind=BF):
            return shape_of(shape, kind), full_spec(shape)

        def head_cols(array):
            return array, pl.BlockSpec((array.shape[0], HD), lambda h, *_: (0, h))

        def head_rows(array):
            return array, pl.BlockSpec((HD, array.shape[1]), lambda h, *_: (h, 0))

        def row_pieces(r, width):
            rows_out = n_tp // 2 * block
            spec = pl.BlockSpec((rows_out, width), lambda *_: (r, 0))
            return [(shape_of((n_rows * rows_out, width)), spec)] * 2

        def pieces_of(layout, width):
            return [new((len(rels) * block, width)) for rels in layout]

        hbm = pl.BlockSpec(memory_space=pl.ANY)
        chunks = -(-ff_dim // 256)

        def rows_of(width, r, spec=None):
            return shape_of((n_rows * length, width)), spec or pl.BlockSpec((length, width), lambda *_: (r, 0))

        def row_block(array, r):
            return array, pl.BlockSpec((length, array.shape[1]), lambda *_: (r, 0))

        def going(held, *pairs):
            return [(index, held[key]) for index, key in pairs] if held else []

        def front(r, held):
            return step(
                front_kernel,
                [row_of(layer_in, r), gain_row(attn_gain), whole(key_value), row_of(cosine, r), row_of(sine, r)],
                [rows_of(model_dim, r), new((length, 2 * HD))], name="front", carried=going(held, (0, 0)),
            )

        def query(r, held):
            return step(
                query_kernel,
                [row_block(normed, r), whole(query_down), gain_row(latent_gain), whole(query_up),
                 row_of(cosine, r), row_of(sine, r)],
                [rows_of(lat_dim, r), new((block, lat_dim), F32), new((block, 128), F32), new((length, q_width))],
                scratch=[pltpu.VMEM((length, lat_dim), F32)], name="query", carried=going(held, (0, 0)),
            )

        def attend(r, held):
            return step(
                functools.partial(attend_kernel, r, spread(routes[(r + 1) % 2]), layouts[r]),
                [head_cols(queries[r]), whole(near[r]), whole(far[r]), head_rows(attn_out)],
                [
                    rows_of(q_width, r, pl.BlockSpec((length, HD), lambda h, *_: (r, h))),
                    (shape_of((heads, 1, length), F32), pl.BlockSpec((1, 1, length), lambda h, *_: (h, 0, 0))),
                ] + pieces_of(layouts[r], model_dim),
                docs=True, grid=(heads,),
                scratch=[pltpu.VMEM((length, model_dim), F32), pltpu.VMEM((length, 2 * half_keys), F32)],
                name="attend", carried=going(held, (0, 0)),
            )

        def mid_step(r, parts):
            return step(
                middle_kernel, [first(p, block) for p in parts] + [own_of(layer_in, r), gain_row(ffn_gain)],
                [new((block, model_dim), F32), new((block, model_dim))], name="middle",
            )

        def ffn(r, held):
            return step(
                functools.partial(ffn_kernel, len(normed2[r]), range(n_tp), layouts[r], halves),
                [whole(p) for p in normed2[r]] + [row_of(out_grad, r),
                 (gate_proj, hbm), (up_proj, hbm), (down_proj, hbm)],
                [rows_of(model_dim, r),
                 (shape_of((3, n_rows * length, ff_dim)), pl.BlockSpec((3, length, ff_dim), lambda *_: (0, r, 0)))]
                + row_pieces(r, model_dim) + pieces_of(layouts[r], model_dim),
                scratch=[
                    pltpu.VMEM((model_dim, ff_dim), BF), pltpu.VMEM((model_dim, ff_dim), BF),
                    pltpu.VMEM((ff_dim, model_dim), BF), pltpu.VMEM((length, model_dim), F32),
                    pltpu.SemaphoreType.DMA((3, chunks)),
                ],
                name="ffn", carried=going(held, *[(i, i) for i in range(4)]),
            )

        def mid_back(r, parts):
            return step(
                mid_back_kernel,
                [first(p, block) for p in parts] + [whole(middle[r]), own_of(out_grad, r), gain_row(ffn_gain)],
                [new((block, model_dim))], name="mid_back",
            )[0]

        def attend_back(r, held):
            return step(
                functools.partial(attend_back_kernel, r, spread(routes[(r + 1) % 2]), len(mid_low[r]), range(n_tp), halves),
                [whole(p) for p in mid_low[r]]
                + [head_cols(queries[r]), whole(near[r]), whole(far[r]),
                   (lse[r], pl.BlockSpec((1, 1, length), lambda h, *_: (h, 0, 0))),
                   head_rows(attn_out), head_cols(query_up), row_of(cosine, r), row_of(sine, r)],
                [rows_of(model_dim, r), rows_of(q_width, r, pl.BlockSpec((length, HD), lambda h, *_: (r, h))),
                 new((half_keys, 2 * HD)), new((half_keys, 2 * HD))] + row_pieces(r, lat_dim),
                docs=True, grid=(heads,),
                scratch=[pltpu.VMEM((2 * half_keys, length), F32), pltpu.VMEM((2 * half_keys, 2 * HD), F32),
                         pltpu.VMEM((length, lat_dim), F32)],
                name="attend_back", carried=going(held, (0, 0), (1, 1), (4, 4), (5, 5)),
            )

        def halve_rows(parts, count):
            half = count // 2 * block
            width = parts[0].shape[1]
            values = [(p.reshape(n_rows, -1, width), (slice(None), slice(half, 2 * half))) for p in parts]
            away = total(values, BF).reshape(n_rows * half, width)
            return parts + [swap(away, "tp", 1 << tp_route[count.bit_length() - 2])]

        def joined_pair(held):
            pair = jnp.concatenate([after(held[0]), held[1]], axis=0)
            last.append(pair)
            return pair

        def gather_start(piece):
            return piece, swap(piece, "tp", 1 << tp_route[0])

        def gather_end(held):
            for bit in tp_route[1:]:
                held = joined_pair(held)
                held = held, swap(held, "tp", 1 << bit)
            return list(held)

        def both(array):
            return [array, swap(array, "seq", 1)]

        def weight_grad(acts, deltas, by_cols, route):
            acts, deltas = [[a if isinstance(a, tuple) else (a, None) for a in pair] for pair in (acts, deltas)]
            bits = routes[route][:-1]
            order = [o for o in spread(bits)]
            count = n_seq // 2
            size = (deltas if by_cols else acts)[0][0].shape[-1] // n_seq
            if size % 128:
                flat = [jnp.concatenate([a for a, _ in pair], axis=0) for pair in (acts, deltas)]
                full = dot_rows(*flat).astype(BF)
                blocks = jnp.take(full.reshape(n_seq, -1, full.shape[1]), jnp.stack([seq_me ^ o for o in order]), axis=0)
                parts, left = halve([blocks.reshape(-1, full.shape[1])], count * size, "seq", bits[-1])
            else:

                def operands(arrays, cut):
                    out = []
                    for array, which in arrays:
                        lead = array.shape[:-1]
                        if which is not None:
                            out.append((array, pl.BlockSpec((1,) + array.shape[1:], lambda i, t: (which, 0, 0))))
                        elif cut:
                            zeros = (0,) * len(lead)
                            out.append((array, pl.BlockSpec(lead + (size,), lambda i, t, z=zeros: z + (t[i],))))
                        else:
                            out.append(whole(array))
                    return out

                shape = (acts[0][0].shape[-1], size) if by_cols else (size, deltas[0][0].shape[-1])
                half = count // 2
                part = shape_of((half * shape[0], shape[1]))
                keep, away = step(
                    grad_kernel, operands(acts, not by_cols) + operands(deltas, by_cols),
                    [(part, pl.BlockSpec(shape, lambda i, t: (jnp.minimum(i, half - 1), 0))),
                     (part, pl.BlockSpec(shape, lambda i, t: (jnp.maximum(i - half, 0), 0)))],
                    table=jnp.stack([seq_me ^ o for o in order]).astype(jnp.int32), grid=(count,), name="grad",
                )
                parts, left = [keep, swap(away, "seq", 1 << bits[-1])], keep.shape[0]
            yield parts[-1]
            parts, left = halve_all(parts, left, "seq", bits[:-1])
            yield parts[-1]
            yield add(parts, left, 0, F32)

        held, out = [], None
        for r in rows:
            out = front(r, out)
            held.append([out[1], swap(out[1], "seq", 1 << routes[(r + 1) % 2][0])])
        normed = out[0]
        normed_both = both(normed)
        unit_lat, inv_lat, queries = [], [], []

        def widen(r, bit):
            pair = joined_pair(held[r])
            held[r] = [pair, swap(pair, "seq", 1 << bit)]

        for bit in range(1, seq_bits - 1):
            for r in rows:
                widen(r, routes[(r + 1) % 2][bit])
        out = None
        for r in rows:
            out = query(r, out)
            unit_lat.append(out[1]), inv_lat.append(out[2]), queries.append(out[3])
        wait(normed_both[1])
        latent_norm = out[0]
        near, far = [None] * n_rows, [None] * n_rows
        lse, part1, out = [], [], None

        def sent_over(pieces):
            if len(pieces) == 2:
                return [pieces[0], swap(pieces[1], "tp", 1)]
            return [pieces[0]] + [swap(pieces[r], "tp", r) for r in range(1, n_tp)]

        for r in rows:
            widen(r, 0)
            near[r], far[r] = held[r]
            out = attend(r, out)
            lse.append(out[1])
            part1.append(sent_over(out[2:]))
        context = out[0]
        sent = n_tp // 2 * block
        middle, normed2 = [], []
        mid, n2 = mid_step(0, part1[0])
        middle.append(mid)
        normed2.append(gather(n2))
        part1[1], _ = halve_all(part1[1], sent, "tp", tp_route[:-1])
        wait(*normed2[0])
        mid, n2 = mid_step(1, part1[1])
        middle.append(mid)
        normed2.append(gather(n2))

        part2, out = [], None
        for r in rows:
            out = ffn(r, out)
            part2.append(sent_over(out[4:]))
        n2_all, hidden, ffn_keep, ffn_send = out[:4]
        mid_low = [gather(mid_back(0, part2[0]))]
        wide = model_dim // n_seq

        def own_grad(acts, deltas, grid, shape, spec):
            return step(own_grad_kernel, [acts] + deltas, [(shape_of(shape), spec)], grid=grid, name="own_grad")[0]

        def over_seq(part):
            return lax.psum_scatter(part, "seq", scatter_dimension=0, tiled=True)

        which = lambda k: (hidden, pl.BlockSpec((1,) + hidden.shape[1:], lambda *_: (k, 0, 0)))
        down_part = own_grad(
            which(0), [(out_grad, pl.BlockSpec((n_rows, length, wide), lambda i, *_: (0, 0, i)))],
            (n_seq,), (n_seq * ff_dim, wide), pl.BlockSpec((ff_dim, wide), lambda i, *_: (i, 0)),
        )
        part2[1], _ = halve_all(part2[1], sent, "tp", tp_route[:-1])
        down_sum = over_seq(after(down_part))
        gate_up_part = own_grad(
            (n2_all, pl.BlockSpec((n_rows * length, wide), lambda i, *_: (0, i))), [which(1), which(2)],
            (n_seq,), (model_dim, 2 * ff_dim), pl.BlockSpec((wide, 2 * ff_dim), lambda i, *_: (i, 0)),
        )
        wait(*mid_low[0])
        mid_low.append(gather(mid_back(1, part2[1])))

        kv_parts = []
        ffn_parts = [ffn_keep, swap(after(ffn_send), "tp", 1)]
        gate_up_sum = over_seq(after(gate_up_part))
        out = attend_back(0, None)
        kv_parts.append(([out[2], swap(out[3], "seq", 1)], half_keys))
        pause()
        kv_parts[0] = halve(*kv_parts[0], "seq", routes[1][-2])
        wait(*mid_low[1])
        out = attend_back(1, out)
        low_all, query_low = out[:2]
        kv_parts.append(([out[2], swap(out[3], "seq", 1)], half_keys))
        lat_parts = [out[4], swap(out[5], "tp", 1)]
        pause()
        kv_parts[0] = halve_all(*kv_parts[0], "seq", routes[1][:-2])
        pause()
        kv_parts[1] = halve(*kv_parts[1], "seq", routes[0][-2])
        out_part = own_grad(
            whole(context), [(low_all, pl.BlockSpec((n_rows * length, wide), lambda i, *_: (0, i)))],
            (n_seq,), (n_seq * q_width, wide), pl.BlockSpec((q_width, wide), lambda i, *_: (i, 0)),
        )
        for count in [n_tp >> i for i in range(1, tp_bits)]:
            lat_parts = halve_rows(lat_parts, count)
        pause()
        kv_parts[1] = halve_all(*kv_parts[1], "seq", routes[0][:-2])
        pause()
        for count in [n_tp >> i for i in range(1, tp_bits)]:
            ffn_parts = halve_rows(ffn_parts, count)
        query_part = own_grad(
            whole(latent_norm), [whole(query_low)], (1,), (lat_dim, q_width), full_spec((lat_dim, q_width)),
        )
        lat_low = step(
            functools.partial(latent_back_kernel, n_rows),
            [whole(p) for p in lat_parts] + [whole(u) for u in unit_lat] + [whole(i) for i in inv_lat]
            + [gain_row(latent_gain)],
            [new((n_rows * block, lat_dim))], name="latent_back",
        )[0]
        lat_blocks = gather_start(lat_low)
        kv_sum = step(
            functools.partial(kv_split_kernel, n_rows, singles),
            [first(p, length) for parts, _ in kv_parts for p in parts],
            [new((n_rows * block, 2 * HD))] * n_tp,
            scratch=[pltpu.VMEM((length, 2 * HD), F32)], name="kv_split",
        )
        kv_sum = sent_over(kv_sum)
        pause()
        out_sum, query_sum = over_seq(after(out_part)), over_seq(after(query_part))
        wait(down_sum)
        lat_blocks = gather_end(lat_blocks)
        pause()
        own_rows = pl.BlockSpec((n_rows, block, HD // 2), lambda i, info, *_: (0, info[0], 0))
        kv_low = step(
            functools.partial(key_back_kernel, n_rows),
            [whole(p) for p in kv_sum] + [(cosine, own_rows), (sine, own_rows)],
            [new((n_rows * block, 2 * HD))], name="key_back",
        )[0]
        kv_blocks = gather(kv_low)
        pause()

        def join(blocks, rels):
            width = blocks[0].shape[1]
            cols = width // n_tp
            count = n_rows * length
            out = step(
                functools.partial(join_kernel, n_rows, rels, len(blocks)), [whole(b) for b in blocks],
                [new((count, width))] + ([] if cols % 128 else [new((count, cols))]), name="join",
            )
            if cols % 128:
                return out[0], lax.dynamic_slice_in_dim(out[0], tp_me * cols, cols, 1)
            return out

        lat_all, lat_part = join(lat_blocks, tp_rels)
        lat_part_both = both(lat_part)
        pause()
        grad_lat = weight_grad(normed_both, lat_part_both, False, 0)
        lat_2 = next(grad_lat)
        kv_all, kv_part = join(kv_blocks, range(n_tp))
        kv_part_both = both(kv_part)
        ffn_own = step(
            functools.partial(ffn_sum_kernel, n_rows), [whole(p) for p in ffn_parts] + [whole(m) for m in middle],
            [new((n_rows * block, model_dim))], name="ffn_sum",
        )[0]
        ffn_blocks = gather_start(ffn_own)

        def input_step(r, held):
            return step(
                input_kernel,
                [row_block(lat_all, r), row_block(kv_all, r), row_of(layer_in, r), whole(query_down), whole(key_value),
                 row_block(low_all, r), gain_row(attn_gain)],
                [(shape_of(layer_in.shape), pl.BlockSpec((1, length, model_dim), lambda *_: (r, 0, 0)))],
                name="input", carried=going(held, (0, 0)),
            )

        out = input_step(0, None)
        grad_kv = weight_grad(normed_both, kv_part_both, False, 1)
        kv_2 = next(grad_kv)
        lat_3 = next(grad_lat)
        pause()
        lat_sum = next(grad_lat)
        kv_3 = next(grad_kv)
        ffn_blocks = gather_end(ffn_blocks)
        input_grad = input_step(1, out)[0]
        shared_lat = gather(after(lat_sum).astype(BF))
        pause()
        kv_grad_sum = next(grad_kv)
        gate_up_grad = total([(gate_up_sum, slice(None))], F32)
        gate_grad, up_grad = gate_up_grad[:, :ff_dim], gate_up_grad[:, ff_dim:]
        query_up_grad = total([(query_sum, slice(None))], F32)

        own_dim, own_lat = model_dim // n_seq, lat_dim // n_seq

        def own_part(array, count):
            return lax.dynamic_slice_in_dim(array, seq_me * count, count, 0)

        def row_sums(weight, grad):
            return jnp.sum(own_part(weight, grad.shape[0]).astype(F32) * grad, axis=1)

        def own_columns(weight):
            cols = weight.shape[1] // n_tp
            return lax.dynamic_slice_in_dim(weight, tp_me * cols, cols, 1)

        tp_sums = jnp.concatenate(
            [
                row_sums(gate_proj, gate_grad) + row_sums(up_proj, up_grad),
                row_sums(own_columns(query_down), lat_sum) + row_sums(own_columns(key_value), kv_grad_sum),
                row_sums(query_up, query_up_grad),
            ]
        )
        kv_rows = jnp.concatenate([kv_grad_sum, tp_sums.reshape(-1, kv_grad_sum.shape[1])], axis=0).astype(BF)
        wait(*shared_lat)
        shared_kv = gather(after(kv_rows))
        pause()
        layer_out = step(
            functools.partial(spread_kernel, tp_rels), [whole(p) for p in ffn_blocks], [new(layer_in.shape)],
            name="spread",
        )[0]
        out_weight_grad = total([(out_sum, slice(None))], F32)
        down_grad = total([(down_sum, slice(None))], F32)

        def shared_grad(pieces):
            cols = pieces[0].shape[1]
            if cols % 128:
                blocks = jnp.take(jnp.stack(pieces)[:, :own_dim], jnp.stack([tp_me ^ r for r in range(n_tp)]), axis=0)
                return blocks.astype(F32).transpose(1, 0, 2).reshape(own_dim, n_tp * cols)
            return step(
                functools.partial(shared_kernel, n_tp), [first(p, own_dim) for p in pieces],
                [new((own_dim, n_tp * cols), F32)], name="shared",
            )[0]

        kv_grad = shared_grad(shared_kv)
        down_q = shared_grad(shared_lat)
        tp_sums = sum(p[own_dim:].astype(F32) for p in shared_kv).reshape(-1)
        ffn_gain_grad = tp_sums[:own_dim] / own_part(ffn_gain, own_dim)
        attn_gain_grad = tp_sums[own_dim : 2 * own_dim] / own_part(attn_gain, own_dim)
        latent_gain_grad = tp_sums[2 * own_dim :] / own_part(latent_gain, own_lat)
        return (
            layer_out, input_grad, attn_gain_grad, down_q, latent_gain_grad, query_up_grad,
            kv_grad, out_weight_grad.reshape(q_width, own_dim), ffn_gain_grad, gate_grad, up_grad,
            down_grad.reshape(ff_dim, own_dim),
        )

    return shards


def solution(mesh):
    return jax.shard_map(
        build(mesh.shape["seq"], mesh.shape["tp"]),
        mesh=mesh,
        in_specs=(
            P(None, "seq", None), P(), P(), P(), P(None, "tp"), P(), P("tp", None), P(),
            P(None, "tp"), P(None, "tp"), P("tp", None), P(None, "seq", None), P(),
        ),
        out_specs=(
            P(None, "seq", None), P(None, "seq", None), P("seq"), P("seq", None), P("seq"),
            P("seq", "tp"), P("seq", None), P("tp", "seq"), P("seq"), P("seq", "tp"),
            P("seq", "tp"), P("tp", "seq"),
        ),
        check_vma=False,
    )
```

```python
import functools

import jax
import jax.numpy as jnp
from jax import lax
from jax.experimental import pallas as pl
from jax.experimental.pallas import tpu as pltpu
from jax.sharding import PartitionSpec as P

HD = 256
EPS = 1e-05
ROPE_BASE = 10000.0
NEG_FILL = -1e30
BF = jnp.bfloat16
F32 = jnp.float32
VMEM_BYTES = 58 * 1024 * 1024
COST = 1e12
HEADS_PER_STEP = 2


def dot(left, right):
    return jnp.dot(left, right, preferred_element_type=F32)


def dot_rows(left, right):
    return lax.dot_general(left, right, (((0,), (0,)), ((), ())), preferred_element_type=F32)


def dot_cols(left, right):
    return lax.dot_general(left, right, (((1,), (1,)), ((), ())), preferred_element_type=F32)


def inverse_rms(values):
    return lax.rsqrt(jnp.mean(values * values, axis=-1, keepdims=True) + EPS)


def back_norm(grad_out, unit_rows, inv_rms, gain):
    scaled = grad_out * gain
    return inv_rms * (scaled - unit_rows * jnp.mean(scaled * unit_rows, axis=-1, keepdims=True))


def turn(values, cosine, sine):
    half = HD // 2
    front, back = values[:, :half], values[:, half:]
    return front * cosine - back * sine, back * cosine + front * sine


def full_spec(shape):
    return pl.BlockSpec(tuple(shape), lambda *_: (0,) * len(shape))


def shape_of(shape, kind=BF):
    return jax.ShapeDtypeStruct(tuple(shape), kind)


def write_pieces(me, source, outs, layout):
    block = outs[0].shape[0] // len(layout[0])
    for out, rels in zip(outs, layout):
        for j, rel in enumerate(rels):
            out[j * block : (j + 1) * block, :] = source[block_rows(me ^ rel, block), :].astype(BF)


MICROS = {
    "front": 4, "query": 7, "attend": 13, "middle": 3, "ffn": 19, "mid_back": 3, "grad": 9, "ffn_grad": 22, "head_grad": 14, "pause": 3, "attend_back": 20,
    "latent_back": 3, "ffn_sum": 3, "spread": 3, "kv_split": 3, "key_back": 3, "join": 3, "input": 8, "shared": 3,
}


def run(kernel, scalars, inputs, outputs, grid=(1,), scratch=(), name=None, carried=()):
    n_in, n_scalars = len(inputs), len(scalars)
    moved = sum(a.size * a.dtype.itemsize for a, _ in inputs)

    def body(*refs):
        kernel(*refs[: n_scalars + n_in], *refs[n_scalars + n_in + len(carried) :])

    return pl.pallas_call(
        body,
        out_shape=[s for s, _ in outputs],
        grid_spec=pltpu.PrefetchScalarGridSpec(
            num_scalar_prefetch=n_scalars,
            grid=grid,
            in_specs=[s for _, s in inputs] + [pl.BlockSpec(memory_space=pl.ANY)] * len(carried),
            out_specs=[s for _, s in outputs],
            scratch_shapes=list(scratch),
        ),
        input_output_aliases={n_scalars + n_in + k: index for k, (index, _) in enumerate(carried)},
        compiler_params=pltpu.CompilerParams(
            dimension_semantics=("arbitrary",) * len(grid), vmem_limit_bytes=VMEM_BYTES
        ),
        cost_estimate=pl.CostEstimate(flops=int(MICROS[name] * COST), bytes_accessed=moved, transcendentals=0),
        name=name,
    )(*scalars, *[a for a, _ in inputs], *[a for _, a in carried])


def total_of(refs):
    total = refs[0][...].astype(F32)
    for ref in refs[1:]:
        total = total + ref[...].astype(F32)
    return total


def row_total(refs, r, n_rows, block):
    total = 0.0
    for ref in refs:
        at = r * (ref.shape[0] // n_rows)
        total = total + ref[at : at + block, :].astype(F32)
    return total


def block_rows(index, size):
    return pl.ds(pl.multiple_of(index * size, size), size)


def front_kernel(info, x_ref, gain_ref, w_ref, cos_ref, sin_ref, n_ref, kv_ref):
    x = x_ref[0].astype(F32)
    normed = (x * inverse_rms(x) * gain_ref[...]).astype(BF)
    n_ref[...] = normed
    kv = dot(normed, w_ref[...])
    front, back = turn(kv[:, :HD], cos_ref[0], sin_ref[0])
    kv_ref[:, : HD // 2] = front.astype(BF)
    kv_ref[:, HD // 2 : HD] = back.astype(BF)
    kv_ref[:, HD:] = kv[:, HD:].astype(BF)


def query_kernel(info, n_ref, wd_ref, gain_ref, wu_ref, cos_ref, sin_ref, ln_ref, ul_ref, il_ref, q_ref, held):
    latent = dot(n_ref[...], wd_ref[...])
    inv = inverse_rms(latent)
    unit = latent * inv
    normed = (unit * gain_ref[...]).astype(BF)
    ln_ref[...] = normed
    block = ul_ref.shape[0]
    held[...] = latent
    mine = held[block_rows(info[0], block), :]
    inv_mine = inverse_rms(mine)
    ul_ref[...] = mine * inv_mine
    il_ref[...] = jnp.broadcast_to(inv_mine, il_ref.shape)
    raw = dot(normed, wu_ref[...])
    cosine, sine = cos_ref[0], sin_ref[0]
    for h in range(raw.shape[1] // HD):
        front, back = turn(raw[:, h * HD : (h + 1) * HD], cosine, sine)
        q_ref[:, h * HD : h * HD + HD // 2] = front.astype(BF)
        q_ref[:, h * HD + HD // 2 : (h + 1) * HD] = back.astype(BF)


def starts_of(docs, row, places):
    end, start = 0, jnp.zeros_like(places)
    for d in range(docs.shape[1]):
        size = docs[row, d]
        end = end + size
        start = start + jnp.where(places >= end, size, 0)
    return start


def attend_kernel(row, order, layout, info, docs, q_ref, ka_ref, kb_ref, w_ref, ctx_ref, lse_ref, *rest):
    pieces, (acc, bias) = rest[: len(layout)], rest[len(layout) :]
    h = pl.program_id(0)
    length = q_ref.shape[0]
    half = len(order) // 2 * length
    me_tp, me_seq = info[0], info[1]

    @pl.when(h == 0)
    def _():
        places = me_seq * length + lax.broadcasted_iota(jnp.int32, (length, 1), 0)
        start = starts_of(docs, row, places)
        column = lax.broadcasted_iota(jnp.int32, (1, length), 1)
        for b, rel in enumerate(order):
            key = (me_seq ^ rel) * length + column
            allowed = (key >= start) & (key <= places)
            bias[:, b * length : (b + 1) * length] = jnp.where(allowed, 0.0, NEG_FILL)

    scale = jnp.asarray(HD ** (-0.5), BF)
    for i in range(q_ref.shape[1] // HD):
        cols = slice(i * HD, (i + 1) * HD)
        q = q_ref[:, cols] * scale
        sa = dot_cols(q, ka_ref[:, :HD]) + bias[:, :half]
        sb = dot_cols(q, kb_ref[:, :HD]) + bias[:, half:]
        peak = jnp.maximum(jnp.max(sa, axis=-1, keepdims=True), jnp.max(sb, axis=-1, keepdims=True))
        pa = jnp.exp(sa - peak)
        pb = jnp.exp(sb - peak)
        total = jnp.sum(pa, axis=-1, keepdims=True) + jnp.sum(pb, axis=-1, keepdims=True)
        out = dot(pa.astype(BF), ka_ref[:, HD:]) + dot(pb.astype(BF), kb_ref[:, HD:])
        out = (out / total).astype(BF)
        ctx_ref[:, cols] = out
        lse = jnp.broadcast_to(peak + jnp.log(total), (length, 128))
        lse_ref[i] = jnp.transpose(lse)[:1, :]
    part = dot(ctx_ref[...], w_ref[...])

    @pl.when(h == 0)
    def _():
        acc[...] = part

    @pl.when(h > 0)
    def _():
        acc[...] += part

    @pl.when(h == pl.num_programs(0) - 1)
    def _():
        write_pieces(me_tp, acc, pieces, layout)


def middle_kernel(info, *refs):
    parts, (x_ref, gain_ref, mid_ref, n2_ref) = refs[:-4], refs[-4:]
    mid = x_ref[0].astype(F32) + total_of(parts)
    mid_ref[...] = mid
    n2_ref[...] = (mid * inverse_rms(mid) * gain_ref[...]).astype(BF)


def place_pieces(me, pieces, out_ref, rels):
    per = len(rels) // len(pieces)
    block = pieces[0].shape[0] // per
    for i, rel in enumerate(rels):
        at = i % per * block
        out_ref[block_rows(me ^ rel, block), :] = pieces[i // per][at : at + block, :]


def ffn_kernel(n_parts, rels, layout, ff_layout, info, *refs):
    parts = refs[:n_parts]
    dy_ref, wg_hbm, wu_hbm, wd_hbm = refs[n_parts : n_parts + 4]
    outs = refs[n_parts + 4 :]
    n2_ref, hidden_ref = outs[:2]
    ff_refs, pieces = outs[2:4], outs[4 : 4 + len(layout)]
    wg, wu, wd, acc, sems = outs[4 + len(layout) :]
    me = info[0]
    width = hidden_ref.shape[2]
    step = 256
    chunks = [(i, min(step, width - i)) for i in range(0, width, step)]

    def copies(c):
        at, size = chunks[c]
        return (
            pltpu.make_async_copy(wg_hbm.at[:, pl.ds(at, size)], wg.at[:, pl.ds(at, size)], sems.at[0, c]),
            pltpu.make_async_copy(wu_hbm.at[:, pl.ds(at, size)], wu.at[:, pl.ds(at, size)], sems.at[1, c]),
            pltpu.make_async_copy(wd_hbm.at[pl.ds(at, size), :], wd.at[pl.ds(at, size), :], sems.at[2, c]),
        )

    for c in range(len(chunks)):
        for copy in copies(c):
            copy.start()
    place_pieces(me, parts, n2_ref, rels)
    n2 = n2_ref[...]
    dy = dy_ref[0]
    for c, (at, size) in enumerate(chunks):
        here = slice(at, at + size)
        for copy in copies(c):
            copy.wait()
        gate = dot(n2, wg[:, here])
        up = dot(n2, wu[:, here])
        dhid = dot_cols(dy, wd[here, :])
        sig = 1.0 / (1.0 + jnp.exp(-gate))
        swish = gate * sig
        hidden_ref[0, :, here] = (swish * up).astype(BF)
        hidden_ref[1, :, here] = (dhid * up * sig * (1.0 + gate * (1.0 - sig))).astype(BF)
        hidden_ref[2, :, here] = (dhid * swish).astype(BF)
    hid, dgate, dup = hidden_ref[0], hidden_ref[1], hidden_ref[2]
    cut = min(512, acc.shape[1])
    for at in range(0, acc.shape[1], cut):
        here = slice(at, at + cut)
        acc[:, here] = dot_cols(dgate, wg[here, :]) + dot_cols(dup, wu[here, :])
    write_pieces(me, acc, pieces, layout)
    for at in range(0, acc.shape[1], cut):
        here = slice(at, at + cut)
        acc[:, here] = dot(hid, wd[:, here])
    write_pieces(me, acc, ff_refs, ff_layout)


def mid_back_kernel(info, *refs):
    parts, (mid_ref, dy_ref, gain_ref, low_ref) = refs[:-4], refs[-4:]
    d2 = total_of(parts)
    mid = mid_ref[...]
    inv = inverse_rms(mid)
    unit = mid * inv
    low_ref[...] = (dy_ref[0].astype(F32) + back_norm(d2, unit, inv, gain_ref[...])).astype(BF)


def attend_back_kernel(row, order, n_parts, rels, layout, info, docs, *refs):
    lows, refs = refs[:n_parts], refs[n_parts:]
    q_ref, ka_ref, kb_ref, lse_ref, wo_ref, wq_ref, cos_ref, sin_ref = refs[:8]
    low_ref, qlow_ref, keep_ref, send_ref = refs[8:12]
    pieces = refs[12:14]
    bias, dkv, lat = refs[14:]
    h = pl.program_id(0)
    length = q_ref.shape[0]
    half = len(order) // 2 * length
    me_tp, me_seq = info[0], info[1]
    scale = HD ** (-0.5)

    @pl.when(h == 0)
    def _():
        place_pieces(me_tp, lows, low_ref, rels)
        places = me_seq * length + lax.broadcasted_iota(jnp.int32, (1, length), 1)
        start = starts_of(docs, row, places)
        column = lax.broadcasted_iota(jnp.int32, (length, 1), 0)
        for b, rel in enumerate(order):
            key = (me_seq ^ rel) * length + column
            allowed = (key >= start) & (key <= places)
            bias[b * length : (b + 1) * length, :] = jnp.where(allowed, 0.0, NEG_FILL)

    dctx_all = dot_cols(low_ref[...], wo_ref[...]).astype(BF)
    for n in range(q_ref.shape[1] // HD):
        cols = slice(n * HD, (n + 1) * HD)
        q = q_ref[:, cols] * jnp.asarray(scale, BF)
        dctx = dctx_all[:, cols]
        lse = lse_ref[n]
        probs, dprobs = [], []
        delta = 0.0
        for i, kv_ref in enumerate((ka_ref, kb_ref)):
            scores = dot_cols(kv_ref[:, :HD], q) + bias[i * half : (i + 1) * half, :]
            prob = jnp.exp(scores - lse)
            dprob = dot_cols(kv_ref[:, HD:], dctx)
            delta = delta + jnp.sum(prob * dprob, axis=0, keepdims=True)
            probs.append(prob), dprobs.append(dprob)
        dq = 0.0
        for i, kv_ref in enumerate((ka_ref, kb_ref)):
            rows = slice(i * half, (i + 1) * half)
            dscore = (probs[i] * (dprobs[i] - delta)).astype(BF)
            dq = dq + dot_rows(dscore, kv_ref[:, :HD])
            dk = dot(dscore, q)
            dv = dot(probs[i].astype(BF), dctx)
            if n == 0:

                @pl.when(h == 0)
                def _():
                    dkv[rows, :HD] = dk
                    dkv[rows, HD:] = dv

                @pl.when(h > 0)
                def _():
                    dkv[rows, :HD] += dk
                    dkv[rows, HD:] += dv

            else:
                dkv[rows, :HD] += dk
                dkv[rows, HD:] += dv

        front, back = turn(dq * scale, cos_ref[0], -sin_ref[0])
        qlow_ref[:, n * HD : n * HD + HD // 2] = front.astype(BF)
        qlow_ref[:, n * HD + HD // 2 : (n + 1) * HD] = back.astype(BF)
    part = dot_cols(qlow_ref[...], wq_ref[...])

    @pl.when(h == 0)
    def _():
        lat[...] = part

    @pl.when(h > 0)
    def _():
        lat[...] += part

    @pl.when(h == pl.num_programs(0) - 1)
    def _():
        keep_ref[...] = dkv[:half, :].astype(BF)
        send_ref[...] = dkv[half:, :].astype(BF)
        write_pieces(me_tp, lat, pieces, layout)


def kv_split_kernel(n_rows, layout, info, *refs):
    pieces, held = refs[-1 - len(layout) : -1], refs[-1]
    count = (len(refs) - 1 - len(layout)) // n_rows
    rows = pieces[0].shape[0] // n_rows
    for r in range(n_rows):
        held[...] = total_of(refs[r * count : (r + 1) * count])
        outs = [piece.at[r * rows : (r + 1) * rows, :] for piece in pieces]
        write_pieces(info[0], held, outs, layout)


def latent_back_kernel(n_rows, info, *refs):
    units, invs = refs[-2 - 2 * n_rows : -2 - n_rows], refs[-2 - n_rows : -2]
    parts, (gain_ref, low_ref) = refs[: -2 - 2 * n_rows], refs[-2:]
    block = low_ref.shape[0] // n_rows
    for r in range(n_rows):
        rows = slice(r * block, (r + 1) * block)
        unit, grad = units[r][...], row_total(parts, r, n_rows, block)
        low_ref[rows, :] = back_norm(grad, unit, invs[r][:, :1], gain_ref[...]).astype(BF)


def key_back_kernel(n_rows, info, *refs):
    parts, (cos_ref, sin_ref, out_ref) = refs[:-3], refs[-3:]
    block = out_ref.shape[0] // n_rows
    for r in range(n_rows):
        rows = slice(r * block, (r + 1) * block)
        total = row_total(parts, r, n_rows, block)
        front, back = turn(total[:, :HD], cos_ref[r], -sin_ref[r])
        out_ref[rows, : HD // 2] = front.astype(BF)
        out_ref[rows, HD // 2 : HD] = back.astype(BF)
        out_ref[rows, HD:] = total[:, HD:].astype(BF)


def ffn_sum_kernel(n_rows, info, *refs):
    parts, mids, out_ref = refs[: -1 - n_rows], refs[-1 - n_rows : -1], refs[-1]
    block = out_ref.shape[0] // n_rows
    for r in range(n_rows):
        out_ref[r * block : (r + 1) * block, :] = (row_total(parts, r, n_rows, block) + mids[r][...]).astype(BF)


def spread_kernel(rels, info, *refs):
    pieces, out_ref = refs[:-1], refs[-1]
    n_rows, per = out_ref.shape[0], len(rels) // len(pieces)
    block = out_ref.shape[1] // len(rels)
    for i, rel in enumerate(rels):
        for row in range(n_rows):
            at = (i % per * n_rows + row) * block
            out_ref[row, block_rows(info[0] ^ rel, block), :] = pieces[i // per][at : at + block, :]


def join_kernel(n_rows, rels, count, info, *refs):
    pieces, all_ref = refs[:count], refs[count]
    me, n_tp = info[0], len(rels)
    per = n_tp // count
    block = pieces[0].shape[0] // (n_rows * per)
    for i, rel in enumerate(rels):
        for r in range(n_rows):
            at = (i % per * n_rows + r) * block
            all_ref[block_rows(r * n_tp + (me ^ rel), block), :] = pieces[i // per][at : at + block, :]
    if len(refs) > count + 1:
        part_ref = refs[count + 1]
        part_ref[...] = all_ref[:, block_rows(me, part_ref.shape[1])]


def input_kernel(info, lat_ref, kv_ref, x_ref, wd_ref, wkv_ref, low_ref, gain_ref, out_ref):
    dn = dot_cols(lat_ref[...], wd_ref[...]) + dot_cols(kv_ref[...], wkv_ref[...])
    x = x_ref[0].astype(F32)
    inv = inverse_rms(x)
    unit = x * inv
    out_ref[0] = (low_ref[...].astype(F32) + back_norm(dn, unit, inv, gain_ref[...])).astype(BF)


def grad_kernel(table, *refs):
    count = (len(refs) - 2) // 2
    keep_ref, send_ref = refs[2 * count :]

    def load(ref):
        value = ref[...]
        return value.reshape(-1, value.shape[-1])

    total = dot_rows(load(refs[0]), load(refs[count]))
    for i in range(1, count):
        total = total + dot_rows(load(refs[i]), load(refs[count + i]))
    total = total.astype(BF)
    i, half = pl.program_id(0), pl.num_programs(0) // 2

    @pl.when(i < half)
    def _():
        keep_ref[...] = total

    @pl.when(i >= half)
    def _():
        send_ref[...] = total


def ffn_grad_kernel(info, hidden_ref, n2_ref, dy_ref, out_ref):
    dy = dy_ref[...]
    dy = dy.reshape(-1, dy.shape[-1])
    width = hidden_ref.shape[2]
    out_ref[:, :width] = dot_rows(dy, hidden_ref[0]).astype(BF)
    out_ref[:, width : 2 * width] = dot_rows(n2_ref[...], hidden_ref[1]).astype(BF)
    out_ref[:, 2 * width :] = dot_rows(n2_ref[...], hidden_ref[2]).astype(BF)


def head_grad_kernel(info, context_ref, low_ref, latent_ref, query_ref, out_ref):
    rows, width = context_ref.shape[1], low_ref.shape[1]
    out_ref[:rows, :] = dot_rows(context_ref[...], low_ref[...]).astype(BF)
    count = latent_ref.shape[1]
    part = dot_rows(latent_ref[...], query_ref[...]).astype(BF)
    for i in range(part.shape[1] // width):
        out_ref[rows + i * count : rows + (i + 1) * count, :] = part[:, i * width : (i + 1) * width]


def pause_kernel(info, out_ref):
    for i in range(out_ref.shape[0]):
        out_ref[i] = info[i]


def shared_kernel(n_tp, info, *refs):
    for pieces, out_ref in ((refs[:n_tp], refs[2 * n_tp]), (refs[n_tp : 2 * n_tp], refs[2 * n_tp + 1])):
        for r in range(n_tp):
            width = pieces[r].shape[1]
            out_ref[:, block_rows(info[0] ^ r, width)] = pieces[r][...].astype(F32)


def build(n_seq, n_tp):
    seq_bits = n_seq.bit_length() - 1
    tp_bits = n_tp.bit_length() - 1

    def swap(value, axis, mask):
        count = n_seq if axis == "seq" else n_tp
        return lax.ppermute(value, axis, [(i, i ^ mask) for i in range(count)])

    def spread(bits):
        order = [0]
        for bit in bits:
            order = order + [o | (1 << bit) for o in order]
        return order

    upward = list(range(1, seq_bits))
    routes = (upward + [0], upward[::-1] + [0])
    tp_route = list(reversed(range(tp_bits)))
    tp_rels = spread(tp_route)
    halves = [tp_rels[: n_tp // 2], tp_rels[n_tp // 2 :]]
    singles = [[r] for r in range(n_tp)]
    layouts = [singles, halves]

    def gather(block):
        return [block] + [swap(block, "tp", r) for r in range(1, n_tp)]

    def shards(
        layer_in, attn_gain, query_down, latent_gain, query_up, key_value, attn_out,
        ffn_gain, gate_proj, up_proj, down_proj, out_grad, doc_lengths,
    ):
        n_rows, length, model_dim = layer_in.shape
        lat_dim, q_width = query_up.shape
        ff_dim = gate_proj.shape[1]
        heads = q_width // HD
        block = length // n_tp
        half_keys = n_seq // 2 * length
        rows = range(n_rows)
        seq_me, tp_me = lax.axis_index("seq"), lax.axis_index("tp")
        state = [jnp.stack([tp_me, seq_me, jnp.zeros_like(tp_me)]).astype(jnp.int32)]
        last, due = [], []

        def wait(*arrays):
            due.extend(arrays)

        def pause():
            state[0] = step(
                pause_kernel, [], [(shape_of((3,), jnp.int32), pl.BlockSpec(memory_space=pltpu.SMEM))], name="pause",
            )[0]

        def after(value):
            ready = last[-1:] + due
            due.clear()
            return lax.optimization_barrier((value, *ready))[0] if ready else value

        def step(kernel, inputs, outputs, table=None, docs=False, **kw):
            scalars = (after(state[0] if table is None else table),) + ((doc_lengths,) if docs else ())
            out = run(kernel, scalars, inputs, outputs, **kw)
            last.append(min(out, key=lambda o: o.size))
            return out

        def total(values, kind):
            out = after(values[-1][0])[values[-1][1]].astype(F32)
            for array, index in values[:-1]:
                out = out + array[index].astype(F32)
            out = out.astype(kind)
            last.append(out)
            return out

        def add(parts, rows, at, kind):
            return total([(p, slice(at * rows, (at + 1) * rows)) for p in parts], kind)

        def halve(parts, rows, axis, bit):
            half = rows // 2
            return parts + [swap(add(parts, half, 1, BF), axis, 1 << bit)], half

        def halve_all(parts, rows, axis, bits):
            for bit in reversed(bits):
                parts, rows = halve(parts, rows, axis, bit)
            return parts, rows

        places = seq_me * length + jnp.arange(length, dtype=jnp.int32)
        ends = jnp.cumsum(doc_lengths, axis=1)
        passed = places[None, :, None] >= ends[:, None, :]
        inner = places[None, :] - jnp.sum(jnp.where(passed, doc_lengths[:, None, :], 0), axis=-1)
        frequency = ROPE_BASE ** (-jnp.arange(HD // 2, dtype=F32) / (HD // 2))
        angles = inner.astype(F32)[:, :, None] * frequency
        cosine, sine = jnp.cos(angles), jnp.sin(angles)
        gain_row = lambda gain: (gain.reshape(1, -1), full_spec((1, gain.shape[0])))

        def whole(array):
            return array, full_spec(array.shape)

        def first(array, count):
            return array, full_spec((count, array.shape[1]))

        def row_of(array, r):
            return array, pl.BlockSpec((1,) + array.shape[1:], lambda *_: (r, 0, 0))

        def own_of(array, r):
            shape = (1, block, array.shape[2])
            return array, pl.BlockSpec(shape, lambda i, info, *_: (r, info[0], 0))

        def new(shape, kind=BF):
            return shape_of(shape, kind), full_spec(shape)

        per_step = min(HEADS_PER_STEP, heads)
        group = per_step * HD

        def head_cols(array):
            return array, pl.BlockSpec((array.shape[0], group), lambda h, *_: (0, h))

        def head_rows(array):
            return array, pl.BlockSpec((group, array.shape[1]), lambda h, *_: (h, 0))

        def row_pieces(r, width):
            rows_out = n_tp // 2 * block
            spec = pl.BlockSpec((rows_out, width), lambda *_: (r, 0))
            return [(shape_of((n_rows * rows_out, width)), spec)] * 2

        def pieces_of(layout, width):
            return [new((len(rels) * block, width)) for rels in layout]

        hbm = pl.BlockSpec(memory_space=pl.ANY)
        chunks = -(-ff_dim // 256)

        def rows_of(width, r, spec=None):
            return shape_of((n_rows * length, width)), spec or pl.BlockSpec((length, width), lambda *_: (r, 0))

        def row_block(array, r):
            return array, pl.BlockSpec((length, array.shape[1]), lambda *_: (r, 0))

        def going(held, *pairs):
            return [(index, held[key]) for index, key in pairs] if held else []

        def front(r, held):
            return step(
                front_kernel,
                [row_of(layer_in, r), gain_row(attn_gain), whole(key_value), row_of(cosine, r), row_of(sine, r)],
                [rows_of(model_dim, r), new((length, 2 * HD))], name="front", carried=going(held, (0, 0)),
            )

        def query(r, held):
            return step(
                query_kernel,
                [row_block(normed, r), whole(query_down), gain_row(latent_gain), whole(query_up),
                 row_of(cosine, r), row_of(sine, r)],
                [rows_of(lat_dim, r), new((block, lat_dim), F32), new((block, 128), F32), new((length, q_width))],
                scratch=[pltpu.VMEM((length, lat_dim), F32)], name="query", carried=going(held, (0, 0)),
            )

        def attend(r, held):
            return step(
                functools.partial(attend_kernel, r, spread(routes[(r + 1) % 2]), layouts[r]),
                [head_cols(queries[r]), whole(near[r]), whole(far[r]), head_rows(attn_out)],
                [
                    rows_of(q_width, r, pl.BlockSpec((length, group), lambda h, *_: (r, h))),
                    (shape_of((heads, 1, length), F32), pl.BlockSpec((per_step, 1, length), lambda h, *_: (h, 0, 0))),
                ] + pieces_of(layouts[r], model_dim),
                docs=True, grid=(heads // per_step,),
                scratch=[pltpu.VMEM((length, model_dim), F32), pltpu.VMEM((length, 2 * half_keys), F32)],
                name="attend", carried=going(held, (0, 0)),
            )

        def mid_step(r, parts):
            return step(
                middle_kernel, [first(p, block) for p in parts] + [own_of(layer_in, r), gain_row(ffn_gain)],
                [new((block, model_dim), F32), new((block, model_dim))], name="middle",
            )

        def ffn(r, held):
            return step(
                functools.partial(ffn_kernel, len(normed2[r]), range(n_tp), layouts[r], halves),
                [whole(p) for p in normed2[r]] + [row_of(out_grad, r),
                 (gate_proj, hbm), (up_proj, hbm), (down_proj, hbm)],
                [rows_of(model_dim, r),
                 (shape_of((3, n_rows * length, ff_dim)), pl.BlockSpec((3, length, ff_dim), lambda *_: (0, r, 0)))]
                + row_pieces(r, model_dim) + pieces_of(layouts[r], model_dim),
                scratch=[
                    pltpu.VMEM((model_dim, ff_dim), BF), pltpu.VMEM((model_dim, ff_dim), BF),
                    pltpu.VMEM((ff_dim, model_dim), BF), pltpu.VMEM((length, model_dim), F32),
                    pltpu.SemaphoreType.DMA((3, chunks)),
                ],
                name="ffn", carried=going(held, *[(i, i) for i in range(4)]),
            )

        def mid_back(r, parts):
            return step(
                mid_back_kernel,
                [first(p, block) for p in parts] + [whole(middle[r]), own_of(out_grad, r), gain_row(ffn_gain)],
                [new((block, model_dim))], name="mid_back",
            )[0]

        def attend_back(r, held):
            return step(
                functools.partial(attend_back_kernel, r, spread(routes[(r + 1) % 2]), len(mid_low[r]), range(n_tp), halves),
                [whole(p) for p in mid_low[r]]
                + [head_cols(queries[r]), whole(near[r]), whole(far[r]),
                   (lse[r], pl.BlockSpec((per_step, 1, length), lambda h, *_: (h, 0, 0))),
                   head_rows(attn_out), head_cols(query_up), row_of(cosine, r), row_of(sine, r)],
                [rows_of(model_dim, r), rows_of(q_width, r, pl.BlockSpec((length, group), lambda h, *_: (r, h))),
                 new((half_keys, 2 * HD)), new((half_keys, 2 * HD))] + row_pieces(r, lat_dim),
                docs=True, grid=(heads // per_step,),
                scratch=[pltpu.VMEM((2 * half_keys, length), F32), pltpu.VMEM((2 * half_keys, 2 * HD), F32),
                         pltpu.VMEM((length, lat_dim), F32)],
                name="attend_back", carried=going(held, (0, 0), (1, 1), (4, 4), (5, 5)),
            )

        def halve_rows(parts, count):
            half = count // 2 * block
            width = parts[0].shape[1]
            values = [(p.reshape(n_rows, -1, width), (slice(None), slice(half, 2 * half))) for p in parts]
            away = total(values, BF).reshape(n_rows * half, width)
            return parts + [swap(away, "tp", 1 << tp_route[count.bit_length() - 2])]

        def joined_pair(held):
            pair = jnp.concatenate([after(held[0]), held[1]], axis=0)
            last.append(pair)
            return pair

        def gather_start(piece):
            return piece, swap(piece, "tp", 1 << tp_route[0])

        def gather_end(held):
            for bit in tp_route[1:]:
                held = joined_pair(held)
                held = held, swap(held, "tp", 1 << bit)
            return list(held)

        def both(array):
            return [array, swap(array, "seq", 1)]

        def weight_grad(acts, deltas, by_cols, route):
            acts, deltas = [[a if isinstance(a, tuple) else (a, None) for a in pair] for pair in (acts, deltas)]
            bits = routes[route][:-1]
            order = [o for o in spread(bits)]
            count = n_seq // 2
            size = (deltas if by_cols else acts)[0][0].shape[-1] // n_seq
            if size % 128:
                flat = [jnp.concatenate([a for a, _ in pair], axis=0) for pair in (acts, deltas)]
                full = dot_rows(*flat).astype(BF)
                blocks = jnp.take(full.reshape(n_seq, -1, full.shape[1]), jnp.stack([seq_me ^ o for o in order]), axis=0)
                parts, left = halve([blocks.reshape(-1, full.shape[1])], count * size, "seq", bits[-1])
            else:

                def operands(arrays, cut):
                    out = []
                    for array, which in arrays:
                        lead = array.shape[:-1]
                        if which is not None:
                            out.append((array, pl.BlockSpec((1,) + array.shape[1:], lambda i, t: (which, 0, 0))))
                        elif cut:
                            zeros = (0,) * len(lead)
                            out.append((array, pl.BlockSpec(lead + (size,), lambda i, t, z=zeros: z + (t[i],))))
                        else:
                            out.append(whole(array))
                    return out

                shape = (acts[0][0].shape[-1], size) if by_cols else (size, deltas[0][0].shape[-1])
                half = count // 2
                part = shape_of((half * shape[0], shape[1]))
                keep, away = step(
                    grad_kernel, operands(acts, not by_cols) + operands(deltas, by_cols),
                    [(part, pl.BlockSpec(shape, lambda i, t: (jnp.minimum(i, half - 1), 0))),
                     (part, pl.BlockSpec(shape, lambda i, t: (jnp.maximum(i - half, 0), 0)))],
                    table=jnp.stack([seq_me ^ o for o in order]).astype(jnp.int32), grid=(count,), name="grad",
                )
                parts, left = [keep, swap(away, "seq", 1 << bits[-1])], keep.shape[0]
            yield parts[-1]
            parts, left = halve_all(parts, left, "seq", bits[:-1])
            yield parts[-1]
            yield add(parts, left, 0, F32)

        held, out = [], None
        for r in rows:
            out = front(r, out)
            held.append([out[1], swap(out[1], "seq", 1 << routes[(r + 1) % 2][0])])
        normed = out[0]
        normed_both = both(normed)
        unit_lat, inv_lat, queries = [], [], []

        def widen(r, bit):
            pair = joined_pair(held[r])
            held[r] = [pair, swap(pair, "seq", 1 << bit)]

        for bit in range(1, seq_bits - 1):
            for r in rows:
                widen(r, routes[(r + 1) % 2][bit])
        out = None
        for r in rows:
            out = query(r, out)
            unit_lat.append(out[1]), inv_lat.append(out[2]), queries.append(out[3])
        wait(normed_both[1])
        latent_norm = out[0]
        near, far = [None] * n_rows, [None] * n_rows
        lse, part1, out = [], [], None

        def sent_over(pieces):
            if len(pieces) == 2:
                return [pieces[0], swap(pieces[1], "tp", 1)]
            return [pieces[0]] + [swap(pieces[r], "tp", r) for r in range(1, n_tp)]

        for r in rows:
            widen(r, 0)
            near[r], far[r] = held[r]
            out = attend(r, out)
            lse.append(out[1])
            part1.append(sent_over(out[2:]))
        context = out[0]
        sent = n_tp // 2 * block
        middle, normed2 = [], []
        mid, n2 = mid_step(0, part1[0])
        middle.append(mid)
        normed2.append(gather(n2))
        part1[1], _ = halve_all(part1[1], sent, "tp", tp_route[:-1])
        wait(*normed2[0])
        mid, n2 = mid_step(1, part1[1])
        middle.append(mid)
        normed2.append(gather(n2))

        part2, out = [], None
        for r in rows:
            out = ffn(r, out)
            part2.append(sent_over(out[4:]))
        n2_all, hidden, ffn_keep, ffn_send = out[:4]
        mid_low = [gather(mid_back(0, part2[0]))]
        wide = model_dim // n_seq

        def over_seq(part):
            return lax.psum_scatter(part, "seq", scatter_dimension=0, tiled=True)

        ffn_part = step(
            ffn_grad_kernel,
            [whole(hidden), (n2_all, pl.BlockSpec((n_rows * length, wide), lambda i, *_: (0, i))),
             (out_grad, pl.BlockSpec((n_rows, length, wide), lambda i, *_: (0, 0, i)))],
            [(shape_of((model_dim, 3 * ff_dim)), pl.BlockSpec((wide, 3 * ff_dim), lambda i, *_: (i, 0)))],
            grid=(n_seq,), name="ffn_grad",
        )[0]
        ffn_sum = over_seq(ffn_part)
        part2[1], _ = halve_all(part2[1], sent, "tp", tp_route[:-1])
        wait(*mid_low[0])
        mid_low.append(gather(mid_back(1, part2[1])))

        kv_parts = []
        ffn_parts = [ffn_keep, swap(after(ffn_send), "tp", 1)]
        out = attend_back(0, None)
        kv_parts.append(([out[2], swap(out[3], "seq", 1)], half_keys))
        pause()
        kv_parts[0] = halve(*kv_parts[0], "seq", routes[1][-2])
        wait(*mid_low[1])
        out = attend_back(1, out)
        low_all, query_low = out[:2]
        kv_parts.append(([out[2], swap(out[3], "seq", 1)], half_keys))
        lat_parts = [out[4], swap(out[5], "tp", 1)]
        pause()
        kv_parts[0] = halve_all(*kv_parts[0], "seq", routes[1][:-2])
        kv_parts[1] = halve(*kv_parts[1], "seq", routes[0][-2])
        for count in [n_tp >> i for i in range(1, tp_bits)]:
            ffn_parts = halve_rows(ffn_parts, count)
        own_lat = lat_dim // n_seq
        pieces = q_width // wide
        rows_out = q_width + pieces * own_lat
        if own_lat % 128:
            out_blocks = dot_rows(context, low_all).reshape(q_width, n_seq, wide).transpose(1, 0, 2)
            query_blocks = dot_rows(latent_norm, query_low).reshape(n_seq, own_lat, pieces, wide).transpose(0, 2, 1, 3)
            head_part = jnp.concatenate([out_blocks, query_blocks.reshape(n_seq, -1, wide)], axis=1)
            head_part = head_part.astype(BF).reshape(-1, wide)
        else:
            head_part = step(
                head_grad_kernel,
                [whole(context), (low_all, pl.BlockSpec((n_rows * length, wide), lambda i, *_: (0, i))),
                 (latent_norm, pl.BlockSpec((n_rows * length, own_lat), lambda i, *_: (0, i))), whole(query_low)],
                [(shape_of((n_seq * rows_out, wide)), pl.BlockSpec((rows_out, wide), lambda i, *_: (i, 0)))],
                grid=(n_seq,), name="head_grad",
            )[0]
        for count in [n_tp >> i for i in range(1, tp_bits)]:
            lat_parts = halve_rows(lat_parts, count)
        pause()
        kv_parts[1] = halve_all(*kv_parts[1], "seq", routes[0][:-2])
        lat_low = step(
            functools.partial(latent_back_kernel, n_rows),
            [whole(p) for p in lat_parts] + [whole(u) for u in unit_lat] + [whole(i) for i in inv_lat]
            + [gain_row(latent_gain)],
            [new((n_rows * block, lat_dim))], name="latent_back",
        )[0]
        lat_blocks = gather_start(lat_low)
        kv_sum = step(
            functools.partial(kv_split_kernel, n_rows, singles),
            [first(p, length) for parts, _ in kv_parts for p in parts],
            [new((n_rows * block, 2 * HD))] * n_tp,
            scratch=[pltpu.VMEM((length, 2 * HD), F32)], name="kv_split",
        )
        kv_sum = sent_over(kv_sum)
        pause()
        head_sum = over_seq(after(head_part))
        lat_blocks = gather_end(lat_blocks)
        pause()
        own_rows = pl.BlockSpec((n_rows, block, HD // 2), lambda i, info, *_: (0, info[0], 0))
        kv_low = step(
            functools.partial(key_back_kernel, n_rows),
            [whole(p) for p in kv_sum] + [(cosine, own_rows), (sine, own_rows)],
            [new((n_rows * block, 2 * HD))], name="key_back",
        )[0]
        kv_blocks = gather(kv_low)
        pause()

        def join(blocks, rels):
            width = blocks[0].shape[1]
            cols = width // n_tp
            count = n_rows * length
            out = step(
                functools.partial(join_kernel, n_rows, rels, len(blocks)), [whole(b) for b in blocks],
                [new((count, width))] + ([] if cols % 128 else [new((count, cols))]), name="join",
            )
            if cols % 128:
                return out[0], lax.dynamic_slice_in_dim(out[0], tp_me * cols, cols, 1)
            return out

        ffn_own = step(
            functools.partial(ffn_sum_kernel, n_rows), [whole(p) for p in ffn_parts] + [whole(m) for m in middle],
            [new((n_rows * block, model_dim))], name="ffn_sum",
        )[0]
        lat_all, lat_part = join(lat_blocks, tp_rels)
        lat_part_both = both(lat_part)
        kv_all, kv_part = join(kv_blocks, range(n_tp))
        kv_part_both = both(kv_part)
        ffn_blocks = gather_start(after(ffn_own))
        grad_lat = weight_grad(normed_both, lat_part_both, False, 0)
        lat_2 = next(grad_lat)
        grad_kv = weight_grad(normed_both, kv_part_both, False, 1)
        kv_2 = next(grad_kv)

        def input_step(r, held):
            return step(
                input_kernel,
                [row_block(lat_all, r), row_block(kv_all, r), row_of(layer_in, r), whole(query_down), whole(key_value),
                 row_block(low_all, r), gain_row(attn_gain)],
                [(shape_of(layer_in.shape), pl.BlockSpec((1, length, model_dim), lambda *_: (r, 0, 0)))],
                name="input", carried=going(held, (0, 0)),
            )

        out = input_step(0, None)
        lat_3 = next(grad_lat)
        kv_3 = next(grad_kv)
        input_grad = input_step(1, out)[0]
        lat_sum = next(grad_lat)
        shared_lat = gather(lat_sum.astype(BF))
        ffn_blocks = gather_end(ffn_blocks)
        pause()
        kv_grad_sum = next(grad_kv)
        ffn_grads = total([(ffn_sum, slice(None))], F32)
        down_grad, gate_grad, up_grad = ffn_grads[:, :ff_dim].T, ffn_grads[:, ff_dim : 2 * ff_dim], ffn_grads[:, 2 * ff_dim :]
        head_grads = total([(head_sum, slice(None))], F32)
        out_weight_grad = head_grads[:q_width]
        query_up_grad = head_grads[q_width:].reshape(pieces, own_lat, wide).transpose(1, 0, 2).reshape(own_lat, q_width)

        own_dim = model_dim // n_seq

        def own_part(array, count):
            return lax.dynamic_slice_in_dim(array, seq_me * count, count, 0)

        def row_sums(weight, grad):
            return jnp.sum(own_part(weight, grad.shape[0]).astype(F32) * grad, axis=1)

        def own_columns(weight):
            cols = weight.shape[1] // n_tp
            return lax.dynamic_slice_in_dim(weight, tp_me * cols, cols, 1)

        tp_sums = jnp.concatenate(
            [
                row_sums(gate_proj, gate_grad) + row_sums(up_proj, up_grad),
                row_sums(own_columns(query_down), lat_sum) + row_sums(own_columns(key_value), kv_grad_sum),
                row_sums(query_up, query_up_grad),
            ]
        )
        kv_rows = jnp.concatenate([kv_grad_sum, tp_sums.reshape(-1, kv_grad_sum.shape[1])], axis=0).astype(BF)
        wait(*shared_lat)
        shared_kv = gather(after(kv_rows))
        pause()
        layer_out = step(
            functools.partial(spread_kernel, tp_rels), [whole(p) for p in ffn_blocks], [new(layer_in.shape)],
            name="spread",
        )[0]
        if kv_part.shape[1] % 128:

            def side_by_side(pieces):
                cols = pieces[0].shape[1]
                blocks = jnp.take(jnp.stack(pieces)[:, :own_dim], jnp.stack([tp_me ^ r for r in range(n_tp)]), axis=0)
                return blocks.astype(F32).transpose(1, 0, 2).reshape(own_dim, n_tp * cols)

            down_q, kv_grad = side_by_side(shared_lat), side_by_side(shared_kv)
        else:
            down_q, kv_grad = step(
                functools.partial(shared_kernel, n_tp),
                [whole(p) for p in shared_lat] + [first(p, own_dim) for p in shared_kv],
                [new((own_dim, lat_dim), F32), new((own_dim, 2 * HD), F32)], name="shared",
            )
        tp_sums = sum(p[own_dim:].astype(F32) for p in shared_kv).reshape(-1)
        ffn_gain_grad = tp_sums[:own_dim] / own_part(ffn_gain, own_dim)
        attn_gain_grad = tp_sums[own_dim : 2 * own_dim] / own_part(attn_gain, own_dim)
        latent_gain_grad = tp_sums[2 * own_dim :] / own_part(latent_gain, own_lat)
        return (
            layer_out, input_grad, attn_gain_grad, down_q, latent_gain_grad, query_up_grad,
            kv_grad, out_weight_grad.reshape(q_width, own_dim), ffn_gain_grad, gate_grad, up_grad,
            down_grad.reshape(ff_dim, own_dim),
        )

    return shards


def solution(mesh):
    return jax.shard_map(
        build(mesh.shape["seq"], mesh.shape["tp"]),
        mesh=mesh,
        in_specs=(
            P(None, "seq", None), P(), P(), P(), P(None, "tp"), P(), P("tp", None), P(),
            P(None, "tp"), P(None, "tp"), P("tp", None), P(None, "seq", None), P(),
        ),
        out_specs=(
            P(None, "seq", None), P(None, "seq", None), P("seq"), P("seq", None), P("seq"),
            P("seq", "tp"), P("seq", None), P("tp", "seq"), P("seq"), P("seq", "tp"),
            P("seq", "tp"), P("tp", "seq"),
        ),
        check_vma=False,
    )
```

```python
import functools

import jax
import jax.numpy as jnp
from jax import lax
from jax.experimental import pallas as pl
from jax.experimental.pallas import tpu as pltpu
from jax.sharding import PartitionSpec as P

HD = 256
EPS = 1e-05
ROPE_BASE = 10000.0
NEG_FILL = -1e30
BF = jnp.bfloat16
F32 = jnp.float32
MIB = 1024 * 1024
VMEM_BYTES = 20 * MIB
COST = 1e12
HEADS_PER_STEP = 4


def dot(left, right):
    return jnp.dot(left, right, preferred_element_type=F32)


def dot_rows(left, right):
    return lax.dot_general(left, right, (((0,), (0,)), ((), ())), preferred_element_type=F32)


def dot_cols(left, right):
    return lax.dot_general(left, right, (((1,), (1,)), ((), ())), preferred_element_type=F32)


def inverse_rms(values):
    return lax.rsqrt(jnp.mean(values * values, axis=-1, keepdims=True) + EPS)


def back_norm(grad_out, unit_rows, inv_rms, gain):
    scaled = grad_out * gain
    return inv_rms * (scaled - unit_rows * jnp.mean(scaled * unit_rows, axis=-1, keepdims=True))


def turn(values, cosine, sine):
    half = HD // 2
    front, back = values[:, :half], values[:, half:]
    return front * cosine - back * sine, back * cosine + front * sine


def full_spec(shape):
    return pl.BlockSpec(tuple(shape), lambda *_: (0,) * len(shape))


def shape_of(shape, kind=BF):
    return jax.ShapeDtypeStruct(tuple(shape), kind)


def write_pieces(me, source, outs, layout):
    block = outs[0].shape[0] // len(layout[0])
    for out, rels in zip(outs, layout):
        for j, rel in enumerate(rels):
            out[j * block : (j + 1) * block, :] = source[block_rows(me ^ rel, block), :].astype(BF)


MICROS = {
    "front": 4, "query": 7, "attend": 13, "middle": 3, "ffn": 19, "mid_back": 3, "grad": 9, "ffn_grad": 22, "head_grad": 14, "pause": 3, "attend_back": 20,
    "latent_back": 3, "ffn_sum": 3, "spread": 3, "kv_split": 3, "key_back": 3, "join": 3, "input": 8, "shared": 3,
}


def run(kernel, scalars, inputs, outputs, grid=(1,), scratch=(), name=None, carried=(), vmem=VMEM_BYTES):
    n_in, n_scalars = len(inputs), len(scalars)
    moved = sum(a.size * a.dtype.itemsize for a, _ in inputs)

    def body(*refs):
        kernel(*refs[: n_scalars + n_in], *refs[n_scalars + n_in + len(carried) :])

    return pl.pallas_call(
        body,
        out_shape=[s for s, _ in outputs],
        grid_spec=pltpu.PrefetchScalarGridSpec(
            num_scalar_prefetch=n_scalars,
            grid=grid,
            in_specs=[s for _, s in inputs] + [pl.BlockSpec(memory_space=pl.ANY)] * len(carried),
            out_specs=[s for _, s in outputs],
            scratch_shapes=list(scratch),
        ),
        input_output_aliases={n_scalars + n_in + k: index for k, (index, _) in enumerate(carried)},
        compiler_params=pltpu.CompilerParams(
            dimension_semantics=("arbitrary",) * len(grid), vmem_limit_bytes=vmem
        ),
        cost_estimate=pl.CostEstimate(flops=int(MICROS[name] * COST), bytes_accessed=moved, transcendentals=0),
        name=name,
    )(*scalars, *[a for a, _ in inputs], *[a for _, a in carried])


def total_of(refs):
    total = refs[0][...].astype(F32)
    for ref in refs[1:]:
        total = total + ref[...].astype(F32)
    return total


def row_total(refs, r, n_rows, block):
    total = 0.0
    for ref in refs:
        at = r * (ref.shape[0] // n_rows)
        total = total + ref[at : at + block, :].astype(F32)
    return total


def block_rows(index, size):
    return pl.ds(pl.multiple_of(index * size, size), size)


def front_kernel(info, x_ref, gain_ref, w_ref, cos_ref, sin_ref, n_ref, kv_ref):
    x = x_ref[0].astype(F32)
    normed = (x * inverse_rms(x) * gain_ref[...]).astype(BF)
    n_ref[...] = normed
    kv = dot(normed, w_ref[...])
    front, back = turn(kv[:, :HD], cos_ref[0], sin_ref[0])
    kv_ref[:, : HD // 2] = front.astype(BF)
    kv_ref[:, HD // 2 : HD] = back.astype(BF)
    kv_ref[:, HD:] = kv[:, HD:].astype(BF)


def query_kernel(info, n_ref, wd_ref, gain_ref, wu_ref, cos_ref, sin_ref, ln_ref, ul_ref, il_ref, q_ref, held):
    latent = dot(n_ref[...], wd_ref[...])
    inv = inverse_rms(latent)
    unit = latent * inv
    normed = (unit * gain_ref[...]).astype(BF)
    ln_ref[...] = normed
    block = ul_ref.shape[0]
    held[...] = latent
    mine = held[block_rows(info[0], block), :]
    inv_mine = inverse_rms(mine)
    ul_ref[...] = mine * inv_mine
    il_ref[...] = jnp.broadcast_to(inv_mine, il_ref.shape)
    raw = dot(normed, wu_ref[...])
    cosine, sine = cos_ref[0], sin_ref[0]
    for h in range(raw.shape[1] // HD):
        front, back = turn(raw[:, h * HD : (h + 1) * HD], cosine, sine)
        q_ref[:, h * HD : h * HD + HD // 2] = front.astype(BF)
        q_ref[:, h * HD + HD // 2 : (h + 1) * HD] = back.astype(BF)


def starts_of(docs, row, places):
    end, start = 0, jnp.zeros_like(places)
    for d in range(docs.shape[1]):
        size = docs[row, d]
        end = end + size
        start = start + jnp.where(places >= end, size, 0)
    return start


def attend_kernel(row, order, layout, info, docs, q_ref, ka_ref, kb_ref, w_ref, ctx_ref, lse_ref, *rest):
    pieces, (acc, bias) = rest[: len(layout)], rest[len(layout) :]
    h = pl.program_id(0)
    length = q_ref.shape[0]
    half = len(order) // 2 * length
    me_tp, me_seq = info[0], info[1]

    @pl.when(h == 0)
    def _():
        places = me_seq * length + lax.broadcasted_iota(jnp.int32, (length, 1), 0)
        start = starts_of(docs, row, places)
        column = lax.broadcasted_iota(jnp.int32, (1, length), 1)
        for b, rel in enumerate(order):
            key = (me_seq ^ rel) * length + column
            allowed = (key >= start) & (key <= places)
            bias[:, b * length : (b + 1) * length] = jnp.where(allowed, 0.0, NEG_FILL)

    scale = jnp.asarray(HD ** (-0.5), BF)
    for i in range(q_ref.shape[1] // HD):
        cols = slice(i * HD, (i + 1) * HD)
        q = q_ref[:, cols] * scale
        sa = dot_cols(q, ka_ref[:, :HD]) + bias[:, :half]
        sb = dot_cols(q, kb_ref[:, :HD]) + bias[:, half:]
        peak = jnp.maximum(jnp.max(sa, axis=-1, keepdims=True), jnp.max(sb, axis=-1, keepdims=True))
        pa = jnp.exp(sa - peak)
        pb = jnp.exp(sb - peak)
        total = jnp.sum(pa, axis=-1, keepdims=True) + jnp.sum(pb, axis=-1, keepdims=True)
        out = dot(pa.astype(BF), ka_ref[:, HD:]) + dot(pb.astype(BF), kb_ref[:, HD:])
        out = (out / total).astype(BF)
        ctx_ref[:, cols] = out
        lse = jnp.broadcast_to(peak + jnp.log(total), (length, 128))
        lse_ref[i] = jnp.transpose(lse)[:1, :]
    part = dot(ctx_ref[...], w_ref[...])

    @pl.when(h == 0)
    def _():
        acc[...] = part

    @pl.when(h > 0)
    def _():
        acc[...] += part

    @pl.when(h == pl.num_programs(0) - 1)
    def _():
        write_pieces(me_tp, acc, pieces, layout)


def middle_kernel(info, *refs):
    parts, (x_ref, gain_ref, mid_ref, n2_ref) = refs[:-4], refs[-4:]
    mid = x_ref[0].astype(F32) + total_of(parts)
    mid_ref[...] = mid
    n2_ref[...] = (mid * inverse_rms(mid) * gain_ref[...]).astype(BF)


def place_pieces(me, pieces, out_ref, rels):
    per = len(rels) // len(pieces)
    block = pieces[0].shape[0] // per
    for i, rel in enumerate(rels):
        at = i % per * block
        out_ref[block_rows(me ^ rel, block), :] = pieces[i // per][at : at + block, :]


def ffn_kernel(n_parts, rels, layout, ff_layout, info, *refs):
    parts = refs[:n_parts]
    dy_ref, wg, wu, wd = refs[n_parts : n_parts + 4]
    outs = refs[n_parts + 4 :]
    n2_ref, hidden_ref = outs[:2]
    ff_refs, pieces = outs[2:4], outs[4 : 4 + len(layout)]
    acc = outs[4 + len(layout)]
    me = info[0]
    width = hidden_ref.shape[2]
    size = 512
    full, rest = width // size, width % size
    model = acc.shape[1]
    cut = min(1024, model)

    place_pieces(me, parts, n2_ref, rels)

    def hidden_part(c, at, count):
        here = pl.ds(at, count)
        gate = dot(n2_ref[...], wg[:, here])
        up = dot(n2_ref[...], wu[:, here])
        dhid = dot_cols(dy_ref[0], wd[here, :])
        sig = 1.0 / (1.0 + jnp.exp(-gate))
        swish = gate * sig
        hidden_ref[0, :, here] = (swish * up).astype(BF)
        hidden_ref[1, :, here] = (dhid * up * sig * (1.0 + gate * (1.0 - sig))).astype(BF)
        hidden_ref[2, :, here] = (dhid * swish).astype(BF)

    @pl.loop(0, full)
    def _(c):
        hidden_part(c, pl.multiple_of(c * size, size), size)

    if rest:
        hidden_part(full, full * size, rest)

    @pl.loop(0, model // cut)
    def _(n):
        here = pl.ds(pl.multiple_of(n * cut, cut), cut)
        acc[:, here] = dot_cols(hidden_ref[1], wg[here, :]) + dot_cols(hidden_ref[2], wu[here, :])

    write_pieces(me, acc, pieces, layout)

    @pl.loop(0, model // cut)
    def _(n):
        here = pl.ds(pl.multiple_of(n * cut, cut), cut)
        acc[:, here] = dot(hidden_ref[0], wd[:, here])

    write_pieces(me, acc, ff_refs, ff_layout)


def mid_back_kernel(info, *refs):
    parts, (mid_ref, dy_ref, gain_ref, low_ref) = refs[:-4], refs[-4:]
    d2 = total_of(parts)
    mid = mid_ref[...]
    inv = inverse_rms(mid)
    unit = mid * inv
    low_ref[...] = (dy_ref[0].astype(F32) + back_norm(d2, unit, inv, gain_ref[...])).astype(BF)


def attend_back_kernel(row, order, n_parts, rels, layout, info, docs, *refs):
    lows, refs = refs[:n_parts], refs[n_parts:]
    q_ref, ka_ref, kb_ref, lse_ref, wo_ref, wq_ref, cos_ref, sin_ref = refs[:8]
    low_ref, qlow_ref, keep_ref, send_ref = refs[8:12]
    pieces = refs[12:14]
    bias, dkv, lat = refs[14:]
    h = pl.program_id(0)
    length = q_ref.shape[0]
    half = len(order) // 2 * length
    me_tp, me_seq = info[0], info[1]
    scale = HD ** (-0.5)

    @pl.when(h == 0)
    def _():
        place_pieces(me_tp, lows, low_ref, rels)
        places = me_seq * length + lax.broadcasted_iota(jnp.int32, (1, length), 1)
        start = starts_of(docs, row, places)
        column = lax.broadcasted_iota(jnp.int32, (length, 1), 0)
        for b, rel in enumerate(order):
            key = (me_seq ^ rel) * length + column
            allowed = (key >= start) & (key <= places)
            bias[b * length : (b + 1) * length, :] = jnp.where(allowed, 0.0, NEG_FILL)

    dctx_all = dot_cols(low_ref[...], wo_ref[...]).astype(BF)
    for n in range(q_ref.shape[1] // HD):
        cols = slice(n * HD, (n + 1) * HD)
        q = q_ref[:, cols] * jnp.asarray(scale, BF)
        dctx = dctx_all[:, cols]
        lse = lse_ref[n]
        probs, dprobs = [], []
        delta = 0.0
        for i, kv_ref in enumerate((ka_ref, kb_ref)):
            scores = dot_cols(kv_ref[:, :HD], q) + bias[i * half : (i + 1) * half, :]
            prob = jnp.exp(scores - lse)
            dprob = dot_cols(kv_ref[:, HD:], dctx)
            delta = delta + jnp.sum(prob * dprob, axis=0, keepdims=True)
            probs.append(prob), dprobs.append(dprob)
        dq = 0.0
        for i, kv_ref in enumerate((ka_ref, kb_ref)):
            rows = slice(i * half, (i + 1) * half)
            dscore = (probs[i] * (dprobs[i] - delta)).astype(BF)
            dq = dq + dot_rows(dscore, kv_ref[:, :HD])
            dk = dot(dscore, q)
            dv = dot(probs[i].astype(BF), dctx)
            if n == 0:

                @pl.when(h == 0)
                def _():
                    dkv[rows, :HD] = dk
                    dkv[rows, HD:] = dv

                @pl.when(h > 0)
                def _():
                    dkv[rows, :HD] += dk
                    dkv[rows, HD:] += dv

            else:
                dkv[rows, :HD] += dk
                dkv[rows, HD:] += dv

        front, back = turn(dq * scale, cos_ref[0], -sin_ref[0])
        qlow_ref[:, n * HD : n * HD + HD // 2] = front.astype(BF)
        qlow_ref[:, n * HD + HD // 2 : (n + 1) * HD] = back.astype(BF)
    part = dot_cols(qlow_ref[...], wq_ref[...])

    @pl.when(h == 0)
    def _():
        lat[...] = part

    @pl.when(h > 0)
    def _():
        lat[...] += part

    @pl.when(h == pl.num_programs(0) - 1)
    def _():
        keep_ref[...] = dkv[:half, :].astype(BF)
        send_ref[...] = dkv[half:, :].astype(BF)
        write_pieces(me_tp, lat, pieces, layout)


def kv_split_kernel(n_rows, layout, info, *refs):
    pieces, held = refs[-1 - len(layout) : -1], refs[-1]
    count = (len(refs) - 1 - len(layout)) // n_rows
    rows = pieces[0].shape[0] // n_rows
    for r in range(n_rows):
        held[...] = total_of(refs[r * count : (r + 1) * count])
        outs = [piece.at[r * rows : (r + 1) * rows, :] for piece in pieces]
        write_pieces(info[0], held, outs, layout)


def latent_back_kernel(n_rows, info, *refs):
    units, invs = refs[-2 - 2 * n_rows : -2 - n_rows], refs[-2 - n_rows : -2]
    parts, (gain_ref, low_ref) = refs[: -2 - 2 * n_rows], refs[-2:]
    block = low_ref.shape[0] // n_rows
    for r in range(n_rows):
        rows = slice(r * block, (r + 1) * block)
        unit, grad = units[r][...], row_total(parts, r, n_rows, block)
        low_ref[rows, :] = back_norm(grad, unit, invs[r][:, :1], gain_ref[...]).astype(BF)


def key_back_kernel(n_rows, info, *refs):
    parts, (cos_ref, sin_ref, out_ref) = refs[:-3], refs[-3:]
    block = out_ref.shape[0] // n_rows
    for r in range(n_rows):
        rows = slice(r * block, (r + 1) * block)
        total = row_total(parts, r, n_rows, block)
        front, back = turn(total[:, :HD], cos_ref[r], -sin_ref[r])
        out_ref[rows, : HD // 2] = front.astype(BF)
        out_ref[rows, HD // 2 : HD] = back.astype(BF)
        out_ref[rows, HD:] = total[:, HD:].astype(BF)


def ffn_sum_kernel(n_rows, info, *refs):
    parts, mids, out_ref = refs[: -1 - n_rows], refs[-1 - n_rows : -1], refs[-1]
    block = out_ref.shape[0] // n_rows
    for r in range(n_rows):
        out_ref[r * block : (r + 1) * block, :] = (row_total(parts, r, n_rows, block) + mids[r][...]).astype(BF)


def spread_kernel(rels, info, *refs):
    pieces, out_ref = refs[:-1], refs[-1]
    n_rows, per = out_ref.shape[0], len(rels) // len(pieces)
    block = out_ref.shape[1] // len(rels)
    for i, rel in enumerate(rels):
        for row in range(n_rows):
            at = (i % per * n_rows + row) * block
            out_ref[row, block_rows(info[0] ^ rel, block), :] = pieces[i // per][at : at + block, :]


def join_kernel(n_rows, rels, count, info, *refs):
    pieces, all_ref = refs[:count], refs[count]
    me, n_tp = info[0], len(rels)
    per = n_tp // count
    block = pieces[0].shape[0] // (n_rows * per)
    for i, rel in enumerate(rels):
        for r in range(n_rows):
            at = (i % per * n_rows + r) * block
            all_ref[block_rows(r * n_tp + (me ^ rel), block), :] = pieces[i // per][at : at + block, :]
    if len(refs) > count + 1:
        part_ref = refs[count + 1]
        part_ref[...] = all_ref[:, block_rows(me, part_ref.shape[1])]


def input_kernel(info, lat_ref, kv_ref, x_ref, wd_ref, wkv_ref, low_ref, gain_ref, out_ref):
    dn = dot_cols(lat_ref[...], wd_ref[...]) + dot_cols(kv_ref[...], wkv_ref[...])
    x = x_ref[0].astype(F32)
    inv = inverse_rms(x)
    unit = x * inv
    out_ref[0] = (low_ref[...].astype(F32) + back_norm(dn, unit, inv, gain_ref[...])).astype(BF)


def grad_kernel(table, *refs):
    count = (len(refs) - 2) // 2
    keep_ref, send_ref = refs[2 * count :]

    def load(ref):
        value = ref[...]
        return value.reshape(-1, value.shape[-1])

    total = dot_rows(load(refs[0]), load(refs[count]))
    for i in range(1, count):
        total = total + dot_rows(load(refs[i]), load(refs[count + i]))
    total = total.astype(BF)
    i, half = pl.program_id(0), pl.num_programs(0) // 2

    @pl.when(i < half)
    def _():
        keep_ref[...] = total

    @pl.when(i >= half)
    def _():
        send_ref[...] = total


def ffn_grad_kernel(info, hidden_ref, n2_ref, dy_ref, out_ref):
    dy = dy_ref[...]
    dy = dy.reshape(-1, dy.shape[-1])
    width = hidden_ref.shape[2]
    out_ref[:, :width] = dot_rows(dy, hidden_ref[0]).astype(BF)
    out_ref[:, width : 2 * width] = dot_rows(n2_ref[...], hidden_ref[1]).astype(BF)
    out_ref[:, 2 * width :] = dot_rows(n2_ref[...], hidden_ref[2]).astype(BF)


def head_grad_kernel(info, context_ref, low_ref, latent_ref, query_ref, out_ref):
    rows, width = context_ref.shape[1], low_ref.shape[1]
    out_ref[:rows, :] = dot_rows(context_ref[...], low_ref[...]).astype(BF)
    count = latent_ref.shape[1]
    part = dot_rows(latent_ref[...], query_ref[...]).astype(BF)
    for i in range(part.shape[1] // width):
        out_ref[rows + i * count : rows + (i + 1) * count, :] = part[:, i * width : (i + 1) * width]


def pause_kernel(info, out_ref):
    for i in range(out_ref.shape[0]):
        out_ref[i] = info[i]


def shared_kernel(n_tp, info, *refs):
    for pieces, out_ref in ((refs[:n_tp], refs[2 * n_tp]), (refs[n_tp : 2 * n_tp], refs[2 * n_tp + 1])):
        for r in range(n_tp):
            width = pieces[r].shape[1]
            out_ref[:, block_rows(info[0] ^ r, width)] = pieces[r][...].astype(F32)


def build(n_seq, n_tp):
    seq_bits = n_seq.bit_length() - 1
    tp_bits = n_tp.bit_length() - 1

    def swap(value, axis, mask):
        count = n_seq if axis == "seq" else n_tp
        return lax.ppermute(value, axis, [(i, i ^ mask) for i in range(count)])

    def spread(bits):
        order = [0]
        for bit in bits:
            order = order + [o | (1 << bit) for o in order]
        return order

    upward = list(range(1, seq_bits))
    routes = (upward + [0], upward[::-1] + [0])
    tp_route = list(reversed(range(tp_bits)))
    tp_rels = spread(tp_route)
    halves = [tp_rels[: n_tp // 2], tp_rels[n_tp // 2 :]]
    singles = [[r] for r in range(n_tp)]
    layouts = [singles, halves]

    def gather(block):
        return [block] + [swap(block, "tp", r) for r in range(1, n_tp)]

    def shards(
        layer_in, attn_gain, query_down, latent_gain, query_up, key_value, attn_out,
        ffn_gain, gate_proj, up_proj, down_proj, out_grad, doc_lengths,
    ):
        n_rows, length, model_dim = layer_in.shape
        lat_dim, q_width = query_up.shape
        ff_dim = gate_proj.shape[1]
        heads = q_width // HD
        block = length // n_tp
        half_keys = n_seq // 2 * length
        rows = range(n_rows)
        seq_me, tp_me = lax.axis_index("seq"), lax.axis_index("tp")
        state = [jnp.stack([tp_me, seq_me, jnp.zeros_like(tp_me)]).astype(jnp.int32)]
        last, due = [], []

        def wait(*arrays):
            due.extend(arrays)

        def pause():
            state[0] = step(
                pause_kernel, [], [(shape_of((3,), jnp.int32), pl.BlockSpec(memory_space=pltpu.SMEM))], name="pause",
            )[0]

        def after(value):
            ready = last[-1:] + due
            due.clear()
            return lax.optimization_barrier((value, *ready))[0] if ready else value

        def step(kernel, inputs, outputs, table=None, docs=False, **kw):
            scalars = (after(state[0] if table is None else table),) + ((doc_lengths,) if docs else ())
            out = run(kernel, scalars, inputs, outputs, **kw)
            last.append(min(out, key=lambda o: o.size))
            return out

        def total(values, kind):
            out = after(values[-1][0])[values[-1][1]].astype(F32)
            for array, index in values[:-1]:
                out = out + array[index].astype(F32)
            out = out.astype(kind)
            last.append(out)
            return out

        def add(parts, rows, at, kind):
            return total([(p, slice(at * rows, (at + 1) * rows)) for p in parts], kind)

        def halve(parts, rows, axis, bit):
            half = rows // 2
            return parts + [swap(add(parts, half, 1, BF), axis, 1 << bit)], half

        def halve_all(parts, rows, axis, bits):
            for bit in reversed(bits):
                parts, rows = halve(parts, rows, axis, bit)
            return parts, rows

        places = seq_me * length + jnp.arange(length, dtype=jnp.int32)
        ends = jnp.cumsum(doc_lengths, axis=1)
        passed = places[None, :, None] >= ends[:, None, :]
        inner = places[None, :] - jnp.sum(jnp.where(passed, doc_lengths[:, None, :], 0), axis=-1)
        frequency = ROPE_BASE ** (-jnp.arange(HD // 2, dtype=F32) / (HD // 2))
        angles = inner.astype(F32)[:, :, None] * frequency
        cosine, sine = jnp.cos(angles), jnp.sin(angles)
        gain_row = lambda gain: (gain.reshape(1, -1), full_spec((1, gain.shape[0])))

        def whole(array):
            return array, full_spec(array.shape)

        def first(array, count):
            return array, full_spec((count, array.shape[1]))

        def row_of(array, r):
            return array, pl.BlockSpec((1,) + array.shape[1:], lambda *_: (r, 0, 0))

        def own_of(array, r):
            shape = (1, block, array.shape[2])
            return array, pl.BlockSpec(shape, lambda i, info, *_: (r, info[0], 0))

        def new(shape, kind=BF):
            return shape_of(shape, kind), full_spec(shape)

        per_step = min(HEADS_PER_STEP, heads)
        group = per_step * HD

        def head_cols(array):
            return array, pl.BlockSpec((array.shape[0], group), lambda h, *_: (0, h))

        def head_rows(array):
            return array, pl.BlockSpec((group, array.shape[1]), lambda h, *_: (h, 0))

        def row_pieces(r, width):
            rows_out = n_tp // 2 * block
            spec = pl.BlockSpec((rows_out, width), lambda *_: (r, 0))
            return [(shape_of((n_rows * rows_out, width)), spec)] * 2

        def pieces_of(layout, width):
            return [new((len(rels) * block, width)) for rels in layout]

        on_chip = pl.BlockSpec(memory_space=pltpu.VMEM)
        weights = [pltpu.with_memory_space_constraint(w, pltpu.VMEM) for w in (gate_proj, up_proj, down_proj)]

        def rows_of(width, r, spec=None):
            return shape_of((n_rows * length, width)), spec or pl.BlockSpec((length, width), lambda *_: (r, 0))

        def row_block(array, r):
            return array, pl.BlockSpec((length, array.shape[1]), lambda *_: (r, 0))

        def going(held, *pairs):
            return [(index, held[key]) for index, key in pairs] if held else []

        def front(r, held):
            return step(
                front_kernel,
                [row_of(layer_in, r), gain_row(attn_gain), whole(key_value), row_of(cosine, r), row_of(sine, r)],
                [rows_of(model_dim, r), new((length, 2 * HD))], name="front", carried=going(held, (0, 0)),
            )

        def query(r, held):
            return step(
                query_kernel,
                [row_block(normed, r), whole(query_down), gain_row(latent_gain), whole(query_up),
                 row_of(cosine, r), row_of(sine, r)],
                [rows_of(lat_dim, r), new((block, lat_dim), F32), new((block, 128), F32), new((length, q_width))],
                scratch=[pltpu.VMEM((length, lat_dim), F32)], name="query", carried=going(held, (0, 0)),
            )

        def attend(r, held):
            return step(
                functools.partial(attend_kernel, r, spread(routes[(r + 1) % 2]), layouts[r]),
                [head_cols(queries[r]), whole(near[r]), whole(far[r]), head_rows(attn_out)],
                [
                    rows_of(q_width, r, pl.BlockSpec((length, group), lambda h, *_: (r, h))),
                    (shape_of((heads, 1, length), F32), pl.BlockSpec((per_step, 1, length), lambda h, *_: (h, 0, 0))),
                ] + pieces_of(layouts[r], model_dim),
                docs=True, grid=(heads // per_step,),
                scratch=[pltpu.VMEM((length, model_dim), F32), pltpu.VMEM((length, 2 * half_keys), F32)],
                name="attend", vmem=min(58, 26 * half_keys // 1024) * MIB, carried=going(held, (0, 0)),
            )

        def mid_step(r, parts):
            return step(
                middle_kernel, [first(p, block) for p in parts] + [own_of(layer_in, r), gain_row(ffn_gain)],
                [new((block, model_dim), F32), new((block, model_dim))], name="middle", vmem=24 * MIB,
            )

        def ffn(r, held):
            return step(
                functools.partial(ffn_kernel, len(normed2[r]), range(n_tp), layouts[r], halves),
                [whole(p) for p in normed2[r]] + [row_of(out_grad, r),
                 (weights[0], on_chip), (weights[1], on_chip), (weights[2], on_chip)],
                [rows_of(model_dim, r),
                 (shape_of((3, n_rows * length, ff_dim)), pl.BlockSpec((3, length, ff_dim), lambda *_: (0, r, 0)))]
                + row_pieces(r, model_dim) + pieces_of(layouts[r], model_dim),
                scratch=[pltpu.VMEM((length, model_dim), F32)], vmem=24 * MIB,
                name="ffn", carried=going(held, *[(i, i) for i in range(4)]),
            )

        def mid_back(r, parts):
            return step(
                mid_back_kernel,
                [first(p, block) for p in parts] + [whole(middle[r]), own_of(out_grad, r), gain_row(ffn_gain)],
                [new((block, model_dim))], name="mid_back",
            )[0]

        def attend_back(r, held):
            return step(
                functools.partial(attend_back_kernel, r, spread(routes[(r + 1) % 2]), len(mid_low[r]), range(n_tp), halves),
                [whole(p) for p in mid_low[r]]
                + [head_cols(queries[r]), whole(near[r]), whole(far[r]),
                   (lse[r], pl.BlockSpec((per_step, 1, length), lambda h, *_: (h, 0, 0))),
                   head_rows(attn_out), head_cols(query_up), row_of(cosine, r), row_of(sine, r)],
                [rows_of(model_dim, r), rows_of(q_width, r, pl.BlockSpec((length, group), lambda h, *_: (r, h))),
                 new((half_keys, 2 * HD)), new((half_keys, 2 * HD))] + row_pieces(r, lat_dim),
                docs=True, grid=(heads // per_step,),
                scratch=[pltpu.VMEM((2 * half_keys, length), F32), pltpu.VMEM((2 * half_keys, 2 * HD), F32),
                         pltpu.VMEM((length, lat_dim), F32)],
                name="attend_back", vmem=min(58, 32 * half_keys // 1024) * MIB, carried=going(held, (0, 0), (1, 1), (4, 4), (5, 5)),
            )

        def halve_rows(parts, count):
            half = count // 2 * block
            width = parts[0].shape[1]
            values = [(p.reshape(n_rows, -1, width), (slice(None), slice(half, 2 * half))) for p in parts]
            away = total(values, BF).reshape(n_rows * half, width)
            return parts + [swap(away, "tp", 1 << tp_route[count.bit_length() - 2])]

        def joined_pair(held):
            pair = jnp.concatenate([after(held[0]), held[1]], axis=0)
            last.append(pair)
            return pair

        def gather_start(piece):
            return piece, swap(piece, "tp", 1 << tp_route[0])

        def gather_end(held):
            for bit in tp_route[1:]:
                held = joined_pair(held)
                held = held, swap(held, "tp", 1 << bit)
            return list(held)

        def both(array):
            return [array, swap(array, "seq", 1)]

        def weight_grad(acts, deltas, by_cols, route):
            acts, deltas = [[a if isinstance(a, tuple) else (a, None) for a in pair] for pair in (acts, deltas)]
            bits = routes[route][:-1]
            order = [o for o in spread(bits)]
            count = n_seq // 2
            size = (deltas if by_cols else acts)[0][0].shape[-1] // n_seq
            if size % 128:
                flat = [jnp.concatenate([a for a, _ in pair], axis=0) for pair in (acts, deltas)]
                full = dot_rows(*flat).astype(BF)
                blocks = jnp.take(full.reshape(n_seq, -1, full.shape[1]), jnp.stack([seq_me ^ o for o in order]), axis=0)
                parts, left = halve([blocks.reshape(-1, full.shape[1])], count * size, "seq", bits[-1])
            else:

                def operands(arrays, cut):
                    out = []
                    for array, which in arrays:
                        lead = array.shape[:-1]
                        if which is not None:
                            out.append((array, pl.BlockSpec((1,) + array.shape[1:], lambda i, t: (which, 0, 0))))
                        elif cut:
                            zeros = (0,) * len(lead)
                            out.append((array, pl.BlockSpec(lead + (size,), lambda i, t, z=zeros: z + (t[i],))))
                        else:
                            out.append(whole(array))
                    return out

                shape = (acts[0][0].shape[-1], size) if by_cols else (size, deltas[0][0].shape[-1])
                half = count // 2
                part = shape_of((half * shape[0], shape[1]))
                keep, away = step(
                    grad_kernel, operands(acts, not by_cols) + operands(deltas, by_cols),
                    [(part, pl.BlockSpec(shape, lambda i, t: (jnp.minimum(i, half - 1), 0))),
                     (part, pl.BlockSpec(shape, lambda i, t: (jnp.maximum(i - half, 0), 0)))],
                    table=jnp.stack([seq_me ^ o for o in order]).astype(jnp.int32), grid=(count,), name="grad",
                )
                parts, left = [keep, swap(away, "seq", 1 << bits[-1])], keep.shape[0]
            yield parts[-1]
            parts, left = halve_all(parts, left, "seq", bits[:-1])
            yield parts[-1]
            yield add(parts, left, 0, F32)

        held, out = [], None
        for r in rows:
            out = front(r, out)
            held.append([out[1], swap(out[1], "seq", 1 << routes[(r + 1) % 2][0])])
        normed = out[0]
        normed_both = both(normed)
        unit_lat, inv_lat, queries = [], [], []

        def widen(r, bit):
            pair = joined_pair(held[r])
            held[r] = [pair, swap(pair, "seq", 1 << bit)]

        for bit in range(1, seq_bits - 1):
            for r in rows:
                widen(r, routes[(r + 1) % 2][bit])
        out = None
        for r in rows:
            out = query(r, out)
            unit_lat.append(out[1]), inv_lat.append(out[2]), queries.append(out[3])
        wait(normed_both[1])
        latent_norm = out[0]
        near, far = [None] * n_rows, [None] * n_rows
        lse, part1, out = [], [], None

        def sent_over(pieces):
            if len(pieces) == 2:
                return [pieces[0], swap(pieces[1], "tp", 1)]
            return [pieces[0]] + [swap(pieces[r], "tp", r) for r in range(1, n_tp)]

        for r in rows:
            widen(r, 0)
            near[r], far[r] = held[r]
            out = attend(r, out)
            lse.append(out[1])
            part1.append(sent_over(out[2:]))
        context = out[0]
        sent = n_tp // 2 * block
        middle, normed2 = [], []
        mid, n2 = mid_step(0, part1[0])
        middle.append(mid)
        normed2.append(gather(n2))
        part1[1], _ = halve_all(part1[1], sent, "tp", tp_route[:-1])
        wait(*normed2[0])
        mid, n2 = mid_step(1, part1[1])
        middle.append(mid)
        normed2.append(gather(n2))

        part2, out = [], None
        for r in rows:
            out = ffn(r, out)
            part2.append(sent_over(out[4:]))
        n2_all, hidden, ffn_keep, ffn_send = out[:4]
        mid_low = [gather(mid_back(0, part2[0]))]
        wide = model_dim // n_seq

        def over_seq(part):
            return lax.psum_scatter(part, "seq", scatter_dimension=0, tiled=True)

        ffn_part = step(
            ffn_grad_kernel,
            [whole(hidden), (n2_all, pl.BlockSpec((n_rows * length, wide), lambda i, *_: (0, i))),
             (out_grad, pl.BlockSpec((n_rows, length, wide), lambda i, *_: (0, 0, i)))],
            [(shape_of((model_dim, 3 * ff_dim)), pl.BlockSpec((wide, 3 * ff_dim), lambda i, *_: (i, 0)))],
            grid=(n_seq,), name="ffn_grad",
        )[0]
        ffn_sum = over_seq(ffn_part)
        part2[1], _ = halve_all(part2[1], sent, "tp", tp_route[:-1])
        wait(*mid_low[0])
        mid_low.append(gather(mid_back(1, part2[1])))

        kv_parts = []
        ffn_parts = [ffn_keep, swap(after(ffn_send), "tp", 1)]
        out = attend_back(0, None)
        kv_parts.append(([out[2], swap(out[3], "seq", 1)], half_keys))
        pause()
        kv_parts[0] = halve(*kv_parts[0], "seq", routes[1][-2])
        wait(*mid_low[1])
        out = attend_back(1, out)
        low_all, query_low = out[:2]
        kv_parts.append(([out[2], swap(out[3], "seq", 1)], half_keys))
        lat_parts = [out[4], swap(out[5], "tp", 1)]
        pause()
        kv_parts[0] = halve_all(*kv_parts[0], "seq", routes[1][:-2])
        kv_parts[1] = halve(*kv_parts[1], "seq", routes[0][-2])
        for count in [n_tp >> i for i in range(1, tp_bits)]:
            ffn_parts = halve_rows(ffn_parts, count)
        own_lat = lat_dim // n_seq
        pieces = q_width // wide
        rows_out = q_width + pieces * own_lat
        if own_lat % 128:
            out_blocks = dot_rows(context, low_all).reshape(q_width, n_seq, wide).transpose(1, 0, 2)
            query_blocks = dot_rows(latent_norm, query_low).reshape(n_seq, own_lat, pieces, wide).transpose(0, 2, 1, 3)
            head_part = jnp.concatenate([out_blocks, query_blocks.reshape(n_seq, -1, wide)], axis=1)
            head_part = head_part.astype(BF).reshape(-1, wide)
        else:
            head_part = step(
                head_grad_kernel,
                [whole(context), (low_all, pl.BlockSpec((n_rows * length, wide), lambda i, *_: (0, i))),
                 (latent_norm, pl.BlockSpec((n_rows * length, own_lat), lambda i, *_: (0, i))), whole(query_low)],
                [(shape_of((n_seq * rows_out, wide)), pl.BlockSpec((rows_out, wide), lambda i, *_: (i, 0)))],
                grid=(n_seq,), name="head_grad",
            )[0]
        for count in [n_tp >> i for i in range(1, tp_bits)]:
            lat_parts = halve_rows(lat_parts, count)
        pause()
        kv_parts[1] = halve_all(*kv_parts[1], "seq", routes[0][:-2])
        lat_low = step(
            functools.partial(latent_back_kernel, n_rows),
            [whole(p) for p in lat_parts] + [whole(u) for u in unit_lat] + [whole(i) for i in inv_lat]
            + [gain_row(latent_gain)],
            [new((n_rows * block, lat_dim))], name="latent_back",
        )[0]
        lat_blocks = gather_start(lat_low)
        kv_sum = step(
            functools.partial(kv_split_kernel, n_rows, singles),
            [first(p, length) for parts, _ in kv_parts for p in parts],
            [new((n_rows * block, 2 * HD))] * n_tp,
            scratch=[pltpu.VMEM((length, 2 * HD), F32)], name="kv_split",
        )
        kv_sum = sent_over(kv_sum)
        ffn_own = step(
            functools.partial(ffn_sum_kernel, n_rows), [whole(p) for p in ffn_parts] + [whole(m) for m in middle],
            [new((n_rows * block, model_dim))], name="ffn_sum",
        )[0]
        head_sum = over_seq(after(head_part))
        lat_blocks = gather_end(lat_blocks)
        pause()
        own_dim = model_dim // n_seq

        def own_part(array, count):
            return lax.dynamic_slice_in_dim(array, seq_me * count, count, 0)

        def row_sums(weight, grad):
            return jnp.sum(own_part(weight, grad.shape[0]).astype(F32) * grad, axis=1)

        ffn_grads = total([(ffn_sum, slice(None))], F32)
        down_grad, gate_grad, up_grad = ffn_grads[:, :ff_dim].T, ffn_grads[:, ff_dim : 2 * ff_dim], ffn_grads[:, 2 * ff_dim :]
        ffn_rows = row_sums(gate_proj, gate_grad) + row_sums(up_proj, up_grad)
        last.append(ffn_rows)
        own_rows = pl.BlockSpec((n_rows, block, HD // 2), lambda i, info, *_: (0, info[0], 0))
        kv_low = step(
            functools.partial(key_back_kernel, n_rows),
            [whole(p) for p in kv_sum] + [(cosine, own_rows), (sine, own_rows)],
            [new((n_rows * block, 2 * HD))], name="key_back",
        )[0]
        kv_blocks = gather(kv_low)
        pause()

        def join(blocks, rels):
            width = blocks[0].shape[1]
            cols = width // n_tp
            count = n_rows * length
            out = step(
                functools.partial(join_kernel, n_rows, rels, len(blocks)), [whole(b) for b in blocks],
                [new((count, width))] + ([] if cols % 128 else [new((count, cols))]), name="join",
            )
            if cols % 128:
                return out[0], lax.dynamic_slice_in_dim(out[0], tp_me * cols, cols, 1)
            return out

        lat_all, lat_part = join(lat_blocks, tp_rels)
        lat_part_both = both(lat_part)
        kv_all, kv_part = join(kv_blocks, range(n_tp))
        kv_part_both = both(kv_part)
        ffn_blocks = gather_start(after(ffn_own))
        grad_lat = weight_grad(normed_both, lat_part_both, False, 0)
        lat_2 = next(grad_lat)
        grad_kv = weight_grad(normed_both, kv_part_both, False, 1)
        kv_2 = next(grad_kv)

        def input_step(r, held):
            return step(
                input_kernel,
                [row_block(lat_all, r), row_block(kv_all, r), row_of(layer_in, r), whole(query_down), whole(key_value),
                 row_block(low_all, r), gain_row(attn_gain)],
                [(shape_of(layer_in.shape), pl.BlockSpec((1, length, model_dim), lambda *_: (r, 0, 0)))],
                name="input", carried=going(held, (0, 0)),
            )

        out = input_step(0, None)
        lat_3 = next(grad_lat)
        kv_3 = next(grad_kv)
        input_grad = input_step(1, out)[0]
        lat_sum = next(grad_lat)
        shared_lat = gather(lat_sum.astype(BF))
        ffn_blocks = gather_end(ffn_blocks)
        pause()
        kv_grad_sum = next(grad_kv)
        head_grads = total([(head_sum, slice(None))], F32)
        out_weight_grad = head_grads[:q_width]
        query_up_grad = head_grads[q_width:].reshape(pieces, own_lat, wide).transpose(1, 0, 2).reshape(own_lat, q_width)

        def own_columns(weight):
            cols = weight.shape[1] // n_tp
            return lax.dynamic_slice_in_dim(weight, tp_me * cols, cols, 1)

        tp_sums = jnp.concatenate(
            [
                ffn_rows,
                row_sums(own_columns(query_down), lat_sum) + row_sums(own_columns(key_value), kv_grad_sum),
                row_sums(query_up, query_up_grad),
            ]
        )
        kv_rows = jnp.concatenate([kv_grad_sum, tp_sums.reshape(-1, kv_grad_sum.shape[1])], axis=0).astype(BF)
        wait(*shared_lat)
        shared_kv = gather(after(kv_rows))
        pause()
        layer_out = step(
            functools.partial(spread_kernel, tp_rels), [whole(p) for p in ffn_blocks], [new(layer_in.shape)],
            name="spread",
        )[0]
        if kv_part.shape[1] % 128:

            def side_by_side(pieces):
                cols = pieces[0].shape[1]
                blocks = jnp.take(jnp.stack(pieces)[:, :own_dim], jnp.stack([tp_me ^ r for r in range(n_tp)]), axis=0)
                return blocks.astype(F32).transpose(1, 0, 2).reshape(own_dim, n_tp * cols)

            down_q, kv_grad = side_by_side(shared_lat), side_by_side(shared_kv)
        else:
            down_q, kv_grad = step(
                functools.partial(shared_kernel, n_tp),
                [whole(p) for p in shared_lat] + [first(p, own_dim) for p in shared_kv],
                [new((own_dim, lat_dim), F32), new((own_dim, 2 * HD), F32)], name="shared",
            )
        tp_sums = sum(p[own_dim:].astype(F32) for p in shared_kv).reshape(-1)
        ffn_gain_grad = tp_sums[:own_dim] / own_part(ffn_gain, own_dim)
        attn_gain_grad = tp_sums[own_dim : 2 * own_dim] / own_part(attn_gain, own_dim)
        latent_gain_grad = tp_sums[2 * own_dim :] / own_part(latent_gain, own_lat)
        return (
            layer_out, input_grad, attn_gain_grad, down_q, latent_gain_grad, query_up_grad,
            kv_grad, out_weight_grad.reshape(q_width, own_dim), ffn_gain_grad, gate_grad, up_grad,
            down_grad.reshape(ff_dim, own_dim),
        )

    return shards


def solution(mesh):
    return jax.shard_map(
        build(mesh.shape["seq"], mesh.shape["tp"]),
        mesh=mesh,
        in_specs=(
            P(None, "seq", None), P(), P(), P(), P(None, "tp"), P(), P("tp", None), P(),
            P(None, "tp"), P(None, "tp"), P("tp", None), P(None, "seq", None), P(),
        ),
        out_specs=(
            P(None, "seq", None), P(None, "seq", None), P("seq"), P("seq", None), P("seq"),
            P("seq", "tp"), P("seq", None), P("tp", "seq"), P("seq"), P("seq", "tp"),
            P("seq", "tp"), P("tp", "seq"),
        ),
        check_vma=False,
    )
```

```python
import functools

import jax
import jax.numpy as jnp
from jax import lax
from jax.experimental import pallas as pl
from jax.experimental.pallas import tpu as pltpu
from jax.sharding import PartitionSpec as P

HD = 256
EPS = 1e-05
ROPE_BASE = 10000.0
NEG_FILL = -1e30
BF = jnp.bfloat16
F32 = jnp.float32
MIB = 1024 * 1024
VMEM_BYTES = 20 * MIB
COST = 1e12
HEADS_PER_STEP = 4


def dot(left, right):
    return jnp.dot(left, right, preferred_element_type=F32)


def dot_rows(left, right):
    return lax.dot_general(left, right, (((0,), (0,)), ((), ())), preferred_element_type=F32)


def dot_cols(left, right):
    return lax.dot_general(left, right, (((1,), (1,)), ((), ())), preferred_element_type=F32)


def inverse_rms(values):
    return lax.rsqrt(jnp.mean(values * values, axis=-1, keepdims=True) + EPS)


def back_norm(grad_out, unit_rows, inv_rms, gain):
    scaled = grad_out * gain
    return inv_rms * (scaled - unit_rows * jnp.mean(scaled * unit_rows, axis=-1, keepdims=True))


def turn(values, cosine, sine):
    half = HD // 2
    front, back = values[:, :half], values[:, half:]
    return front * cosine - back * sine, back * cosine + front * sine


def full_spec(shape):
    return pl.BlockSpec(tuple(shape), lambda *_: (0,) * len(shape))


def shape_of(shape, kind=BF):
    return jax.ShapeDtypeStruct(tuple(shape), kind)


def write_pieces(me, source, outs, layout):
    block = outs[0].shape[0] // len(layout[0])
    for out, rels in zip(outs, layout):
        for j, rel in enumerate(rels):
            out[j * block : (j + 1) * block, :] = source[block_rows(me ^ rel, block), :].astype(BF)


MICROS = {
    "front": 4, "query": 7, "attend": 13, "middle": 3, "ffn": 19, "mid_back": 3, "grad": 9, "ffn_grad": 22, "head_grad": 14, "pause": 3, "attend_back": 20,
    "latent_back": 3, "ffn_sum": 3, "spread": 3, "kv_split": 3, "key_back": 3, "join": 3, "input": 8, "shared": 3,
}


def run(kernel, scalars, inputs, outputs, grid=(1,), scratch=(), name=None, carried=(), vmem=VMEM_BYTES):
    n_in, n_scalars = len(inputs), len(scalars)
    moved = sum(a.size * a.dtype.itemsize for a, _ in inputs)

    def body(*refs):
        kernel(*refs[: n_scalars + n_in], *refs[n_scalars + n_in + len(carried) :])

    return pl.pallas_call(
        body,
        out_shape=[s for s, _ in outputs],
        grid_spec=pltpu.PrefetchScalarGridSpec(
            num_scalar_prefetch=n_scalars,
            grid=grid,
            in_specs=[s for _, s in inputs] + [pl.BlockSpec(memory_space=pl.ANY)] * len(carried),
            out_specs=[s for _, s in outputs],
            scratch_shapes=list(scratch),
        ),
        input_output_aliases={n_scalars + n_in + k: index for k, (index, _) in enumerate(carried)},
        compiler_params=pltpu.CompilerParams(
            dimension_semantics=("arbitrary",) * len(grid), vmem_limit_bytes=vmem
        ),
        cost_estimate=pl.CostEstimate(flops=int(MICROS[name] * COST), bytes_accessed=moved, transcendentals=0),
        name=name,
    )(*scalars, *[a for a, _ in inputs], *[a for _, a in carried])


def total_of(refs):
    total = refs[0][...].astype(F32)
    for ref in refs[1:]:
        total = total + ref[...].astype(F32)
    return total


def row_total(refs, r, n_rows, block):
    total = 0.0
    for ref in refs:
        at = r * (ref.shape[0] // n_rows)
        total = total + ref[at : at + block, :].astype(F32)
    return total


def block_rows(index, size):
    return pl.ds(pl.multiple_of(index * size, size), size)


def front_kernel(info, x_ref, gain_ref, w_ref, cos_ref, sin_ref, n_ref, kv_ref):
    x = x_ref[0].astype(F32)
    normed = (x * inverse_rms(x) * gain_ref[...]).astype(BF)
    n_ref[...] = normed
    kv = dot(normed, w_ref[...])
    front, back = turn(kv[:, :HD], cos_ref[0], sin_ref[0])
    kv_ref[:, : HD // 2] = front.astype(BF)
    kv_ref[:, HD // 2 : HD] = back.astype(BF)
    kv_ref[:, HD:] = kv[:, HD:].astype(BF)


def query_kernel(info, n_ref, wd_ref, gain_ref, wu_ref, cos_ref, sin_ref, ln_ref, ul_ref, il_ref, q_ref, held):
    latent = dot(n_ref[...], wd_ref[...])
    inv = inverse_rms(latent)
    unit = latent * inv
    normed = (unit * gain_ref[...]).astype(BF)
    ln_ref[...] = normed
    block = ul_ref.shape[0]
    held[...] = latent
    mine = held[block_rows(info[0], block), :]
    inv_mine = inverse_rms(mine)
    ul_ref[...] = mine * inv_mine
    il_ref[...] = jnp.broadcast_to(inv_mine, il_ref.shape)
    raw = dot(normed, wu_ref[...])
    cosine, sine = cos_ref[0], sin_ref[0]
    for h in range(raw.shape[1] // HD):
        front, back = turn(raw[:, h * HD : (h + 1) * HD], cosine, sine)
        q_ref[:, h * HD : h * HD + HD // 2] = front.astype(BF)
        q_ref[:, h * HD + HD // 2 : (h + 1) * HD] = back.astype(BF)


def starts_of(docs, row, places):
    end, start = 0, jnp.zeros_like(places)
    for d in range(docs.shape[1]):
        size = docs[row, d]
        end = end + size
        start = start + jnp.where(places >= end, size, 0)
    return start


def attend_kernel(row, order, layout, info, docs, q_ref, ka_ref, kb_ref, w_ref, ctx_ref, lse_ref, *rest):
    pieces, (acc, bias) = rest[: len(layout)], rest[len(layout) :]
    h = pl.program_id(0)
    length = q_ref.shape[0]
    half = len(order) // 2 * length
    me_tp, me_seq = info[0], info[1]

    @pl.when(h == 0)
    def _():
        places = me_seq * length + lax.broadcasted_iota(jnp.int32, (length, 1), 0)
        start = starts_of(docs, row, places)
        column = lax.broadcasted_iota(jnp.int32, (1, length), 1)
        for b, rel in enumerate(order):
            key = (me_seq ^ rel) * length + column
            allowed = (key >= start) & (key <= places)
            bias[:, b * length : (b + 1) * length] = jnp.where(allowed, 0.0, NEG_FILL)

    scale = jnp.asarray(HD ** (-0.5), BF)
    for i in range(q_ref.shape[1] // HD):
        cols = slice(i * HD, (i + 1) * HD)
        q = q_ref[:, cols] * scale
        sa = dot_cols(q, ka_ref[:, :HD]) + bias[:, :half]
        sb = dot_cols(q, kb_ref[:, :HD]) + bias[:, half:]
        peak = jnp.maximum(jnp.max(sa, axis=-1, keepdims=True), jnp.max(sb, axis=-1, keepdims=True))
        pa = jnp.exp(sa - peak)
        pb = jnp.exp(sb - peak)
        total = jnp.sum(pa, axis=-1, keepdims=True) + jnp.sum(pb, axis=-1, keepdims=True)
        out = dot(pa.astype(BF), ka_ref[:, HD:]) + dot(pb.astype(BF), kb_ref[:, HD:])
        out = (out / total).astype(BF)
        ctx_ref[:, cols] = out
        lse = jnp.broadcast_to(peak + jnp.log(total), (length, 128))
        lse_ref[i] = jnp.transpose(lse)[:1, :]
    part = dot(ctx_ref[...], w_ref[...])

    @pl.when(h == 0)
    def _():
        acc[...] = part

    @pl.when(h > 0)
    def _():
        acc[...] += part

    @pl.when(h == pl.num_programs(0) - 1)
    def _():
        write_pieces(me_tp, acc, pieces, layout)


def middle_kernel(info, *refs):
    parts, (x_ref, gain_ref, mid_ref, n2_ref) = refs[:-4], refs[-4:]
    mid = x_ref[0].astype(F32) + total_of(parts)
    mid_ref[...] = mid
    n2_ref[...] = (mid * inverse_rms(mid) * gain_ref[...]).astype(BF)


def place_pieces(me, pieces, out_ref, rels):
    per = len(rels) // len(pieces)
    block = pieces[0].shape[0] // per
    for i, rel in enumerate(rels):
        at = i % per * block
        out_ref[block_rows(me ^ rel, block), :] = pieces[i // per][at : at + block, :]


def ffn_kernel(n_parts, rels, layout, ff_layout, info, *refs):
    parts = refs[:n_parts]
    dy_ref, wg, wu, wd = refs[n_parts : n_parts + 4]
    outs = refs[n_parts + 4 :]
    n2_ref, hidden_ref = outs[:2]
    ff_refs, pieces = outs[2:4], outs[4 : 4 + len(layout)]
    acc = outs[4 + len(layout)]
    me = info[0]
    width = hidden_ref.shape[2]
    size = 512
    full, rest = width // size, width % size
    model = acc.shape[1]
    cut = min(1024, model)

    place_pieces(me, parts, n2_ref, rels)

    def hidden_part(c, at, count):
        here = pl.ds(at, count)
        gate = dot(n2_ref[...], wg[:, here])
        up = dot(n2_ref[...], wu[:, here])
        dhid = dot_cols(dy_ref[0], wd[here, :])
        sig = 1.0 / (1.0 + jnp.exp(-gate))
        swish = gate * sig
        hidden_ref[0, :, here] = (swish * up).astype(BF)
        hidden_ref[1, :, here] = (dhid * up * sig * (1.0 + gate * (1.0 - sig))).astype(BF)
        hidden_ref[2, :, here] = (dhid * swish).astype(BF)

    @pl.loop(0, full)
    def _(c):
        hidden_part(c, pl.multiple_of(c * size, size), size)

    if rest:
        hidden_part(full, full * size, rest)

    @pl.loop(0, model // cut)
    def _(n):
        here = pl.ds(pl.multiple_of(n * cut, cut), cut)
        acc[:, here] = dot_cols(hidden_ref[1], wg[here, :]) + dot_cols(hidden_ref[2], wu[here, :])

    write_pieces(me, acc, pieces, layout)

    @pl.loop(0, model // cut)
    def _(n):
        here = pl.ds(pl.multiple_of(n * cut, cut), cut)
        acc[:, here] = dot(hidden_ref[0], wd[:, here])

    write_pieces(me, acc, ff_refs, ff_layout)


def mid_back_kernel(info, *refs):
    parts, (mid_ref, dy_ref, gain_ref, low_ref) = refs[:-4], refs[-4:]
    d2 = total_of(parts)
    mid = mid_ref[...]
    inv = inverse_rms(mid)
    unit = mid * inv
    low_ref[...] = (dy_ref[0].astype(F32) + back_norm(d2, unit, inv, gain_ref[...])).astype(BF)


def attend_back_kernel(row, order, n_parts, rels, layout, info, docs, *refs):
    lows, refs = refs[:n_parts], refs[n_parts:]
    q_ref, ka_ref, kb_ref, lse_ref, wo_ref, wq_ref, cos_ref, sin_ref = refs[:8]
    low_ref, qlow_ref, keep_ref, send_ref = refs[8:12]
    pieces = refs[12:14]
    bias, dkv, lat = refs[14:]
    h = pl.program_id(0)
    length = q_ref.shape[0]
    half = len(order) // 2 * length
    me_tp, me_seq = info[0], info[1]
    scale = HD ** (-0.5)

    @pl.when(h == 0)
    def _():
        place_pieces(me_tp, lows, low_ref, rels)
        places = me_seq * length + lax.broadcasted_iota(jnp.int32, (1, length), 1)
        start = starts_of(docs, row, places)
        column = lax.broadcasted_iota(jnp.int32, (length, 1), 0)
        for b, rel in enumerate(order):
            key = (me_seq ^ rel) * length + column
            allowed = (key >= start) & (key <= places)
            bias[b * length : (b + 1) * length, :] = jnp.where(allowed, 0.0, NEG_FILL)

    dctx_all = dot_cols(low_ref[...], wo_ref[...]).astype(BF)
    for n in range(q_ref.shape[1] // HD):
        cols = slice(n * HD, (n + 1) * HD)
        q = q_ref[:, cols] * jnp.asarray(scale, BF)
        dctx = dctx_all[:, cols]
        lse = lse_ref[n]
        probs, dprobs = [], []
        delta = 0.0
        for i, kv_ref in enumerate((ka_ref, kb_ref)):
            scores = dot_cols(kv_ref[:, :HD], q) + bias[i * half : (i + 1) * half, :]
            prob = jnp.exp(scores - lse)
            dprob = dot_cols(kv_ref[:, HD:], dctx)
            delta = delta + jnp.sum(prob * dprob, axis=0, keepdims=True)
            probs.append(prob), dprobs.append(dprob)
        dq = 0.0
        for i, kv_ref in enumerate((ka_ref, kb_ref)):
            rows = slice(i * half, (i + 1) * half)
            dscore = (probs[i] * (dprobs[i] - delta)).astype(BF)
            dq = dq + dot_rows(dscore, kv_ref[:, :HD])
            dk = dot(dscore, q)
            dv = dot(probs[i].astype(BF), dctx)
            if n == 0:

                @pl.when(h == 0)
                def _():
                    dkv[rows, :HD] = dk
                    dkv[rows, HD:] = dv

                @pl.when(h > 0)
                def _():
                    dkv[rows, :HD] += dk
                    dkv[rows, HD:] += dv

            else:
                dkv[rows, :HD] += dk
                dkv[rows, HD:] += dv

        front, back = turn(dq * scale, cos_ref[0], -sin_ref[0])
        qlow_ref[:, n * HD : n * HD + HD // 2] = front.astype(BF)
        qlow_ref[:, n * HD + HD // 2 : (n + 1) * HD] = back.astype(BF)
    part = dot_cols(qlow_ref[...], wq_ref[...])

    @pl.when(h == 0)
    def _():
        lat[...] = part

    @pl.when(h > 0)
    def _():
        lat[...] += part

    @pl.when(h == pl.num_programs(0) - 1)
    def _():
        keep_ref[...] = dkv[:half, :].astype(BF)
        send_ref[...] = dkv[half:, :].astype(BF)
        write_pieces(me_tp, lat, pieces, layout)


def kv_split_kernel(n_rows, layout, info, *refs):
    pieces, held = refs[-1 - len(layout) : -1], refs[-1]
    count = (len(refs) - 1 - len(layout)) // n_rows
    rows = pieces[0].shape[0] // n_rows
    for r in range(n_rows):
        held[...] = total_of(refs[r * count : (r + 1) * count])
        outs = [piece.at[r * rows : (r + 1) * rows, :] for piece in pieces]
        write_pieces(info[0], held, outs, layout)


def latent_back_kernel(n_rows, info, *refs):
    units, invs = refs[-2 - 2 * n_rows : -2 - n_rows], refs[-2 - n_rows : -2]
    parts, (gain_ref, low_ref) = refs[: -2 - 2 * n_rows], refs[-2:]
    block = low_ref.shape[0] // n_rows
    for r in range(n_rows):
        rows = slice(r * block, (r + 1) * block)
        unit, grad = units[r][...], row_total(parts, r, n_rows, block)
        low_ref[rows, :] = back_norm(grad, unit, invs[r][:, :1], gain_ref[...]).astype(BF)


def key_back_kernel(n_rows, info, *refs):
    parts, (cos_ref, sin_ref, out_ref) = refs[:-3], refs[-3:]
    block = out_ref.shape[0] // n_rows
    for r in range(n_rows):
        rows = slice(r * block, (r + 1) * block)
        total = row_total(parts, r, n_rows, block)
        front, back = turn(total[:, :HD], cos_ref[r], -sin_ref[r])
        out_ref[rows, : HD // 2] = front.astype(BF)
        out_ref[rows, HD // 2 : HD] = back.astype(BF)
        out_ref[rows, HD:] = total[:, HD:].astype(BF)


def ffn_sum_kernel(n_rows, info, *refs):
    parts, mids, out_ref = refs[: -1 - n_rows], refs[-1 - n_rows : -1], refs[-1]
    block = out_ref.shape[0] // n_rows
    for r in range(n_rows):
        out_ref[r * block : (r + 1) * block, :] = (row_total(parts, r, n_rows, block) + mids[r][...]).astype(BF)


def spread_kernel(rels, info, *refs):
    pieces, out_ref = refs[:-1], refs[-1]
    n_rows, per = out_ref.shape[0], len(rels) // len(pieces)
    block = out_ref.shape[1] // len(rels)
    for i, rel in enumerate(rels):
        for row in range(n_rows):
            at = (i % per * n_rows + row) * block
            out_ref[row, block_rows(info[0] ^ rel, block), :] = pieces[i // per][at : at + block, :]


def join_kernel(n_rows, rels, count, info, *refs):
    pieces, all_ref = refs[:count], refs[count]
    me, n_tp = info[0], len(rels)
    per = n_tp // count
    block = pieces[0].shape[0] // (n_rows * per)
    for i, rel in enumerate(rels):
        for r in range(n_rows):
            at = (i % per * n_rows + r) * block
            all_ref[block_rows(r * n_tp + (me ^ rel), block), :] = pieces[i // per][at : at + block, :]
    if len(refs) > count + 1:
        part_ref = refs[count + 1]
        part_ref[...] = all_ref[:, block_rows(me, part_ref.shape[1])]


def input_kernel(info, lat_ref, kv_ref, x_ref, wd_ref, wkv_ref, low_ref, gain_ref, out_ref):
    dn = dot_cols(lat_ref[...], wd_ref[...]) + dot_cols(kv_ref[...], wkv_ref[...])
    x = x_ref[0].astype(F32)
    inv = inverse_rms(x)
    unit = x * inv
    out_ref[0] = (low_ref[...].astype(F32) + back_norm(dn, unit, inv, gain_ref[...])).astype(BF)


def grad_kernel(table, *refs):
    count = (len(refs) - 2) // 2
    keep_ref, send_ref = refs[2 * count :]

    def load(ref):
        value = ref[...]
        return value.reshape(-1, value.shape[-1])

    total = dot_rows(load(refs[0]), load(refs[count]))
    for i in range(1, count):
        total = total + dot_rows(load(refs[i]), load(refs[count + i]))
    total = total.astype(BF)
    i, half = pl.program_id(0), pl.num_programs(0) // 2

    @pl.when(i < half)
    def _():
        keep_ref[...] = total

    @pl.when(i >= half)
    def _():
        send_ref[...] = total


def ffn_grad_kernel(info, hidden_ref, n2_ref, dy_ref, out_ref):
    dy = dy_ref[...]
    dy = dy.reshape(-1, dy.shape[-1])
    width = hidden_ref.shape[2]
    out_ref[:, :width] = dot_rows(dy, hidden_ref[0]).astype(BF)
    out_ref[:, width : 2 * width] = dot_rows(n2_ref[...], hidden_ref[1]).astype(BF)
    out_ref[:, 2 * width :] = dot_rows(n2_ref[...], hidden_ref[2]).astype(BF)


def head_grad_kernel(info, context_ref, low_ref, latent_ref, query_ref, out_ref):
    rows, width = context_ref.shape[1], low_ref.shape[1]
    out_ref[:rows, :] = dot_rows(context_ref[...], low_ref[...]).astype(BF)
    count = latent_ref.shape[1]
    part = dot_rows(latent_ref[...], query_ref[...]).astype(BF)
    for i in range(part.shape[1] // width):
        out_ref[rows + i * count : rows + (i + 1) * count, :] = part[:, i * width : (i + 1) * width]


def pause_kernel(info, out_ref):
    for i in range(out_ref.shape[0]):
        out_ref[i] = info[i]


def shared_kernel(n_tp, info, *refs):
    for pieces, out_ref in ((refs[:n_tp], refs[2 * n_tp]), (refs[n_tp : 2 * n_tp], refs[2 * n_tp + 1])):
        for r in range(n_tp):
            width = pieces[r].shape[1]
            out_ref[:, block_rows(info[0] ^ r, width)] = pieces[r][...].astype(F32)


def build(n_seq, n_tp):
    seq_bits = n_seq.bit_length() - 1
    tp_bits = n_tp.bit_length() - 1

    def swap(value, axis, mask):
        count = n_seq if axis == "seq" else n_tp
        return lax.ppermute(value, axis, [(i, i ^ mask) for i in range(count)])

    def spread(bits):
        order = [0]
        for bit in bits:
            order = order + [o | (1 << bit) for o in order]
        return order

    upward = list(range(1, seq_bits))
    routes = (upward + [0], upward[::-1] + [0])
    tp_route = list(reversed(range(tp_bits)))
    tp_rels = spread(tp_route)
    halves = [tp_rels[: n_tp // 2], tp_rels[n_tp // 2 :]]
    singles = [[r] for r in range(n_tp)]
    layouts = [singles, halves]

    def gather(block):
        return [block] + [swap(block, "tp", r) for r in range(1, n_tp)]

    def shards(
        layer_in, attn_gain, query_down, latent_gain, query_up, key_value, attn_out,
        ffn_gain, gate_proj, up_proj, down_proj, out_grad, doc_lengths,
    ):
        n_rows, length, model_dim = layer_in.shape
        lat_dim, q_width = query_up.shape
        ff_dim = gate_proj.shape[1]
        heads = q_width // HD
        block = length // n_tp
        half_keys = n_seq // 2 * length
        rows = range(n_rows)
        seq_me, tp_me = lax.axis_index("seq"), lax.axis_index("tp")
        state = [jnp.stack([tp_me, seq_me, jnp.zeros_like(tp_me)]).astype(jnp.int32)]
        last, due = [], []

        def wait(*arrays):
            due.extend(arrays)

        def pause():
            state[0] = step(
                pause_kernel, [], [(shape_of((3,), jnp.int32), pl.BlockSpec(memory_space=pltpu.SMEM))], name="pause",
            )[0]

        def after(value):
            ready = last[-1:] + due
            due.clear()
            return lax.optimization_barrier((value, *ready))[0] if ready else value

        def step(kernel, inputs, outputs, table=None, docs=False, **kw):
            scalars = (after(state[0] if table is None else table),) + ((doc_lengths,) if docs else ())
            out = run(kernel, scalars, inputs, outputs, **kw)
            last.append(min(out, key=lambda o: o.size))
            return out

        def total(values, kind):
            out = after(values[-1][0])[values[-1][1]].astype(F32)
            for array, index in values[:-1]:
                out = out + array[index].astype(F32)
            out = out.astype(kind)
            last.append(out)
            return out

        def add(parts, rows, at, kind):
            return total([(p, slice(at * rows, (at + 1) * rows)) for p in parts], kind)

        def halve(parts, rows, axis, bit):
            half = rows // 2
            return parts + [swap(add(parts, half, 1, BF), axis, 1 << bit)], half

        def halve_all(parts, rows, axis, bits):
            for bit in reversed(bits):
                parts, rows = halve(parts, rows, axis, bit)
            return parts, rows

        places = seq_me * length + jnp.arange(length, dtype=jnp.int32)
        ends = jnp.cumsum(doc_lengths, axis=1)
        passed = places[None, :, None] >= ends[:, None, :]
        inner = places[None, :] - jnp.sum(jnp.where(passed, doc_lengths[:, None, :], 0), axis=-1)
        frequency = ROPE_BASE ** (-jnp.arange(HD // 2, dtype=F32) / (HD // 2))
        angles = inner.astype(F32)[:, :, None] * frequency
        cosine, sine = jnp.cos(angles), jnp.sin(angles)
        gain_row = lambda gain: (gain.reshape(1, -1), full_spec((1, gain.shape[0])))

        def whole(array):
            return array, full_spec(array.shape)

        def first(array, count):
            return array, full_spec((count, array.shape[1]))

        def row_of(array, r):
            return array, pl.BlockSpec((1,) + array.shape[1:], lambda *_: (r, 0, 0))

        def own_of(array, r):
            shape = (1, block, array.shape[2])
            return array, pl.BlockSpec(shape, lambda i, info, *_: (r, info[0], 0))

        def new(shape, kind=BF):
            return shape_of(shape, kind), full_spec(shape)

        per_step = min(HEADS_PER_STEP, heads)
        group = per_step * HD

        def head_cols(array):
            return array, pl.BlockSpec((array.shape[0], group), lambda h, *_: (0, h))

        def head_rows(array):
            return array, pl.BlockSpec((group, array.shape[1]), lambda h, *_: (h, 0))

        def row_pieces(r, width):
            rows_out = n_tp // 2 * block
            spec = pl.BlockSpec((rows_out, width), lambda *_: (r, 0))
            return [(shape_of((n_rows * rows_out, width)), spec)] * 2

        def pieces_of(layout, width):
            return [new((len(rels) * block, width)) for rels in layout]

        on_chip = pl.BlockSpec(memory_space=pltpu.VMEM)
        weights = [pltpu.with_memory_space_constraint(w, pltpu.VMEM) for w in (gate_proj, up_proj, down_proj)]

        def rows_of(width, r, spec=None):
            return shape_of((n_rows * length, width)), spec or pl.BlockSpec((length, width), lambda *_: (r, 0))

        def row_block(array, r):
            return array, pl.BlockSpec((length, array.shape[1]), lambda *_: (r, 0))

        def going(held, *pairs):
            return [(index, held[key]) for index, key in pairs] if held else []

        def front(r, held):
            return step(
                front_kernel,
                [row_of(layer_in, r), gain_row(attn_gain), whole(key_value), row_of(cosine, r), row_of(sine, r)],
                [rows_of(model_dim, r), new((length, 2 * HD))], name="front", carried=going(held, (0, 0)),
            )

        def query(r, held):
            return step(
                query_kernel,
                [row_block(normed, r), whole(query_down), gain_row(latent_gain), whole(query_up),
                 row_of(cosine, r), row_of(sine, r)],
                [rows_of(lat_dim, r), new((block, lat_dim), F32), new((block, 128), F32), new((length, q_width))],
                scratch=[pltpu.VMEM((length, lat_dim), F32)], name="query", carried=going(held, (0, 0)),
            )

        def attend(r, held):
            return step(
                functools.partial(attend_kernel, r, spread(routes[(r + 1) % 2]), layouts[r]),
                [head_cols(queries[r]), whole(near[r]), whole(far[r]), head_rows(attn_out)],
                [
                    rows_of(q_width, r, pl.BlockSpec((length, group), lambda h, *_: (r, h))),
                    (shape_of((heads, 1, length), F32), pl.BlockSpec((per_step, 1, length), lambda h, *_: (h, 0, 0))),
                ] + pieces_of(layouts[r], model_dim),
                docs=True, grid=(heads // per_step,),
                scratch=[pltpu.VMEM((length, model_dim), F32), pltpu.VMEM((length, 2 * half_keys), F32)],
                name="attend", vmem=min(58, 26 * half_keys // 1024) * MIB, carried=going(held, (0, 0)),
            )

        def mid_step(r, parts):
            return step(
                middle_kernel, [first(p, block) for p in parts] + [own_of(layer_in, r), gain_row(ffn_gain)],
                [new((block, model_dim), F32), new((block, model_dim))], name="middle", vmem=24 * MIB,
            )

        def ffn(r, held):
            return step(
                functools.partial(ffn_kernel, len(normed2[r]), range(n_tp), layouts[r], halves),
                [whole(p) for p in normed2[r]] + [row_of(out_grad, r),
                 (weights[0], on_chip), (weights[1], on_chip), (weights[2], on_chip)],
                [rows_of(model_dim, r),
                 (shape_of((3, n_rows * length, ff_dim)), pl.BlockSpec((3, length, ff_dim), lambda *_: (0, r, 0)))]
                + row_pieces(r, model_dim) + pieces_of(layouts[r], model_dim),
                scratch=[pltpu.VMEM((length, model_dim), F32)], vmem=24 * MIB,
                name="ffn", carried=going(held, *[(i, i) for i in range(4)]),
            )

        def mid_back(r, parts):
            return step(
                mid_back_kernel,
                [first(p, block) for p in parts] + [whole(middle[r]), own_of(out_grad, r), gain_row(ffn_gain)],
                [new((block, model_dim))], name="mid_back",
            )[0]

        def attend_back(r, held):
            return step(
                functools.partial(attend_back_kernel, r, spread(routes[(r + 1) % 2]), len(mid_low[r]), range(n_tp), halves),
                [whole(p) for p in mid_low[r]]
                + [head_cols(queries[r]), whole(near[r]), whole(far[r]),
                   (lse[r], pl.BlockSpec((per_step, 1, length), lambda h, *_: (h, 0, 0))),
                   head_rows(attn_out), head_cols(query_up), row_of(cosine, r), row_of(sine, r)],
                [rows_of(model_dim, r), rows_of(q_width, r, pl.BlockSpec((length, group), lambda h, *_: (r, h))),
                 new((half_keys, 2 * HD)), new((half_keys, 2 * HD))] + row_pieces(r, lat_dim),
                docs=True, grid=(heads // per_step,),
                scratch=[pltpu.VMEM((2 * half_keys, length), F32), pltpu.VMEM((2 * half_keys, 2 * HD), F32),
                         pltpu.VMEM((length, lat_dim), F32)],
                name="attend_back", vmem=min(58, 32 * half_keys // 1024) * MIB, carried=going(held, (0, 0), (1, 1), (4, 4), (5, 5)),
            )

        def halve_rows(parts, count):
            half = count // 2 * block
            width = parts[0].shape[1]
            values = [(p.reshape(n_rows, -1, width), (slice(None), slice(half, 2 * half))) for p in parts]
            away = total(values, BF).reshape(n_rows * half, width)
            last[-1] = away
            return parts + [swap(away, "tp", 1 << tp_route[count.bit_length() - 2])]

        def joined_pair(held):
            pair = jnp.concatenate([after(held[0]), held[1]], axis=0)
            last.append(pair)
            return pair

        def gather_start(piece):
            return piece, swap(piece, "tp", 1 << tp_route[0])

        def gather_end(held):
            for bit in tp_route[1:]:
                held = joined_pair(held)
                held = held, swap(held, "tp", 1 << bit)
            return list(held)

        def both(array):
            return [array, swap(array, "seq", 1)]

        def weight_grad(acts, deltas, by_cols, route):
            acts, deltas = [[a if isinstance(a, tuple) else (a, None) for a in pair] for pair in (acts, deltas)]
            bits = routes[route][:-1]
            order = [o for o in spread(bits)]
            count = n_seq // 2
            size = (deltas if by_cols else acts)[0][0].shape[-1] // n_seq
            if size % 128:
                flat = [jnp.concatenate([a for a, _ in pair], axis=0) for pair in (acts, deltas)]
                full = dot_rows(*flat).astype(BF)
                blocks = jnp.take(full.reshape(n_seq, -1, full.shape[1]), jnp.stack([seq_me ^ o for o in order]), axis=0)
                parts, left = halve([blocks.reshape(-1, full.shape[1])], count * size, "seq", bits[-1])
            else:

                def operands(arrays, cut):
                    out = []
                    for array, which in arrays:
                        lead = array.shape[:-1]
                        if which is not None:
                            out.append((array, pl.BlockSpec((1,) + array.shape[1:], lambda i, t: (which, 0, 0))))
                        elif cut:
                            zeros = (0,) * len(lead)
                            out.append((array, pl.BlockSpec(lead + (size,), lambda i, t, z=zeros: z + (t[i],))))
                        else:
                            out.append(whole(array))
                    return out

                shape = (acts[0][0].shape[-1], size) if by_cols else (size, deltas[0][0].shape[-1])
                half = count // 2
                part = shape_of((half * shape[0], shape[1]))
                keep, away = step(
                    grad_kernel, operands(acts, not by_cols) + operands(deltas, by_cols),
                    [(part, pl.BlockSpec(shape, lambda i, t: (jnp.minimum(i, half - 1), 0))),
                     (part, pl.BlockSpec(shape, lambda i, t: (jnp.maximum(i - half, 0), 0)))],
                    table=jnp.stack([seq_me ^ o for o in order]).astype(jnp.int32), grid=(count,), name="grad",
                )
                parts, left = [keep, swap(away, "seq", 1 << bits[-1])], keep.shape[0]
            yield parts[-1]
            parts, left = halve_all(parts, left, "seq", bits[:-1])
            yield parts[-1]
            yield add(parts, left, 0, F32)

        held, out = [], None
        for r in rows:
            out = front(r, out)
            held.append([out[1], swap(out[1], "seq", 1 << routes[(r + 1) % 2][0])])
        normed = out[0]
        normed_both = both(normed)
        unit_lat, inv_lat, queries = [], [], []

        def widen(r, bit):
            pair = joined_pair(held[r])
            held[r] = [pair, swap(pair, "seq", 1 << bit)]

        for bit in range(1, seq_bits - 1):
            for r in rows:
                widen(r, routes[(r + 1) % 2][bit])
        out = None
        for r in rows:
            out = query(r, out)
            unit_lat.append(out[1]), inv_lat.append(out[2]), queries.append(out[3])
        wait(normed_both[1])
        latent_norm = out[0]
        near, far = [None] * n_rows, [None] * n_rows
        lse, part1, out = [], [], None

        def sent_over(pieces):
            if len(pieces) == 2:
                return [pieces[0], swap(pieces[1], "tp", 1)]
            return [pieces[0]] + [swap(pieces[r], "tp", r) for r in range(1, n_tp)]

        for r in rows:
            widen(r, 0)
            near[r], far[r] = held[r]
            out = attend(r, out)
            lse.append(out[1])
            part1.append(sent_over(out[2:]))
        context = out[0]
        sent = n_tp // 2 * block
        middle, normed2 = [], []
        mid, n2 = mid_step(0, part1[0])
        middle.append(mid)
        normed2.append(gather(n2))
        part1[1], _ = halve_all(part1[1], sent, "tp", tp_route[:-1])
        wait(*normed2[0])
        mid, n2 = mid_step(1, part1[1])
        middle.append(mid)
        normed2.append(gather(n2))

        part2, out = [], None
        for r in rows:
            out = ffn(r, out)
            part2.append(sent_over(out[4:]))
        n2_all, hidden, ffn_keep, ffn_send = out[:4]
        mid_low = [gather(mid_back(0, part2[0]))]
        wide = model_dim // n_seq

        def over_seq(part):
            return lax.psum_scatter(part, "seq", scatter_dimension=0, tiled=True)

        ffn_part = step(
            ffn_grad_kernel,
            [whole(hidden), (n2_all, pl.BlockSpec((n_rows * length, wide), lambda i, *_: (0, i))),
             (out_grad, pl.BlockSpec((n_rows, length, wide), lambda i, *_: (0, 0, i)))],
            [(shape_of((model_dim, 3 * ff_dim)), pl.BlockSpec((wide, 3 * ff_dim), lambda i, *_: (i, 0)))],
            grid=(n_seq,), name="ffn_grad",
        )[0]
        ffn_sum = over_seq(ffn_part)
        part2[1], _ = halve_all(part2[1], sent, "tp", tp_route[:-1])
        wait(*mid_low[0])
        mid_low.append(gather(mid_back(1, part2[1])))

        kv_parts = []
        ffn_parts = [ffn_keep, swap(after(ffn_send), "tp", 1)]
        out = attend_back(0, None)
        kv_parts.append(([out[2], swap(out[3], "seq", 1)], half_keys))
        pause()
        kv_parts[0] = halve(*kv_parts[0], "seq", routes[1][-2])
        wait(*mid_low[1])
        out = attend_back(1, out)
        low_all, query_low = out[:2]
        kv_parts.append(([out[2], swap(out[3], "seq", 1)], half_keys))
        lat_parts = [out[4], swap(out[5], "tp", 1)]
        pause()
        crossed = seq_bits == 3
        if crossed:
            keep, got = kv_parts[1][0]
            pairs = lambda p: p.reshape(2, 2, length, -1)
            away = total([(pairs(p), (slice(None), 1)) for p in (keep, got)], BF).reshape(2 * length, -1)
            last[-1] = away
            kv_parts[1] = [keep, got, swap(away, "seq", 2)]
        else:
            kv_parts[1] = halve(*kv_parts[1], "seq", routes[0][-2])
        pause()
        for count in [n_tp >> i for i in range(1, tp_bits)]:
            ffn_parts = halve_rows(ffn_parts, count)
        kv_parts[0] = halve_all(*kv_parts[0], "seq", routes[1][:-2])
        own_lat = lat_dim // n_seq
        pieces = q_width // wide
        rows_out = q_width + pieces * own_lat
        if own_lat % 128:
            out_blocks = dot_rows(context, low_all).reshape(q_width, n_seq, wide).transpose(1, 0, 2)
            query_blocks = dot_rows(latent_norm, query_low).reshape(n_seq, own_lat, pieces, wide).transpose(0, 2, 1, 3)
            head_part = jnp.concatenate([out_blocks, query_blocks.reshape(n_seq, -1, wide)], axis=1)
            head_part = head_part.astype(BF).reshape(-1, wide)
        else:
            head_part = step(
                head_grad_kernel,
                [whole(context), (low_all, pl.BlockSpec((n_rows * length, wide), lambda i, *_: (0, i))),
                 (latent_norm, pl.BlockSpec((n_rows * length, own_lat), lambda i, *_: (0, i))), whole(query_low)],
                [(shape_of((n_seq * rows_out, wide)), pl.BlockSpec((rows_out, wide), lambda i, *_: (i, 0)))],
                grid=(n_seq,), name="head_grad",
            )[0]
        for count in [n_tp >> i for i in range(1, tp_bits)]:
            lat_parts = halve_rows(lat_parts, count)
        pause()
        if crossed:
            keep, got, more = kv_parts[1]
            values = [(pairs(p), (1, 0)) for p in (keep, got)] + [(more, slice(length, None))]
            kv_parts[1] = [keep, got, more, swap(total(values, BF), "seq", 4)], length
        else:
            kv_parts[1] = halve_all(*kv_parts[1], "seq", routes[0][:-2])
        lat_low = step(
            functools.partial(latent_back_kernel, n_rows),
            [whole(p) for p in lat_parts] + [whole(u) for u in unit_lat] + [whole(i) for i in inv_lat]
            + [gain_row(latent_gain)],
            [new((n_rows * block, lat_dim))], name="latent_back",
        )[0]
        lat_blocks = gather_start(lat_low)
        kv_sum = step(
            functools.partial(kv_split_kernel, n_rows, singles),
            [first(p, length) for parts, _ in kv_parts for p in parts],
            [new((n_rows * block, 2 * HD))] * n_tp,
            scratch=[pltpu.VMEM((length, 2 * HD), F32)], name="kv_split",
        )
        kv_sum = sent_over(kv_sum)
        ffn_own = step(
            functools.partial(ffn_sum_kernel, n_rows), [whole(p) for p in ffn_parts] + [whole(m) for m in middle],
            [new((n_rows * block, model_dim))], name="ffn_sum",
        )[0]
        head_sum = over_seq(after(head_part))
        own_dim = model_dim // n_seq

        def own_part(array, count):
            return lax.dynamic_slice_in_dim(array, seq_me * count, count, 0)

        def row_sums(weight, grad):
            return jnp.sum(own_part(weight, grad.shape[0]).astype(F32) * grad, axis=1)

        own_rows = pl.BlockSpec((n_rows, block, HD // 2), lambda i, info, *_: (0, info[0], 0))
        kv_low = step(
            functools.partial(key_back_kernel, n_rows),
            [whole(p) for p in kv_sum] + [(cosine, own_rows), (sine, own_rows)],
            [new((n_rows * block, 2 * HD))], name="key_back",
        )[0]
        kv_blocks = gather(kv_low)
        lat_blocks = gather_end(lat_blocks)
        ffn_blocks = gather_start(after(ffn_own))
        pause()
        gate_up = total([(ffn_sum, (slice(None), slice(ff_dim, None)))], F32)
        gate_grad, up_grad = gate_up[:, :ff_dim], gate_up[:, ff_dim:]
        ffn_rows = row_sums(gate_proj, gate_grad) + row_sums(up_proj, up_grad)
        last.append(ffn_rows)

        def join(blocks, rels):
            width = blocks[0].shape[1]
            cols = width // n_tp
            count = n_rows * length
            out = step(
                functools.partial(join_kernel, n_rows, rels, len(blocks)), [whole(b) for b in blocks],
                [new((count, width))] + ([] if cols % 128 else [new((count, cols))]), name="join",
            )
            if cols % 128:
                return out[0], lax.dynamic_slice_in_dim(out[0], tp_me * cols, cols, 1)
            return out

        lat_all, lat_part = join(lat_blocks, tp_rels)
        lat_part_both = both(lat_part)
        kv_all, kv_part = join(kv_blocks, range(n_tp))
        kv_part_both = both(kv_part)
        ffn_blocks = gather_end(ffn_blocks)
        grad_lat = weight_grad(normed_both, lat_part_both, False, 0)
        lat_2 = next(grad_lat)
        grad_kv = weight_grad(normed_both, kv_part_both, False, 1)
        kv_2 = next(grad_kv)

        def input_step(r, held):
            return step(
                input_kernel,
                [row_block(lat_all, r), row_block(kv_all, r), row_of(layer_in, r), whole(query_down), whole(key_value),
                 row_block(low_all, r), gain_row(attn_gain)],
                [(shape_of(layer_in.shape), pl.BlockSpec((1, length, model_dim), lambda *_: (r, 0, 0)))],
                name="input", carried=going(held, (0, 0)),
            )

        out = input_step(0, None)
        lat_3 = next(grad_lat)
        kv_3 = next(grad_kv)
        input_grad = input_step(1, out)[0]
        lat_sum = next(grad_lat)
        shared_lat = gather(lat_sum.astype(BF))
        pause()
        kv_grad_sum = next(grad_kv)
        head_grads = total([(head_sum, slice(None))], F32)
        out_weight_grad = head_grads[:q_width]
        query_up_grad = head_grads[q_width:].reshape(pieces, own_lat, wide).transpose(1, 0, 2).reshape(own_lat, q_width)

        def own_columns(weight):
            cols = weight.shape[1] // n_tp
            return lax.dynamic_slice_in_dim(weight, tp_me * cols, cols, 1)

        tp_sums = jnp.concatenate(
            [
                ffn_rows,
                row_sums(own_columns(query_down), lat_sum) + row_sums(own_columns(key_value), kv_grad_sum),
                row_sums(query_up, query_up_grad),
            ]
        )
        kv_rows = jnp.concatenate([kv_grad_sum, tp_sums.reshape(-1, kv_grad_sum.shape[1])], axis=0).astype(BF)
        wait(*shared_lat)
        shared_kv = gather(after(kv_rows))
        pause()
        down_grad = total([(ffn_sum, (slice(None), slice(0, ff_dim)))], F32).T
        layer_out = step(
            functools.partial(spread_kernel, tp_rels), [whole(p) for p in ffn_blocks], [new(layer_in.shape)],
            name="spread",
        )[0]
        if kv_part.shape[1] % 128:

            def side_by_side(pieces):
                cols = pieces[0].shape[1]
                blocks = jnp.take(jnp.stack(pieces)[:, :own_dim], jnp.stack([tp_me ^ r for r in range(n_tp)]), axis=0)
                return blocks.astype(F32).transpose(1, 0, 2).reshape(own_dim, n_tp * cols)

            down_q, kv_grad = side_by_side(shared_lat), side_by_side(shared_kv)
        else:
            down_q, kv_grad = step(
                functools.partial(shared_kernel, n_tp),
                [whole(p) for p in shared_lat] + [first(p, own_dim) for p in shared_kv],
                [new((own_dim, lat_dim), F32), new((own_dim, 2 * HD), F32)], name="shared",
            )
        tp_sums = sum(p[own_dim:].astype(F32) for p in shared_kv).reshape(-1)
        ffn_gain_grad = tp_sums[:own_dim] / own_part(ffn_gain, own_dim)
        attn_gain_grad = tp_sums[own_dim : 2 * own_dim] / own_part(attn_gain, own_dim)
        latent_gain_grad = tp_sums[2 * own_dim :] / own_part(latent_gain, own_lat)
        return (
            layer_out, input_grad, attn_gain_grad, down_q, latent_gain_grad, query_up_grad,
            kv_grad, out_weight_grad.reshape(q_width, own_dim), ffn_gain_grad, gate_grad, up_grad,
            down_grad.reshape(ff_dim, own_dim),
        )

    return shards


def solution(mesh):
    return jax.shard_map(
        build(mesh.shape["seq"], mesh.shape["tp"]),
        mesh=mesh,
        in_specs=(
            P(None, "seq", None), P(), P(), P(), P(None, "tp"), P(), P("tp", None), P(),
            P(None, "tp"), P(None, "tp"), P("tp", None), P(None, "seq", None), P(),
        ),
        out_specs=(
            P(None, "seq", None), P(None, "seq", None), P("seq"), P("seq", None), P("seq"),
            P("seq", "tp"), P("seq", None), P("tp", "seq"), P("seq"), P("seq", "tp"),
            P("seq", "tp"), P("tp", "seq"),
        ),
        check_vma=False,
    )
```

```python
import functools

import jax
import jax.numpy as jnp
from jax import lax
from jax.experimental import pallas as pl
from jax.experimental.pallas import tpu as pltpu
from jax.sharding import PartitionSpec as P

HD = 256
EPS = 1e-05
ROPE_BASE = 10000.0
NEG_FILL = -1e30
BF = jnp.bfloat16
F32 = jnp.float32
MIB = 1024 * 1024
VMEM_BYTES = 20 * MIB
COST = 1e12
HEADS_PER_STEP = 4


def dot(left, right):
    return jnp.dot(left, right, preferred_element_type=F32)


def dot_rows(left, right):
    return lax.dot_general(left, right, (((0,), (0,)), ((), ())), preferred_element_type=F32)


def dot_cols(left, right):
    return lax.dot_general(left, right, (((1,), (1,)), ((), ())), preferred_element_type=F32)


def inverse_rms(values):
    return lax.rsqrt(jnp.mean(values * values, axis=-1, keepdims=True) + EPS)


def back_norm(grad_out, unit_rows, inv_rms, gain):
    scaled = grad_out * gain
    return inv_rms * (scaled - unit_rows * jnp.mean(scaled * unit_rows, axis=-1, keepdims=True))


def turn(values, cosine, sine):
    half = HD // 2
    front, back = values[:, :half], values[:, half:]
    return front * cosine - back * sine, back * cosine + front * sine


def full_spec(shape):
    return pl.BlockSpec(tuple(shape), lambda *_: (0,) * len(shape))


def shape_of(shape, kind=BF):
    return jax.ShapeDtypeStruct(tuple(shape), kind)


def write_pieces(me, source, outs, layout):
    block = outs[0].shape[0] // len(layout[0])
    for out, rels in zip(outs, layout):
        for j, rel in enumerate(rels):
            out[j * block : (j + 1) * block, :] = source[block_rows(me ^ rel, block), :].astype(BF)


MICROS = {
    "front": 4, "query": 7, "attend": 13, "middle": 3, "ffn": 19, "mid_back": 3, "grad": 9, "ffn_grad": 22, "head_grad": 14, "pause": 3, "attend_back": 20,
    "latent_back": 3, "ffn_sum": 3, "spread": 3, "kv_split": 3, "key_back": 3, "join": 3, "input": 8, "shared": 3,
}


def run(kernel, scalars, inputs, outputs, grid=(1,), scratch=(), name=None, carried=(), vmem=VMEM_BYTES):
    n_in, n_scalars = len(inputs), len(scalars)
    moved = sum(a.size * a.dtype.itemsize for a, _ in inputs)

    def body(*refs):
        kernel(*refs[: n_scalars + n_in], *refs[n_scalars + n_in + len(carried) :])

    return pl.pallas_call(
        body,
        out_shape=[s for s, _ in outputs],
        grid_spec=pltpu.PrefetchScalarGridSpec(
            num_scalar_prefetch=n_scalars,
            grid=grid,
            in_specs=[s for _, s in inputs] + [pl.BlockSpec(memory_space=pl.ANY)] * len(carried),
            out_specs=[s for _, s in outputs],
            scratch_shapes=list(scratch),
        ),
        input_output_aliases={n_scalars + n_in + k: index for k, (index, _) in enumerate(carried)},
        compiler_params=pltpu.CompilerParams(
            dimension_semantics=("arbitrary",) * len(grid), vmem_limit_bytes=vmem
        ),
        cost_estimate=pl.CostEstimate(flops=int(MICROS[name] * COST), bytes_accessed=moved, transcendentals=0),
        name=name,
    )(*scalars, *[a for a, _ in inputs], *[a for _, a in carried])


def total_of(refs):
    total = refs[0][...].astype(F32)
    for ref in refs[1:]:
        total = total + ref[...].astype(F32)
    return total


def row_total(refs, r, n_rows, block):
    total = 0.0
    for ref in refs:
        at = r * (ref.shape[0] // n_rows)
        total = total + ref[at : at + block, :].astype(F32)
    return total


def block_rows(index, size):
    return pl.ds(pl.multiple_of(index * size, size), size)


def front_kernel(info, x_ref, gain_ref, w_ref, cos_ref, sin_ref, n_ref, kv_ref):
    x = x_ref[0].astype(F32)
    normed = (x * inverse_rms(x) * gain_ref[...]).astype(BF)
    n_ref[...] = normed
    kv = dot(normed, w_ref[...])
    front, back = turn(kv[:, :HD], cos_ref[0], sin_ref[0])
    kv_ref[:, : HD // 2] = front.astype(BF)
    kv_ref[:, HD // 2 : HD] = back.astype(BF)
    kv_ref[:, HD:] = kv[:, HD:].astype(BF)


def query_kernel(info, n_ref, wd_ref, gain_ref, wu_ref, cos_ref, sin_ref, ln_ref, ul_ref, il_ref, q_ref, held):
    latent = dot(n_ref[...], wd_ref[...])
    inv = inverse_rms(latent)
    unit = latent * inv
    normed = (unit * gain_ref[...]).astype(BF)
    ln_ref[...] = normed
    block = ul_ref.shape[0]
    held[...] = latent
    mine = held[block_rows(info[0], block), :]
    inv_mine = inverse_rms(mine)
    ul_ref[...] = mine * inv_mine
    il_ref[...] = jnp.broadcast_to(inv_mine, il_ref.shape)
    raw = dot(normed, wu_ref[...])
    cosine, sine = cos_ref[0], sin_ref[0]
    for h in range(raw.shape[1] // HD):
        front, back = turn(raw[:, h * HD : (h + 1) * HD], cosine, sine)
        q_ref[:, h * HD : h * HD + HD // 2] = front.astype(BF)
        q_ref[:, h * HD + HD // 2 : (h + 1) * HD] = back.astype(BF)


def starts_of(docs, row, places):
    end, start = 0, jnp.zeros_like(places)
    for d in range(docs.shape[1]):
        size = docs[row, d]
        end = end + size
        start = start + jnp.where(places >= end, size, 0)
    return start


def attend_kernel(row, order, layout, info, docs, q_ref, ka_ref, kb_ref, w_ref, ctx_ref, lse_ref, *rest):
    pieces, (acc, bias) = rest[: len(layout)], rest[len(layout) :]
    h = pl.program_id(0)
    length = q_ref.shape[0]
    half = len(order) // 2 * length
    me_tp, me_seq = info[0], info[1]

    @pl.when(h == 0)
    def _():
        places = me_seq * length + lax.broadcasted_iota(jnp.int32, (length, 1), 0)
        start = starts_of(docs, row, places)
        column = lax.broadcasted_iota(jnp.int32, (1, length), 1)
        for b, rel in enumerate(order):
            key = (me_seq ^ rel) * length + column
            allowed = (key >= start) & (key <= places)
            bias[:, b * length : (b + 1) * length] = jnp.where(allowed, 0.0, NEG_FILL)

    scale = jnp.asarray(HD ** (-0.5), BF)
    for i in range(q_ref.shape[1] // HD):
        cols = slice(i * HD, (i + 1) * HD)
        q = q_ref[:, cols] * scale
        sa = dot_cols(q, ka_ref[:, :HD]) + bias[:, :half]
        sb = dot_cols(q, kb_ref[:, :HD]) + bias[:, half:]
        peak = jnp.maximum(jnp.max(sa, axis=-1, keepdims=True), jnp.max(sb, axis=-1, keepdims=True))
        pa = jnp.exp(sa - peak)
        pb = jnp.exp(sb - peak)
        total = jnp.sum(pa, axis=-1, keepdims=True) + jnp.sum(pb, axis=-1, keepdims=True)
        out = dot(pa.astype(BF), ka_ref[:, HD:]) + dot(pb.astype(BF), kb_ref[:, HD:])
        out = (out / total).astype(BF)
        ctx_ref[:, cols] = out
        lse = jnp.broadcast_to(peak + jnp.log(total), (length, 128))
        lse_ref[i] = jnp.transpose(lse)[:1, :]
    part = dot(ctx_ref[...], w_ref[...])

    @pl.when(h == 0)
    def _():
        acc[...] = part

    @pl.when(h > 0)
    def _():
        acc[...] += part

    @pl.when(h == pl.num_programs(0) - 1)
    def _():
        write_pieces(me_tp, acc, pieces, layout)


def middle_kernel(info, *refs):
    parts, (x_ref, gain_ref, mid_ref, n2_ref) = refs[:-4], refs[-4:]
    mid = x_ref[0].astype(F32) + total_of(parts)
    mid_ref[...] = mid
    n2_ref[...] = (mid * inverse_rms(mid) * gain_ref[...]).astype(BF)


def place_pieces(me, pieces, out_ref, rels):
    per = len(rels) // len(pieces)
    block = pieces[0].shape[0] // per
    for i, rel in enumerate(rels):
        at = i % per * block
        out_ref[block_rows(me ^ rel, block), :] = pieces[i // per][at : at + block, :]


def ffn_kernel(n_parts, rels, layout, ff_layout, info, *refs):
    parts = refs[:n_parts]
    dy_ref, wg, wu, wd = refs[n_parts : n_parts + 4]
    outs = refs[n_parts + 4 :]
    n2_ref, hidden_ref = outs[:2]
    ff_refs, pieces = outs[2:4], outs[4 : 4 + len(layout)]
    acc = outs[4 + len(layout)]
    me = info[0]
    width = hidden_ref.shape[2]
    size = 512
    full, rest = width // size, width % size
    model = acc.shape[1]
    cut = min(1024, model)

    place_pieces(me, parts, n2_ref, rels)

    def hidden_part(c, at, count):
        here = pl.ds(at, count)
        gate = dot(n2_ref[...], wg[:, here])
        up = dot(n2_ref[...], wu[:, here])
        dhid = dot_cols(dy_ref[0], wd[here, :])
        sig = 1.0 / (1.0 + jnp.exp(-gate))
        swish = gate * sig
        hidden_ref[0, :, here] = (swish * up).astype(BF)
        hidden_ref[1, :, here] = (dhid * up * sig * (1.0 + gate * (1.0 - sig))).astype(BF)
        hidden_ref[2, :, here] = (dhid * swish).astype(BF)

    @pl.loop(0, full)
    def _(c):
        hidden_part(c, pl.multiple_of(c * size, size), size)

    if rest:
        hidden_part(full, full * size, rest)

    @pl.loop(0, model // cut)
    def _(n):
        here = pl.ds(pl.multiple_of(n * cut, cut), cut)
        acc[:, here] = dot_cols(hidden_ref[1], wg[here, :]) + dot_cols(hidden_ref[2], wu[here, :])

    write_pieces(me, acc, pieces, layout)

    @pl.loop(0, model // cut)
    def _(n):
        here = pl.ds(pl.multiple_of(n * cut, cut), cut)
        acc[:, here] = dot(hidden_ref[0], wd[:, here])

    write_pieces(me, acc, ff_refs, ff_layout)


def mid_back_kernel(info, *refs):
    parts, (mid_ref, dy_ref, gain_ref, low_ref) = refs[:-4], refs[-4:]
    d2 = total_of(parts)
    mid = mid_ref[...]
    inv = inverse_rms(mid)
    unit = mid * inv
    low_ref[...] = (dy_ref[0].astype(F32) + back_norm(d2, unit, inv, gain_ref[...])).astype(BF)


def attend_back_kernel(row, order, n_parts, rels, layout, info, docs, *refs):
    lows, refs = refs[:n_parts], refs[n_parts:]
    q_ref, ka_ref, kb_ref, lse_ref, wo_ref, wq_ref, cos_ref, sin_ref = refs[:8]
    low_ref, qlow_ref, keep_ref, send_ref = refs[8:12]
    pieces = refs[12:14]
    bias, dkv, lat = refs[14:]
    h = pl.program_id(0)
    length = q_ref.shape[0]
    half = len(order) // 2 * length
    me_tp, me_seq = info[0], info[1]
    scale = HD ** (-0.5)

    @pl.when(h == 0)
    def _():
        place_pieces(me_tp, lows, low_ref, rels)
        places = me_seq * length + lax.broadcasted_iota(jnp.int32, (1, length), 1)
        start = starts_of(docs, row, places)
        column = lax.broadcasted_iota(jnp.int32, (length, 1), 0)
        for b, rel in enumerate(order):
            key = (me_seq ^ rel) * length + column
            allowed = (key >= start) & (key <= places)
            bias[b * length : (b + 1) * length, :] = jnp.where(allowed, 0.0, NEG_FILL)

    dctx_all = dot_cols(low_ref[...], wo_ref[...]).astype(BF)
    for n in range(q_ref.shape[1] // HD):
        cols = slice(n * HD, (n + 1) * HD)
        q = q_ref[:, cols] * jnp.asarray(scale, BF)
        dctx = dctx_all[:, cols]
        lse = lse_ref[n]
        probs, dprobs = [], []
        delta = 0.0
        for i, kv_ref in enumerate((ka_ref, kb_ref)):
            scores = dot_cols(kv_ref[:, :HD], q) + bias[i * half : (i + 1) * half, :]
            prob = jnp.exp(scores - lse)
            dprob = dot_cols(kv_ref[:, HD:], dctx)
            delta = delta + jnp.sum(prob * dprob, axis=0, keepdims=True)
            probs.append(prob), dprobs.append(dprob)
        dq = 0.0
        for i, kv_ref in enumerate((ka_ref, kb_ref)):
            rows = slice(i * half, (i + 1) * half)
            dscore = (probs[i] * (dprobs[i] - delta)).astype(BF)
            dq = dq + dot_rows(dscore, kv_ref[:, :HD])
            dk = dot(dscore, q)
            dv = dot(probs[i].astype(BF), dctx)
            if n == 0:

                @pl.when(h == 0)
                def _():
                    dkv[rows, :HD] = dk
                    dkv[rows, HD:] = dv

                @pl.when(h > 0)
                def _():
                    dkv[rows, :HD] += dk
                    dkv[rows, HD:] += dv

            else:
                dkv[rows, :HD] += dk
                dkv[rows, HD:] += dv

        front, back = turn(dq * scale, cos_ref[0], -sin_ref[0])
        qlow_ref[:, n * HD : n * HD + HD // 2] = front.astype(BF)
        qlow_ref[:, n * HD + HD // 2 : (n + 1) * HD] = back.astype(BF)
    part = dot_cols(qlow_ref[...], wq_ref[...])

    @pl.when(h == 0)
    def _():
        lat[...] = part

    @pl.when(h > 0)
    def _():
        lat[...] += part

    @pl.when(h == pl.num_programs(0) - 1)
    def _():
        keep_ref[...] = dkv[:half, :].astype(BF)
        send_ref[...] = dkv[half:, :].astype(BF)
        write_pieces(me_tp, lat, pieces, layout)


def kv_split_kernel(n_rows, layout, info, *refs):
    pieces, held = refs[-1 - len(layout) : -1], refs[-1]
    count = (len(refs) - 1 - len(layout)) // n_rows
    rows = pieces[0].shape[0] // n_rows
    for r in range(n_rows):
        held[...] = total_of(refs[r * count : (r + 1) * count])
        outs = [piece.at[r * rows : (r + 1) * rows, :] for piece in pieces]
        write_pieces(info[0], held, outs, layout)


def latent_back_kernel(n_rows, info, *refs):
    units, invs = refs[-2 - 2 * n_rows : -2 - n_rows], refs[-2 - n_rows : -2]
    parts, (gain_ref, low_ref) = refs[: -2 - 2 * n_rows], refs[-2:]
    block = low_ref.shape[0] // n_rows
    for r in range(n_rows):
        rows = slice(r * block, (r + 1) * block)
        unit, grad = units[r][...], row_total(parts, r, n_rows, block)
        low_ref[rows, :] = back_norm(grad, unit, invs[r][:, :1], gain_ref[...]).astype(BF)


def key_back_kernel(n_rows, info, *refs):
    parts, (cos_ref, sin_ref, out_ref) = refs[:-3], refs[-3:]
    block = out_ref.shape[0] // n_rows
    for r in range(n_rows):
        rows = slice(r * block, (r + 1) * block)
        total = row_total(parts, r, n_rows, block)
        front, back = turn(total[:, :HD], cos_ref[r], -sin_ref[r])
        out_ref[rows, : HD // 2] = front.astype(BF)
        out_ref[rows, HD // 2 : HD] = back.astype(BF)
        out_ref[rows, HD:] = total[:, HD:].astype(BF)


def ffn_sum_kernel(n_rows, info, *refs):
    parts, mids, out_ref = refs[: -1 - n_rows], refs[-1 - n_rows : -1], refs[-1]
    block = out_ref.shape[0] // n_rows
    for r in range(n_rows):
        out_ref[r * block : (r + 1) * block, :] = (row_total(parts, r, n_rows, block) + mids[r][...]).astype(BF)


def spread_kernel(rels, info, *refs):
    pieces, out_ref = refs[:-1], refs[-1]
    n_rows, per = out_ref.shape[0], len(rels) // len(pieces)
    block = out_ref.shape[1] // len(rels)
    for i, rel in enumerate(rels):
        for row in range(n_rows):
            at = (i % per * n_rows + row) * block
            out_ref[row, block_rows(info[0] ^ rel, block), :] = pieces[i // per][at : at + block, :]


def join_kernel(n_rows, rels, count, info, *refs):
    pieces, all_ref = refs[:count], refs[count]
    me, n_tp = info[0], len(rels)
    per = n_tp // count
    block = pieces[0].shape[0] // (n_rows * per)
    for i, rel in enumerate(rels):
        for r in range(n_rows):
            at = (i % per * n_rows + r) * block
            all_ref[block_rows(r * n_tp + (me ^ rel), block), :] = pieces[i // per][at : at + block, :]
    if len(refs) > count + 1:
        part_ref = refs[count + 1]
        part_ref[...] = all_ref[:, block_rows(me, part_ref.shape[1])]


def input_kernel(info, lat_ref, kv_ref, x_ref, wd_ref, wkv_ref, low_ref, gain_ref, out_ref):
    dn = dot_cols(lat_ref[...], wd_ref[...]) + dot_cols(kv_ref[...], wkv_ref[...])
    x = x_ref[0].astype(F32)
    inv = inverse_rms(x)
    unit = x * inv
    out_ref[0] = (low_ref[...].astype(F32) + back_norm(dn, unit, inv, gain_ref[...])).astype(BF)


def grad_kernel(table, *refs):
    count = (len(refs) - 2) // 2
    keep_ref, send_ref = refs[2 * count :]

    def load(ref):
        value = ref[...]
        return value.reshape(-1, value.shape[-1])

    total = dot_rows(load(refs[0]), load(refs[count]))
    for i in range(1, count):
        total = total + dot_rows(load(refs[i]), load(refs[count + i]))
    total = total.astype(BF)
    i, half = pl.program_id(0), pl.num_programs(0) // 2

    @pl.when(i < half)
    def _():
        keep_ref[...] = total

    @pl.when(i >= half)
    def _():
        send_ref[...] = total


def ffn_grad_kernel(info, hidden_ref, n2_ref, dy_ref, out_ref):
    dy = dy_ref[...]
    dy = dy.reshape(-1, dy.shape[-1])
    width = hidden_ref.shape[2]
    out_ref[:, :width] = dot_rows(dy, hidden_ref[0]).astype(BF)
    out_ref[:, width : 2 * width] = dot_rows(n2_ref[...], hidden_ref[1]).astype(BF)
    out_ref[:, 2 * width :] = dot_rows(n2_ref[...], hidden_ref[2]).astype(BF)


def head_grad_kernel(info, context_ref, low_ref, latent_ref, query_ref, out_ref):
    rows, width = context_ref.shape[1], low_ref.shape[1]
    out_ref[:rows, :] = dot_rows(context_ref[...], low_ref[...]).astype(BF)
    count = latent_ref.shape[1]
    part = dot_rows(latent_ref[...], query_ref[...]).astype(BF)
    for i in range(part.shape[1] // width):
        out_ref[rows + i * count : rows + (i + 1) * count, :] = part[:, i * width : (i + 1) * width]


def pause_kernel(info, out_ref):
    for i in range(out_ref.shape[0]):
        out_ref[i] = info[i]


def shared_kernel(n_tp, info, *refs):
    for pieces, out_ref in ((refs[:n_tp], refs[2 * n_tp]), (refs[n_tp : 2 * n_tp], refs[2 * n_tp + 1])):
        for r in range(n_tp):
            width = pieces[r].shape[1]
            out_ref[:, block_rows(info[0] ^ r, width)] = pieces[r][...].astype(F32)


def build(n_seq, n_tp):
    seq_bits = n_seq.bit_length() - 1
    tp_bits = n_tp.bit_length() - 1

    def swap(value, axis, mask):
        count = n_seq if axis == "seq" else n_tp
        return lax.ppermute(value, axis, [(i, i ^ mask) for i in range(count)])

    def spread(bits):
        order = [0]
        for bit in bits:
            order = order + [o | (1 << bit) for o in order]
        return order

    upward = list(range(1, seq_bits))
    routes = (upward + [0], upward[::-1] + [0])
    tp_route = list(reversed(range(tp_bits)))
    tp_rels = spread(tp_route)
    halves = [tp_rels[: n_tp // 2], tp_rels[n_tp // 2 :]]
    singles = [[r] for r in range(n_tp)]
    layouts = [singles, halves]

    def gather(block):
        return [block] + [swap(block, "tp", r) for r in range(1, n_tp)]

    def shards(
        layer_in, attn_gain, query_down, latent_gain, query_up, key_value, attn_out,
        ffn_gain, gate_proj, up_proj, down_proj, out_grad, doc_lengths,
    ):
        n_rows, length, model_dim = layer_in.shape
        lat_dim, q_width = query_up.shape
        ff_dim = gate_proj.shape[1]
        heads = q_width // HD
        block = length // n_tp
        half_keys = n_seq // 2 * length
        rows = range(n_rows)
        seq_me, tp_me = lax.axis_index("seq"), lax.axis_index("tp")
        state = [jnp.stack([tp_me, seq_me, jnp.zeros_like(tp_me)]).astype(jnp.int32)]
        last, due = [], []

        def wait(*arrays):
            due.extend(arrays)

        def pause():
            state[0] = step(
                pause_kernel, [], [(shape_of((3,), jnp.int32), pl.BlockSpec(memory_space=pltpu.SMEM))], name="pause",
            )[0]

        def after(value):
            ready = last[-1:] + due
            due.clear()
            return lax.optimization_barrier((value, *ready))[0] if ready else value

        def step(kernel, inputs, outputs, table=None, docs=False, **kw):
            scalars = (after(state[0] if table is None else table),) + ((doc_lengths,) if docs else ())
            out = run(kernel, scalars, inputs, outputs, **kw)
            last.append(min(out, key=lambda o: o.size))
            return out

        def total(values, kind):
            out = after(values[-1][0])[values[-1][1]].astype(F32)
            for array, index in values[:-1]:
                out = out + array[index].astype(F32)
            out = out.astype(kind)
            last.append(out)
            return out

        def add(parts, rows, at, kind):
            return total([(p, slice(at * rows, (at + 1) * rows)) for p in parts], kind)

        def halve(parts, rows, axis, bit):
            half = rows // 2
            return parts + [swap(add(parts, half, 1, BF), axis, 1 << bit)], half

        def halve_all(parts, rows, axis, bits):
            for bit in reversed(bits):
                parts, rows = halve(parts, rows, axis, bit)
            return parts, rows

        places = seq_me * length + jnp.arange(length, dtype=jnp.int32)
        ends = jnp.cumsum(doc_lengths, axis=1)
        passed = places[None, :, None] >= ends[:, None, :]
        inner = places[None, :] - jnp.sum(jnp.where(passed, doc_lengths[:, None, :], 0), axis=-1)
        frequency = ROPE_BASE ** (-jnp.arange(HD // 2, dtype=F32) / (HD // 2))
        angles = inner.astype(F32)[:, :, None] * frequency
        cosine, sine = jnp.cos(angles), jnp.sin(angles)
        gain_row = lambda gain: (gain.reshape(1, -1), full_spec((1, gain.shape[0])))

        def whole(array):
            return array, full_spec(array.shape)

        def first(array, count):
            return array, full_spec((count, array.shape[1]))

        def row_of(array, r):
            return array, pl.BlockSpec((1,) + array.shape[1:], lambda *_: (r, 0, 0))

        def own_of(array, r):
            shape = (1, block, array.shape[2])
            return array, pl.BlockSpec(shape, lambda i, info, *_: (r, info[0], 0))

        def new(shape, kind=BF):
            return shape_of(shape, kind), full_spec(shape)

        per_step = min(HEADS_PER_STEP, heads)
        group = per_step * HD

        def head_cols(array):
            return array, pl.BlockSpec((array.shape[0], group), lambda h, *_: (0, h))

        def head_rows(array):
            return array, pl.BlockSpec((group, array.shape[1]), lambda h, *_: (h, 0))

        def row_pieces(r, width):
            rows_out = n_tp // 2 * block
            spec = pl.BlockSpec((rows_out, width), lambda *_: (r, 0))
            return [(shape_of((n_rows * rows_out, width)), spec)] * 2

        def pieces_of(layout, width):
            return [new((len(rels) * block, width)) for rels in layout]

        on_chip = pl.BlockSpec(memory_space=pltpu.VMEM)
        weights = [pltpu.with_memory_space_constraint(w, pltpu.VMEM) for w in (gate_proj, up_proj, down_proj)]

        def rows_of(width, r, spec=None):
            return shape_of((n_rows * length, width)), spec or pl.BlockSpec((length, width), lambda *_: (r, 0))

        def row_block(array, r):
            return array, pl.BlockSpec((length, array.shape[1]), lambda *_: (r, 0))

        def going(held, *pairs):
            return [(index, held[key]) for index, key in pairs] if held else []

        def front(r, held):
            return step(
                front_kernel,
                [row_of(layer_in, r), gain_row(attn_gain), whole(key_value), row_of(cosine, r), row_of(sine, r)],
                [rows_of(model_dim, r), new((length, 2 * HD))], name="front", carried=going(held, (0, 0)),
            )

        def query(r, held):
            return step(
                query_kernel,
                [row_block(normed, r), whole(query_down), gain_row(latent_gain), whole(query_up),
                 row_of(cosine, r), row_of(sine, r)],
                [rows_of(lat_dim, r), new((block, lat_dim), F32), new((block, 128), F32), new((length, q_width))],
                scratch=[pltpu.VMEM((length, lat_dim), F32)], name="query", carried=going(held, (0, 0)),
            )

        def attend(r, held):
            return step(
                functools.partial(attend_kernel, r, spread(routes[(r + 1) % 2]), layouts[r]),
                [head_cols(queries[r]), whole(near[r]), whole(far[r]), head_rows(attn_out)],
                [
                    rows_of(q_width, r, pl.BlockSpec((length, group), lambda h, *_: (r, h))),
                    (shape_of((heads, 1, length), F32), pl.BlockSpec((per_step, 1, length), lambda h, *_: (h, 0, 0))),
                ] + pieces_of(layouts[r], model_dim),
                docs=True, grid=(heads // per_step,),
                scratch=[pltpu.VMEM((length, model_dim), F32), pltpu.VMEM((length, 2 * half_keys), F32)],
                name="attend", vmem=min(58, 26 * half_keys // 1024) * MIB, carried=going(held, (0, 0)),
            )

        def mid_step(r, parts):
            return step(
                middle_kernel, [first(p, block) for p in parts] + [own_of(layer_in, r), gain_row(ffn_gain)],
                [new((block, model_dim), F32), new((block, model_dim))], name="middle", vmem=24 * MIB,
            )

        def ffn(r, held):
            return step(
                functools.partial(ffn_kernel, len(normed2[r]), range(n_tp), layouts[r], halves),
                [whole(p) for p in normed2[r]] + [row_of(out_grad, r),
                 (weights[0], on_chip), (weights[1], on_chip), (weights[2], on_chip)],
                [rows_of(model_dim, r),
                 (shape_of((3, n_rows * length, ff_dim)), pl.BlockSpec((3, length, ff_dim), lambda *_: (0, r, 0)))]
                + row_pieces(r, model_dim) + pieces_of(layouts[r], model_dim),
                scratch=[pltpu.VMEM((length, model_dim), F32)], vmem=24 * MIB,
                name="ffn", carried=going(held, *[(i, i) for i in range(4)]),
            )

        def mid_back(r, parts):
            return step(
                mid_back_kernel,
                [first(p, block) for p in parts] + [whole(middle[r]), own_of(out_grad, r), gain_row(ffn_gain)],
                [new((block, model_dim))], name="mid_back",
            )[0]

        def attend_back(r, held):
            return step(
                functools.partial(attend_back_kernel, r, spread(routes[(r + 1) % 2]), len(mid_low[r]), range(n_tp), halves),
                [whole(p) for p in mid_low[r]]
                + [head_cols(queries[r]), whole(near[r]), whole(far[r]),
                   (lse[r], pl.BlockSpec((per_step, 1, length), lambda h, *_: (h, 0, 0))),
                   head_rows(attn_out), head_cols(query_up), row_of(cosine, r), row_of(sine, r)],
                [rows_of(model_dim, r), rows_of(q_width, r, pl.BlockSpec((length, group), lambda h, *_: (r, h))),
                 new((half_keys, 2 * HD)), new((half_keys, 2 * HD))] + row_pieces(r, lat_dim),
                docs=True, grid=(heads // per_step,),
                scratch=[pltpu.VMEM((2 * half_keys, length), F32), pltpu.VMEM((2 * half_keys, 2 * HD), F32),
                         pltpu.VMEM((length, lat_dim), F32)],
                name="attend_back", vmem=min(58, 32 * half_keys // 1024) * MIB, carried=going(held, (0, 0), (1, 1), (4, 4), (5, 5)),
            )

        def halve_rows(parts, count):
            half = count // 2 * block
            width = parts[0].shape[1]
            values = [(p.reshape(n_rows, -1, width), (slice(None), slice(half, 2 * half))) for p in parts]
            away = total(values, BF).reshape(n_rows * half, width)
            last[-1] = away
            return parts + [swap(away, "tp", 1 << tp_route[count.bit_length() - 2])]

        def joined_pair(held):
            pair = jnp.concatenate([after(held[0]), held[1]], axis=0)
            last.append(pair)
            return pair

        def gather_start(piece):
            return piece, swap(piece, "tp", 1 << tp_route[0])

        def gather_end(held):
            for bit in tp_route[1:]:
                held = joined_pair(held)
                held = held, swap(held, "tp", 1 << bit)
            return list(held)

        def both(array):
            return [array, swap(array, "seq", 1)]

        def weight_grad(acts, deltas, by_cols, route):
            acts, deltas = [[a if isinstance(a, tuple) else (a, None) for a in pair] for pair in (acts, deltas)]
            bits = routes[route][:-1]
            order = [o for o in spread(bits)]
            count = n_seq // 2
            size = (deltas if by_cols else acts)[0][0].shape[-1] // n_seq
            if size % 128:
                flat = [jnp.concatenate([a for a, _ in pair], axis=0) for pair in (acts, deltas)]
                full = dot_rows(*flat).astype(BF)
                blocks = jnp.take(full.reshape(n_seq, -1, full.shape[1]), jnp.stack([seq_me ^ o for o in order]), axis=0)
                parts, left = halve([blocks.reshape(-1, full.shape[1])], count * size, "seq", bits[-1])
            else:

                def operands(arrays, cut):
                    out = []
                    for array, which in arrays:
                        lead = array.shape[:-1]
                        if which is not None:
                            out.append((array, pl.BlockSpec((1,) + array.shape[1:], lambda i, t: (which, 0, 0))))
                        elif cut:
                            zeros = (0,) * len(lead)
                            out.append((array, pl.BlockSpec(lead + (size,), lambda i, t, z=zeros: z + (t[i],))))
                        else:
                            out.append(whole(array))
                    return out

                shape = (acts[0][0].shape[-1], size) if by_cols else (size, deltas[0][0].shape[-1])
                half = count // 2
                part = shape_of((half * shape[0], shape[1]))
                keep, away = step(
                    grad_kernel, operands(acts, not by_cols) + operands(deltas, by_cols),
                    [(part, pl.BlockSpec(shape, lambda i, t: (jnp.minimum(i, half - 1), 0))),
                     (part, pl.BlockSpec(shape, lambda i, t: (jnp.maximum(i - half, 0), 0)))],
                    table=jnp.stack([seq_me ^ o for o in order]).astype(jnp.int32), grid=(count,), name="grad",
                )
                parts, left = [keep, swap(away, "seq", 1 << bits[-1])], keep.shape[0]
            yield parts[-1]
            parts, left = halve_all(parts, left, "seq", bits[:-1])
            yield parts[-1]
            yield add(parts, left, 0, F32)

        held, out = [], None
        for r in rows:
            out = front(r, out)
            held.append([out[1], swap(out[1], "seq", 1 << routes[(r + 1) % 2][0])])
        normed = out[0]
        normed_both = both(normed)
        unit_lat, inv_lat, queries = [], [], []

        def widen(r, bit):
            pair = joined_pair(held[r])
            held[r] = [pair, swap(pair, "seq", 1 << bit)]

        for bit in range(1, seq_bits - 1):
            for r in rows:
                widen(r, routes[(r + 1) % 2][bit])
        out = None
        for r in rows:
            out = query(r, out)
            unit_lat.append(out[1]), inv_lat.append(out[2]), queries.append(out[3])
        wait(normed_both[1])
        latent_norm = out[0]
        near, far = [None] * n_rows, [None] * n_rows
        lse, part1, out = [], [], None

        def sent_over(pieces):
            if len(pieces) == 2:
                return [pieces[0], swap(pieces[1], "tp", 1)]
            return [pieces[0]] + [swap(pieces[r], "tp", r) for r in range(1, n_tp)]

        for r in rows:
            widen(r, 0)
            near[r], far[r] = held[r]
            out = attend(r, out)
            lse.append(out[1])
            part1.append(sent_over(out[2:]))
        context = out[0]
        sent = n_tp // 2 * block
        middle, normed2 = [], []
        mid, n2 = mid_step(0, part1[0])
        middle.append(mid)
        normed2.append(gather(n2))
        part1[1], _ = halve_all(part1[1], sent, "tp", tp_route[:-1])
        wait(*normed2[0])
        mid, n2 = mid_step(1, part1[1])
        middle.append(mid)
        normed2.append(gather(n2))

        part2, out = [], None
        for r in rows:
            out = ffn(r, out)
            part2.append(sent_over(out[4:]))
        n2_all, hidden, ffn_keep, ffn_send = out[:4]
        mid_low = [gather(mid_back(0, part2[0]))]
        wide = model_dim // n_seq

        def over_seq(part):
            return lax.psum_scatter(part, "seq", scatter_dimension=0, tiled=True)

        ffn_part = step(
            ffn_grad_kernel,
            [whole(hidden), (n2_all, pl.BlockSpec((n_rows * length, wide), lambda i, *_: (0, i))),
             (out_grad, pl.BlockSpec((n_rows, length, wide), lambda i, *_: (0, 0, i)))],
            [(shape_of((model_dim, 3 * ff_dim)), pl.BlockSpec((wide, 3 * ff_dim), lambda i, *_: (i, 0)))],
            grid=(n_seq,), name="ffn_grad",
        )[0]
        ffn_sum = over_seq(ffn_part)
        part2[1], _ = halve_all(part2[1], sent, "tp", tp_route[:-1])
        wait(*mid_low[0])
        mid_low.append(gather(mid_back(1, part2[1])))

        kv_parts = []
        ffn_parts = [ffn_keep, swap(after(ffn_send), "tp", 1)]
        out = attend_back(0, None)
        kv_parts.append(([out[2], swap(out[3], "seq", 1)], half_keys))
        pause()
        kv_parts[0] = halve(*kv_parts[0], "seq", routes[1][-2])
        wait(*mid_low[1])
        out = attend_back(1, out)
        low_all, query_low = out[:2]
        kv_parts.append(([out[2], swap(out[3], "seq", 1)], half_keys))
        lat_parts = [out[4], swap(out[5], "tp", 1)]
        pause()
        crossed = seq_bits == 3
        if crossed:
            keep, got = kv_parts[1][0]
            pairs = lambda p: p.reshape(2, 2, length, -1)
            away = total([(pairs(p), (slice(None), 1)) for p in (keep, got)], BF).reshape(2 * length, -1)
            last[-1] = away
            kv_parts[1] = [keep, got, swap(away, "seq", 2)]
        else:
            kv_parts[1] = halve(*kv_parts[1], "seq", routes[0][-2])
        for count in [n_tp >> i for i in range(1, tp_bits)]:
            ffn_parts = halve_rows(ffn_parts, count)
        kv_parts[0] = halve_all(*kv_parts[0], "seq", routes[1][:-2])
        for count in [n_tp >> i for i in range(1, tp_bits)]:
            lat_parts = halve_rows(lat_parts, count)
        own_lat = lat_dim // n_seq
        pieces = q_width // wide
        rows_out = q_width + pieces * own_lat
        if own_lat % 128:
            out_blocks = dot_rows(context, low_all).reshape(q_width, n_seq, wide).transpose(1, 0, 2)
            query_blocks = dot_rows(latent_norm, query_low).reshape(n_seq, own_lat, pieces, wide).transpose(0, 2, 1, 3)
            head_part = jnp.concatenate([out_blocks, query_blocks.reshape(n_seq, -1, wide)], axis=1)
            head_part = head_part.astype(BF).reshape(-1, wide)
        else:
            head_part = step(
                head_grad_kernel,
                [whole(context), (low_all, pl.BlockSpec((n_rows * length, wide), lambda i, *_: (0, i))),
                 (latent_norm, pl.BlockSpec((n_rows * length, own_lat), lambda i, *_: (0, i))), whole(query_low)],
                [(shape_of((n_seq * rows_out, wide)), pl.BlockSpec((rows_out, wide), lambda i, *_: (i, 0)))],
                grid=(n_seq,), name="head_grad",
            )[0]
        pause()
        if crossed:
            keep, got, more = kv_parts[1]
            values = [(pairs(p), (1, 0)) for p in (keep, got)] + [(more, slice(length, None))]
            kv_parts[1] = [keep, got, more, swap(total(values, BF), "seq", 4)], length
        else:
            kv_parts[1] = halve_all(*kv_parts[1], "seq", routes[0][:-2])
        lat_low = step(
            functools.partial(latent_back_kernel, n_rows),
            [whole(p) for p in lat_parts] + [whole(u) for u in unit_lat] + [whole(i) for i in inv_lat]
            + [gain_row(latent_gain)],
            [new((n_rows * block, lat_dim))], name="latent_back",
        )[0]
        lat_blocks = gather_start(lat_low)
        kv_sum = step(
            functools.partial(kv_split_kernel, n_rows, singles),
            [first(p, length) for parts, _ in kv_parts for p in parts],
            [new((n_rows * block, 2 * HD))] * n_tp,
            scratch=[pltpu.VMEM((length, 2 * HD), F32)], name="kv_split",
        )
        kv_sum = sent_over(kv_sum)
        ffn_own = step(
            functools.partial(ffn_sum_kernel, n_rows), [whole(p) for p in ffn_parts] + [whole(m) for m in middle],
            [new((n_rows * block, model_dim))], name="ffn_sum",
        )[0]
        head_sum = over_seq(after(head_part))
        own_dim = model_dim // n_seq

        def own_part(array, count):
            return lax.dynamic_slice_in_dim(array, seq_me * count, count, 0)

        def row_sums(weight, grad):
            return jnp.sum(own_part(weight, grad.shape[0]).astype(F32) * grad, axis=1)

        lat_blocks = gather_end(lat_blocks)
        own_rows = pl.BlockSpec((n_rows, block, HD // 2), lambda i, info, *_: (0, info[0], 0))
        kv_low = step(
            functools.partial(key_back_kernel, n_rows),
            [whole(p) for p in kv_sum] + [(cosine, own_rows), (sine, own_rows)],
            [new((n_rows * block, 2 * HD))], name="key_back",
        )[0]
        kv_blocks = gather(kv_low)
        ffn_blocks = gather_start(after(ffn_own))
        pause()
        gate_up = total([(ffn_sum, (slice(None), slice(ff_dim, None)))], F32)
        gate_grad, up_grad = gate_up[:, :ff_dim], gate_up[:, ff_dim:]
        ffn_rows = row_sums(gate_proj, gate_grad) + row_sums(up_proj, up_grad)
        last.append(ffn_rows)

        def join(blocks, rels):
            width = blocks[0].shape[1]
            cols = width // n_tp
            count = n_rows * length
            out = step(
                functools.partial(join_kernel, n_rows, rels, len(blocks)), [whole(b) for b in blocks],
                [new((count, width))] + ([] if cols % 128 else [new((count, cols))]), name="join",
            )
            if cols % 128:
                return out[0], lax.dynamic_slice_in_dim(out[0], tp_me * cols, cols, 1)
            return out

        lat_all, lat_part = join(lat_blocks, tp_rels)
        lat_part_both = both(lat_part)
        kv_all, kv_part = join(kv_blocks, range(n_tp))
        kv_part_both = both(kv_part)
        ffn_blocks = gather_end(ffn_blocks)
        grad_lat = weight_grad(normed_both, lat_part_both, False, 0)
        lat_2 = next(grad_lat)
        grad_kv = weight_grad(normed_both, kv_part_both, False, 1)
        kv_2 = next(grad_kv)

        def input_step(r, held):
            return step(
                input_kernel,
                [row_block(lat_all, r), row_block(kv_all, r), row_of(layer_in, r), whole(query_down), whole(key_value),
                 row_block(low_all, r), gain_row(attn_gain)],
                [(shape_of(layer_in.shape), pl.BlockSpec((1, length, model_dim), lambda *_: (r, 0, 0)))],
                name="input", carried=going(held, (0, 0)),
            )

        out = input_step(0, None)
        lat_3 = next(grad_lat)
        kv_3 = next(grad_kv)
        input_grad = input_step(1, out)[0]
        lat_sum = next(grad_lat)
        shared_lat = gather(lat_sum.astype(BF))
        pause()
        kv_grad_sum = next(grad_kv)
        head_grads = total([(head_sum, slice(None))], F32)
        out_weight_grad = head_grads[:q_width]
        query_up_grad = head_grads[q_width:].reshape(pieces, own_lat, wide).transpose(1, 0, 2).reshape(own_lat, q_width)

        def own_columns(weight):
            cols = weight.shape[1] // n_tp
            return lax.dynamic_slice_in_dim(weight, tp_me * cols, cols, 1)

        tp_sums = jnp.concatenate(
            [
                ffn_rows,
                row_sums(own_columns(query_down), lat_sum) + row_sums(own_columns(key_value), kv_grad_sum),
                row_sums(query_up, query_up_grad),
            ]
        )
        kv_rows = jnp.concatenate([kv_grad_sum, tp_sums.reshape(-1, kv_grad_sum.shape[1])], axis=0).astype(BF)
        wait(*shared_lat)
        shared_kv = gather(after(kv_rows))
        pause()
        down_grad = total([(ffn_sum, (slice(None), slice(0, ff_dim)))], F32).T
        layer_out = step(
            functools.partial(spread_kernel, tp_rels), [whole(p) for p in ffn_blocks], [new(layer_in.shape)],
            name="spread",
        )[0]
        if kv_part.shape[1] % 128:

            def side_by_side(pieces):
                cols = pieces[0].shape[1]
                blocks = jnp.take(jnp.stack(pieces)[:, :own_dim], jnp.stack([tp_me ^ r for r in range(n_tp)]), axis=0)
                return blocks.astype(F32).transpose(1, 0, 2).reshape(own_dim, n_tp * cols)

            down_q, kv_grad = side_by_side(shared_lat), side_by_side(shared_kv)
        else:
            down_q, kv_grad = step(
                functools.partial(shared_kernel, n_tp),
                [whole(p) for p in shared_lat] + [first(p, own_dim) for p in shared_kv],
                [new((own_dim, lat_dim), F32), new((own_dim, 2 * HD), F32)], name="shared",
            )
        tp_sums = sum(p[own_dim:].astype(F32) for p in shared_kv).reshape(-1)
        ffn_gain_grad = tp_sums[:own_dim] / own_part(ffn_gain, own_dim)
        attn_gain_grad = tp_sums[own_dim : 2 * own_dim] / own_part(attn_gain, own_dim)
        latent_gain_grad = tp_sums[2 * own_dim :] / own_part(latent_gain, own_lat)
        return (
            layer_out, input_grad, attn_gain_grad, down_q, latent_gain_grad, query_up_grad,
            kv_grad, out_weight_grad.reshape(q_width, own_dim), ffn_gain_grad, gate_grad, up_grad,
            down_grad.reshape(ff_dim, own_dim),
        )

    return shards


def solution(mesh):
    return jax.shard_map(
        build(mesh.shape["seq"], mesh.shape["tp"]),
        mesh=mesh,
        in_specs=(
            P(None, "seq", None), P(), P(), P(), P(None, "tp"), P(), P("tp", None), P(),
            P(None, "tp"), P(None, "tp"), P("tp", None), P(None, "seq", None), P(),
        ),
        out_specs=(
            P(None, "seq", None), P(None, "seq", None), P("seq"), P("seq", None), P("seq"),
            P("seq", "tp"), P("seq", None), P("tp", "seq"), P("seq"), P("seq", "tp"),
            P("seq", "tp"), P("tp", "seq"),
        ),
        check_vma=False,
    )
```
